128 devices in a mesh: dp: 2 (over x_lo), space: 64 (over z, y, x_hi, core).
Axes of the slice: x: 4 (x_hi: 2, x_lo: 2; x = x_hi * 2 + x_lo), y: 4, z: 4, core: 2. Of those that a mesh axis runs over, the one named last changes fastest.
Arguments:
- stash: bfloat16 [64, 64, 4, 2160], P('space', None, 'dp'), may hold values from -5 to 5
- piece_map: int32 [64, 64], P(None, 'space'), may hold values from 0 to 63, as said below
- gain_one: float32 [768], replicated, may hold values from 0.5 to 1.5
- spec_one: float32 [2, 8, 96, 96], replicated, may hold values from -0.4375 to 0.4375
- bias_one: float32 [2, 768], replicated, may hold values from -3 to 3
- spec_two: float32 [2, 8, 96, 96], replicated, may hold values from -0.4375 to 0.4375
- bias_two: float32 [2, 768], replicated, may hold values from -0.6 to 0.6
- gain_two: float32 [768], replicated, may hold values from 0.5 to 1.5
- fc_one: bfloat16 [768, 3072], replicated, may hold values from -0.21875 to 0.21875
- bias_fc: float32 [3072], replicated, may hold values from -3 to 3
- fc_two: bfloat16 [3072, 768], replicated, may hold values from -0.109375 to 0.109375
- cotangent: bfloat16 [4, 64, 180, 768], P('dp', 'space'), may hold values from -6 to 6
Outputs:
- grad_input: float32 [4, 64, 180, 768], P('dp', 'space')
- grad_fc_one: float32 [768, 3072], P(None, ('dp', 'space'))
- grad_fc_two: float32 [3072, 768], P(('dp', 'space'))
- grad_bias_fc: float32 [3072], replicated
- grad_bias_out: float32 [768], replicated
- grad_gain_one: float32 [768], replicated
- grad_gain_two: float32 [768], replicated
- grad_spec_one: float32 [2, 8, 96, 96], replicated
- grad_bias_one: float32 [2, 768], replicated
- grad_spec_two: float32 [2, 8, 96, 96], replicated
- grad_bias_two: float32 [2, 768], replicated
The draws below stay inside these ranges and needn't reach their ends.
Inputs may be any that keep to these rules, and one draw needn't show every extreme that they name: `piece_map`: each column holds every number from 0 to 63 once.
All inputs are finite; a program needn't handle non-finite values.
Results may differ from the reference program's by a relative error of at most 0.0046.
Values may be sent and summed in bfloat16 or wider, within the bound.
No kernel may reach another device: no remote copies, remote signals or barrier semaphores. Data moves between devices by JAX's collectives and lax.ppermute only.
A program may use at most 128 MiB of HBM per device.

```python
import jax
import jax.numpy as jnp
from jax import lax

D = 768
FF = 3072
BLOCKS = 8
LON = 180
KW = 64
BLOCK = 96
H = 64
SAMPLES = 4
PIECE = 2160
N_SPACE = 64


def piece_table(key):

    def one_column(column):
        return jax.random.permutation(jax.random.fold_in(key, column), N_SPACE)
    columns = jax.vmap(one_column)(jnp.arange(N_SPACE, dtype=jnp.int32))
    return columns.T.astype(jnp.int32)


def draw_piece_map(key, part):
    return piece_table(jax.random.fold_in(key, 11))


def draw_stash(key, part):
    holder_table = piece_table(jax.random.fold_in(key, 11))
    drawn_field = jnp.clip(jax.random.normal(jax.random.fold_in(key, 29), (SAMPLES, H, LON, D), jnp.float32), -5.0, 5.0)
    pieces = drawn_field.reshape(SAMPLES, N_SPACE, N_SPACE, PIECE)
    pieces = jnp.transpose(pieces, (1, 2, 0, 3))
    owners = jnp.arange(N_SPACE, dtype=jnp.int32)[None, :]
    return pieces[owners, holder_table].astype(jnp.bfloat16)


def block_levels(key, extent, cuts, low, largest):
    loudness, own = 1.0, jax.random.fold_in(key, 6)
    for axis_at, shards_of in cuts:
        steps = jnp.exp(jax.random.uniform(jax.random.fold_in(own, axis_at), (shards_of,), jnp.float32, low / len(cuts), largest / len(cuts)))
        loudness = loudness * jnp.repeat(steps, extent[axis_at] // shards_of).reshape([-1 if axis == axis_at else 1 for axis in range(len(extent))])
    return loudness


def scatter_about(rng, dims, scale, limit, split=(), held_as=jnp.bfloat16):
    drawn = scale * jax.random.normal(rng, dims, jnp.float32)
    if split:
        drawn = drawn * block_levels(rng, dims, split, -0.22, 0.18)
    return jnp.clip(drawn, -limit, limit).astype(held_as)


def setup_inputs(seed: int = 0) -> dict:
    key_of = jax.random.split(jax.random.key(seed), 13)
    return {
        "stash": draw_stash(jax.random.fold_in(key_of[12], 71), 0),
        "piece_map": draw_piece_map(jax.random.fold_in(key_of[12], 71), 0),
        "gain_one": jnp.clip(1.0 + 0.1 * jax.random.normal(key_of[2], (D,), jnp.float32), 0.5, 1.5),
        "spec_one": scatter_about(key_of[3], (2, BLOCKS, BLOCK, BLOCK), (2 * BLOCK) ** -0.5, 0.4375, (), jnp.float32),
        "bias_one": scatter_about(key_of[4], (2, D), 0.5, 3.0, (), jnp.float32),
        "spec_two": scatter_about(key_of[5], (2, BLOCKS, BLOCK, BLOCK), (2 * BLOCK) ** -0.5, 0.4375, (), jnp.float32),
        "bias_two": scatter_about(key_of[6], (2, D), 0.1, 0.6, (), jnp.float32),
        "gain_two": jnp.clip(1.0 + 0.1 * jax.random.normal(key_of[7], (D,), jnp.float32), 0.5, 1.5),
        "fc_one": scatter_about(key_of[8], (D, FF), D ** -0.5, 0.21875),
        "bias_fc": scatter_about(key_of[9], (FF,), 0.5, 3.0, (), jnp.float32),
        "fc_two": scatter_about(key_of[10], (FF, D), FF ** -0.5, 0.109375),
        "cotangent": scatter_about(key_of[11], (SAMPLES, H, LON, D), 1.0, 6.0, ((0, 2), (1, 64))),
    }


epsilon = 1e-05
highest = lax.Precision.HIGHEST

def layer_norm(values, gain_vector):
    centred = values - lax.optimization_barrier(jnp.mean(values, axis=-1, keepdims=True))
    spread = lax.optimization_barrier(jnp.mean(centred * centred, axis=-1, keepdims=True))
    return centred * lax.rsqrt(spread + epsilon) * gain_vector

def smooth_gate(values):
    return jax.nn.gelu(values, approximate=True)

def block_mix(real_part, imag_part, weights, biases):
    blocks = weights.shape[1]
    width_block = weights.shape[2]
    leading = real_part.shape[:-1]
    real_blocks = real_part.reshape(leading + (blocks, width_block))
    imag_blocks = imag_part.reshape(leading + (blocks, width_block))
    bias_real = biases[0].reshape(blocks, width_block)
    bias_imag = biases[1].reshape(blocks, width_block)
    new_real = jnp.einsum('...ni,nio->...no', real_blocks, weights[0], precision=highest) - jnp.einsum('...ni,nio->...no', imag_blocks, weights[1], precision=highest) + bias_real
    new_imag = jnp.einsum('...ni,nio->...no', real_blocks, weights[1], precision=highest) + jnp.einsum('...ni,nio->...no', imag_blocks, weights[0], precision=highest) + bias_imag
    return (new_real.reshape(leading + (blocks * width_block,)), new_imag.reshape(leading + (blocks * width_block,)))

def spectral_mlp(spec_real, spec_imag, spec_one, bias_one, spec_two, bias_two):
    inner_real, inner_imag = block_mix(spec_real, spec_imag, spec_one, bias_one)
    return block_mix(smooth_gate(inner_real), smooth_gate(inner_imag), spec_two, bias_two)

def to_spectrum(normed):
    full = jnp.fft.rfft2(normed, axes=(0, 1), norm='ortho')[:, :KW, :]
    return (jnp.real(full), jnp.imag(full))

def from_spectrum(real_part, imag_part):
    spectrum = lax.complex(real_part, imag_part)
    padded = jnp.pad(spectrum, ((0, 0), (0, LON // 2 + 1 - KW), (0, 0)))
    return jnp.fft.irfft2(padded, s=(H, LON), axes=(0, 1), norm='ortho')

def reference(stash, piece_map, gain_one, spec_one, bias_one, spec_two, bias_two, gain_two, fc_one, bias_fc, fc_two, cotangent):
    holders = jnp.argsort(piece_map, axis=0).astype(jnp.int32)
    owners = jnp.arange(N_SPACE, dtype=jnp.int32)[None, :]
    gathered = stash[holders, owners]
    inputs = jnp.transpose(gathered, (2, 1, 0, 3)).reshape(SAMPLES, H, LON, D)

    def per_sample(carry, pair):
        sample_input, sample_cot = pair
        base_field = sample_input.astype(jnp.float32)
        normed, pull_one = jax.vjp(layer_norm, base_field, gain_one)
        spectrum, pull_spectrum = jax.vjp(to_spectrum, normed)
        mixed_spec, pull_mix = jax.vjp(spectral_mlp, spectrum[0], spectrum[1], spec_one, bias_one, spec_two, bias_two)
        spatial, pull_back = jax.vjp(from_spectrum, mixed_spec[0], mixed_spec[1])
        mixed_field = base_field + normed + spatial
        normed_two, pull_two = jax.vjp(layer_norm, mixed_field, gain_two)
        normed_flat = normed_two.astype(jnp.bfloat16).reshape(H * LON, D)
        hidden_pre = jnp.dot(normed_flat, fc_one, preferred_element_type=jnp.float32) + bias_fc
        active, pull_gate = jax.vjp(smooth_gate, hidden_pre)
        active_flat = active.astype(jnp.bfloat16)
        upstream = sample_cot.reshape(H * LON, D)
        grad_active = jnp.dot(upstream, fc_two.T, preferred_element_type=jnp.float32)
        grad_hidden = pull_gate(grad_active)[0]
        grad_hidden_flat = grad_hidden.astype(jnp.bfloat16)
        grad_normed_two = jnp.dot(grad_hidden_flat, fc_one.T, preferred_element_type=jnp.float32)
        term_one = jnp.dot(normed_flat.T, grad_hidden_flat, preferred_element_type=jnp.float32)
        term_two = jnp.dot(upstream.T, active_flat, preferred_element_type=jnp.float32)
        grad_mixed_norm, grad_gain_two = pull_two(grad_normed_two.reshape(H, LON, D))
        grad_mixed = sample_cot.astype(jnp.float32) + grad_mixed_norm
        grad_spectral = pull_back(grad_mixed)
        pulled = pull_mix(grad_spectral)
        grad_normed = grad_mixed + pull_spectrum((pulled[0], pulled[1]))[0]
        grad_base, grad_gain_one = pull_one(grad_normed)
        grad_sample = grad_mixed + grad_base
        bias_sum = lax.optimization_barrier(jnp.sum(grad_hidden, axis=0))
        out_sum = lax.optimization_barrier(jnp.sum(sample_cot.astype(jnp.float32), axis=(0, 1)))
        updates = (term_one, term_two, bias_sum, out_sum, grad_gain_one, grad_gain_two, pulled[2], pulled[3], pulled[4], pulled[5])
        carry = tuple((old + new for old, new in zip(carry, updates)))
        return (carry, grad_sample)
    start = (jnp.zeros((D, FF), jnp.float32), jnp.zeros((D, FF), jnp.float32), jnp.zeros((FF,), jnp.float32), jnp.zeros((D,), jnp.float32), jnp.zeros((D,), jnp.float32), jnp.zeros((D,), jnp.float32), jnp.zeros((2, BLOCKS, BLOCK, BLOCK), jnp.float32), jnp.zeros((2, D), jnp.float32), jnp.zeros((2, BLOCKS, BLOCK, BLOCK), jnp.float32), jnp.zeros((2, D), jnp.float32))
    sums, grad_input = lax.scan(per_sample, start, (inputs, cotangent))
    grad_scale = 1.0 / float(SAMPLES * H * LON) ** 0.5
    return (grad_input, sums[0] * grad_scale, sums[1].T * grad_scale, sums[2] * grad_scale, sums[3] * grad_scale, sums[4] * grad_scale, sums[5] * grad_scale, sums[6] * grad_scale, sums[7] * grad_scale, sums[8] * grad_scale, sums[9] * grad_scale)
```

```python
import math

import jax
import jax.numpy as jnp
from jax import lax
from jax.sharding import Mesh, PartitionSpec as P

KW = 64
SPACE = ("z", "y", "xh", "c")
EVERY = ("dp",) + SPACE
CHIPS = ("dp", "z", "y", "xh")

epsilon = 1e-05
highest = lax.Precision.HIGHEST
bf16 = jnp.bfloat16
f32 = jnp.float32


def exchange(values, axes):
    return lax.all_to_all(values, axes, split_axis=0, concat_axis=0, tiled=True)


def layer_norm(values, gain_vector):
    centred = values - jnp.mean(values, axis=-1, keepdims=True)
    spread = jnp.mean(centred * centred, axis=-1, keepdims=True)
    return centred * lax.rsqrt(spread + epsilon) * gain_vector


def smooth_gate(values):
    return jax.nn.gelu(values, approximate=True)


def block_mix(real_part, imag_part, weights, biases):
    blocks = weights.shape[1]
    width_block = weights.shape[2]
    leading = real_part.shape[:-1]
    real_blocks = real_part.reshape(leading + (blocks, width_block))
    imag_blocks = imag_part.reshape(leading + (blocks, width_block))
    bias_real = biases[0].reshape(blocks, width_block)
    bias_imag = biases[1].reshape(blocks, width_block)
    new_real = (
        jnp.einsum("...ni,nio->...no", real_blocks, weights[0], precision=highest)
        - jnp.einsum("...ni,nio->...no", imag_blocks, weights[1], precision=highest)
        + bias_real
    )
    new_imag = (
        jnp.einsum("...ni,nio->...no", real_blocks, weights[1], precision=highest)
        + jnp.einsum("...ni,nio->...no", imag_blocks, weights[0], precision=highest)
        + bias_imag
    )
    return (
        new_real.reshape(leading + (blocks * width_block,)),
        new_imag.reshape(leading + (blocks * width_block,)),
    )


def spectral_mlp(spec_real, spec_imag, spec_one, bias_one, spec_two, bias_two):
    inner_real, inner_imag = block_mix(spec_real, spec_imag, spec_one, bias_one)
    return block_mix(smooth_gate(inner_real), smooth_gate(inner_imag), spec_two, bias_two)


def wave_tables(length, total_modes):
    positions = jnp.arange(length, dtype=jnp.int32)
    frequency = jnp.arange(total_modes, dtype=jnp.int32)
    phases = positions[:, None] * frequency[None, :] % length
    angles = phases.astype(f32) * (2.0 * math.pi / length)
    factor = 1.0 / math.sqrt(length)
    return (jnp.cos(angles) * factor, jnp.sin(angles) * factor)


def meridian_apply(table, field):
    return jnp.einsum("hk,hbd->kbd", table, field, precision=highest)


def meridian_forward(real_part, imag_part, merid_cos, merid_sin):
    new_real = meridian_apply(merid_cos, real_part) + meridian_apply(merid_sin, imag_part)
    new_imag = meridian_apply(merid_cos, imag_part) - meridian_apply(merid_sin, real_part)
    return (new_real, new_imag)


def meridian_inverse(real_part, imag_part, merid_cos, merid_sin):
    new_real = meridian_apply(merid_cos, real_part) - meridian_apply(merid_sin, imag_part)
    new_imag = meridian_apply(merid_cos, imag_part) + meridian_apply(merid_sin, real_part)
    return (new_real, new_imag)


def zonal_project(field, table):
    return jnp.einsum("bwd,wk->kbd", field, table, precision=highest)


def zonal_expand(field, table):
    return jnp.einsum("kbd,wk->bwd", field, table, precision=highest)


def pack_pair(real_part, imag_part):
    return jnp.concatenate((real_part, imag_part), axis=1).astype(bf16)


def unpack_pair(both, samples):
    wide = both.astype(f32)
    return wide[:, :samples], wide[:, samples:]


def local(
    stash,
    piece_map,
    gain_one,
    spec_one,
    bias_one,
    spec_two,
    bias_two,
    gain_two,
    fc_one,
    bias_fc,
    fc_two,
    cotangent,
):
    samples, _, lon_cells, width = cotangent.shape
    lat_total = lax.axis_size(SPACE)
    tokens = samples * lon_cells
    hidden = fc_one.shape[1]
    arrived = exchange(stash[0], SPACE)
    ordering = jnp.argsort(piece_map[:, 0])
    placed = jnp.take(arrived, ordering, axis=0)
    inputs = jnp.transpose(placed, (1, 0, 2)).reshape(samples, lon_cells, width)
    base_field = inputs.astype(f32)
    cot = cotangent.reshape(samples, lon_cells, width)
    zonal_cos, zonal_sin = wave_tables(lon_cells, KW)
    doubling = jnp.where(jnp.arange(KW) == 0, 1.0, 2.0).astype(f32)
    back_cos = zonal_cos * doubling
    back_sin = zonal_sin * doubling
    merid_cos, merid_sin = wave_tables(lat_total, lat_total)
    centred = base_field - jnp.mean(base_field, axis=-1, keepdims=True)
    spread = jnp.mean(centred * centred, axis=-1, keepdims=True)
    rstd = lax.rsqrt(spread + epsilon)
    xhat = centred * rstd
    normed = xhat * gain_one
    sent = exchange(
        pack_pair(zonal_project(xhat, zonal_cos), -zonal_project(xhat, zonal_sin)), SPACE
    )
    modes_real, modes_imag = unpack_pair(sent, samples)
    plain_real, plain_imag = meridian_forward(modes_real, modes_imag, merid_cos, merid_sin)
    mixed_spec, pull_mix = jax.vjp(
        spectral_mlp,
        plain_real * gain_one,
        plain_imag * gain_one,
        spec_one,
        bias_one,
        spec_two,
        bias_two,
    )
    back = pack_pair(*meridian_inverse(mixed_spec[0], mixed_spec[1], merid_cos, merid_sin))
    rows_real, rows_imag = unpack_pair(exchange(back, SPACE), samples)
    spatial = zonal_expand(rows_real, back_cos) - zonal_expand(rows_imag, back_sin)
    mixed_field = base_field + normed + spatial
    normed_two, pull_two = jax.vjp(layer_norm, mixed_field, gain_two)
    normed_flat = normed_two.astype(bf16).reshape(tokens, width)
    hidden_pre = jnp.dot(normed_flat, fc_one, preferred_element_type=f32) + bias_fc
    active, pull_gate = jax.vjp(smooth_gate, hidden_pre)
    active_flat = active.astype(bf16)
    upstream = cot.reshape(tokens, width)
    grad_active = jnp.einsum("td,fd->tf", upstream, fc_two, preferred_element_type=f32)
    grad_hidden = pull_gate(grad_active)[0]
    grad_hidden_flat = grad_hidden.astype(bf16)
    grad_normed_two = jnp.einsum("tf,df->td", grad_hidden_flat, fc_one, preferred_element_type=f32)
    chips = lax.axis_size(CHIPS)
    share = hidden // (2 * chips)
    term_one = jnp.einsum(
        "tf,td->fd", grad_hidden_flat, normed_flat, preferred_element_type=f32
    ).astype(bf16)
    term_two = jnp.einsum(
        "tf,td->fd", active_flat, upstream, preferred_element_type=f32
    ).astype(bf16)
    core = lax.axis_index("c")
    paired = []
    for term in (term_one, term_two):
        split = term.reshape(chips, 2, share, width)
        other = lax.dynamic_index_in_dim(split, 1 - core, 1, keepdims=False)
        mine = lax.dynamic_index_in_dim(split, core, 1, keepdims=False)
        got = lax.ppermute(other, "c", [(0, 1), (1, 0)])
        paired.append((mine.astype(f32) + got.astype(f32)).astype(bf16))
    summed = jnp.sum(
        exchange(jnp.concatenate(paired, axis=1), CHIPS).astype(f32), axis=0
    )
    grad_mixed_norm, grad_gain_two = pull_two(grad_normed_two.reshape(mixed_field.shape))
    grad_mixed = cot.astype(f32) + grad_mixed_norm
    back_sent = exchange(
        pack_pair(zonal_project(grad_mixed, back_cos), -zonal_project(grad_mixed, back_sin)),
        SPACE,
    )
    grad_modes_real, grad_modes_imag = unpack_pair(back_sent, samples)
    grad_out = meridian_forward(grad_modes_real, grad_modes_imag, merid_cos, merid_sin)
    pulled = pull_mix(grad_out)
    home = pack_pair(*meridian_inverse(pulled[0], pulled[1], merid_cos, merid_sin))
    home_real, home_imag = unpack_pair(exchange(home, SPACE), samples)
    from_spectrum = zonal_expand(home_real, zonal_cos) - zonal_expand(home_imag, zonal_sin)
    scaled = (grad_mixed + from_spectrum) * gain_one
    grad_base = rstd * (
        scaled
        - jnp.mean(scaled, axis=-1, keepdims=True)
        - xhat * jnp.mean(scaled * xhat, axis=-1, keepdims=True)
    )
    grad_input = grad_mixed + grad_base
    grad_gain_one = (
        jnp.sum(grad_mixed * xhat, axis=(0, 1))
        + jnp.sum(pulled[0] * plain_real + pulled[1] * plain_imag, axis=(0, 1))
    )
    bias_sum = jnp.sum(grad_hidden, axis=0)
    out_sum = jnp.sum(cot, axis=(0, 1), dtype=f32)
    ranks = lax.axis_size(EVERY)
    blocks, inner = spec_one.shape[1:3]
    vectors = (
        bias_sum,
        out_sum,
        grad_gain_one,
        grad_gain_two,
        pulled[3].reshape(-1),
        pulled[5].reshape(-1),
    )
    lines = 4 * blocks * inner // ranks
    spare = 128 - inner
    vector = jnp.concatenate(vectors)
    deep = -(-vector.shape[0] // (ranks * spare))
    vector = jnp.pad(vector, (0, ranks * spare * deep - vector.shape[0]))
    vector = jnp.pad(
        vector.reshape(ranks, deep, spare), ((0, 0), (0, lines - deep), (0, 0))
    )
    square = jnp.stack((pulled[2], pulled[4])).reshape(ranks, lines, inner)
    packet = jnp.concatenate((square, vector), axis=2).astype(bf16)
    total = jnp.sum(exchange(packet, EVERY).astype(f32), axis=0)
    grad_scale = 1.0 / math.sqrt(samples * lax.axis_size("dp") * lat_total * lon_cells)
    total = (total * grad_scale).astype(bf16)
    whole = exchange(jnp.broadcast_to(total, (ranks,) + total.shape), EVERY).astype(f32)
    spec_grads = whole[:, :, :inner].reshape((2,) + spec_one.shape)
    flat = whole[:, :deep, inner:].reshape(-1)
    pieces, at = [], 0
    for item in vectors:
        pieces.append(lax.slice_in_dim(flat, at, at + item.shape[0]))
        at += item.shape[0]
    return (
        grad_input.reshape(cotangent.shape),
        summed[:share].T * grad_scale,
        summed[share:] * grad_scale,
        pieces[0],
        pieces[1],
        pieces[2],
        pieces[3],
        spec_grads[0],
        pieces[4].reshape(bias_one.shape),
        spec_grads[1],
        pieces[5].reshape(bias_two.shape),
    )


def solution(mesh):
    fine = Mesh(mesh.devices.reshape(2, 4, 4, 2, 2), EVERY)
    placed = (
        P(SPACE, None, "dp", None),
        P(None, SPACE),
        P(),
        P(),
        P(),
        P(),
        P(),
        P(),
        P(),
        P(),
        P(),
        P("dp", SPACE, None, None),
    )
    return jax.shard_map(
        local,
        mesh=fine,
        in_specs=placed,
        out_specs=(
            P("dp", SPACE, None, None),
            P(None, EVERY),
            P(EVERY, None),
        )
        + (P(),) * 8,
        check_vma=False,
    )
```

```python
import math

import jax
import jax.numpy as jnp
import numpy as np
from jax import lax
from jax.experimental import pallas as pl
from jax.experimental.pallas import tpu as pltpu
from jax.sharding import Mesh, PartitionSpec as P

KW = 64
SPACE = ("z", "y", "xh", "c")
EVERY = ("dp",) + SPACE

epsilon = 1e-05
bf16 = jnp.bfloat16
f32 = jnp.float32
ROOT = math.sqrt(2.0 / math.pi)
CUBE = 0.044715


def exchange(values, axes):
    return lax.all_to_all(values, axes, split_axis=0, concat_axis=0, tiled=True)


def high_low(table):
    table = np.asarray(table, np.float32)
    high = table.astype(bf16)
    low = (table - high.astype(np.float32)).astype(bf16)
    return np.stack((high, low))


def zonal_tables(samples, lon):
    angle = 2.0 * np.pi * (np.outer(np.arange(KW), np.arange(lon)) % lon) / lon
    both = np.stack((np.cos(angle), -np.sin(angle)), axis=1) / math.sqrt(lon)
    eye = np.eye(samples)
    plain = np.einsum("krw,ab->krabw", both, eye)
    plain = plain.reshape(KW * 2 * samples, samples * lon)
    double = np.where(np.arange(KW) == 0, 1.0, 2.0)
    doubled = plain * np.repeat(double, 2 * samples)[:, None]
    return plain, doubled


def meridian_table(samples, lat):
    angle = 2.0 * np.pi * (np.outer(np.arange(lat), np.arange(lat)) % lat) / lat
    cos, sin = np.cos(angle) / math.sqrt(lat), np.sin(angle) / math.sqrt(lat)
    turn = np.stack((np.stack((cos, sin), -1), np.stack((-sin, cos), -1)))
    whole = np.einsum("qksr,ab->qkasrb", turn, np.eye(samples))
    return whole.reshape(2 * lat * samples, lat * 2 * samples)


def dot(a, b, ca=1, cb=0):
    return lax.dot_general(a, b, (((ca,), (cb,)), ((), ())), preferred_element_type=f32)


def split(a):
    high = a.astype(bf16)
    return high, (a - high.astype(f32)).astype(bf16)


def dot3(a, b, ca=1, cb=0):
    return dot(a[0], b[0], ca, cb) + (dot(a[1], b[0], ca, cb) + dot(a[0], b[1], ca, cb))


def dot2(table, b):
    return dot(table[0], b) + dot(table[1], b)


def bend(x):
    return jnp.tanh(ROOT * (x + CUBE * (x * x * x)))


def smooth_gate(x):
    return 0.5 * x * (1.0 + bend(x))


def gate_slope(x):
    t = bend(x)
    return 0.5 * (1.0 + t) + (0.5 * x) * (1.0 - t * t) * (ROOT * (1.0 + (3.0 * CUBE) * (x * x)))


def normalise(x):
    centred = x - jnp.mean(x, axis=-1, keepdims=True)
    rstd = lax.rsqrt(jnp.mean(centred * centred, axis=-1, keepdims=True) + epsilon)
    return centred * rstd, rstd


def norm_pull(grad, gain, xhat, rstd):
    scaled = grad * gain
    return rstd * (
        scaled
        - jnp.mean(scaled, axis=-1, keepdims=True)
        - xhat * jnp.mean(scaled * xhat, axis=-1, keepdims=True)
    )


def to_rows(block):
    return block.astype(f32).reshape(block.shape[0] * block.shape[1], block.shape[2]).astype(bf16)


def to_pieces(values):
    return values.reshape(values.shape[0] // 4, 4, values.shape[1]).astype(bf16)


def project(values, table_ref, out_ref):
    half = out_ref.shape[2]
    ranks = out_ref.shape[0] // 2
    found = dot3((table_ref[0], table_ref[1]), split(values))
    out_ref[:ranks] = to_pieces(found[:, :half])
    out_ref[ranks:] = to_pieces(found[:, half:])


def expand(rows_ref, table_ref):
    ranks = rows_ref.shape[0] // 2
    table = (table_ref[0], table_ref[1])
    return jnp.concatenate(
        [dot2(table, to_rows(rows_ref[ranks * h : ranks * (h + 1), :4])) for h in range(2)], axis=1
    )


def first_kernel(base_ref, table_ref, sent_ref, xhat_ref, rstd_ref):
    xhat, rstd = normalise(base_ref[...])
    xhat_ref[...] = xhat
    rstd_ref[...] = jnp.broadcast_to(rstd, rstd_ref.shape)
    project(xhat, table_ref, sent_ref)


def field_kernel(rows_ref, table_ref, base_ref, xhat_ref, gains_ref, flat_ref, xhat2_ref, rstd2_ref):
    mixed = base_ref[...] + xhat_ref[...] * gains_ref[0:1] + expand(rows_ref, table_ref)
    xhat2, rstd2 = normalise(mixed)
    xhat2_ref[...] = xhat2
    rstd2_ref[...] = jnp.broadcast_to(rstd2, rstd2_ref.shape)
    flat_ref[...] = (xhat2 * gains_ref[1:2]).astype(bf16)


def back_kernel(
    grad_ref, cot_ref, xhat2_ref, rstd2_ref, xhat_ref, gains_ref, table_ref, sent_ref, mixed_ref, sums_ref
):
    grad = grad_ref[...]
    xhat2 = xhat2_ref[...]
    cot = cot_ref[...].astype(f32)
    mixed = cot + norm_pull(grad, gains_ref[1:2], xhat2, rstd2_ref[:, 0:1])
    mixed_ref[...] = mixed
    sums_ref[0:1] = jnp.sum(cot, axis=0, keepdims=True)
    sums_ref[1:2] = jnp.sum(mixed * xhat_ref[...], axis=0, keepdims=True)
    sums_ref[2:3] = jnp.sum(grad * xhat2, axis=0, keepdims=True)
    project(mixed, table_ref, sent_ref)


def last_kernel(rows_ref, table_ref, mixed_ref, xhat_ref, rstd_ref, gains_ref, out_ref):
    mixed = mixed_ref[...]
    grad = mixed + expand(rows_ref, table_ref)
    result = mixed + norm_pull(grad, gains_ref[0:1], xhat_ref[...], rstd_ref[:, 0:1])
    cells = out_ref.shape[2]
    for sample in range(out_ref.shape[0]):
        out_ref[sample, 0] = result[cells * sample : cells * (sample + 1)]


def mix(real, imag, weights, index):
    wr = (weights[0, index], weights[1, index])
    wi = (weights[0, index + 1], weights[1, index + 1])
    real, imag = split(real), split(imag)
    return dot3(real, wr) - dot3(imag, wi), dot3(real, wi) + dot3(imag, wr)


def mix_pull(real, imag, weights, index):
    wr = (weights[0, index], weights[1, index])
    wi = (weights[0, index + 1], weights[1, index + 1])
    return (
        dot3(real, wr, 1, 1) + dot3(imag, wi, 1, 1),
        dot3(imag, wr, 1, 1) - dot3(real, wi, 1, 1),
    )


def compact(full, inner):
    lane = lax.broadcasted_iota(jnp.int32, (inner, full.shape[1]), 1)
    kept = None
    for j in range(full.shape[0] // inner):
        here = (lane >= inner * j) & (lane < inner * (j + 1))
        part = jnp.where(here, full[inner * j : inner * (j + 1)], 0.0)
        kept = part if kept is None else kept + part
    return kept


def spectral_kernel(rows_ref, table_ref, turned_ref, weights_ref, vectors_ref, sent_ref, plain_ref, pre_ref):
    ranks = rows_ref.shape[0] // 2
    half = 2 * ranks
    table = (table_ref[0], table_ref[1])
    for dp in range(2):
        found = dot2(table, to_rows(rows_ref[ranks * dp : ranks * (dp + 1)]))
        plain_ref[0, half * dp : half * (dp + 1)] = found[:half]
        plain_ref[1, half * dp : half * (dp + 1)] = found[half:]
    gain = vectors_ref[0:1]
    real, imag = mix(plain_ref[0] * gain, plain_ref[1] * gain, weights_ref, 0)
    real = real + vectors_ref[1:2]
    imag = imag + vectors_ref[2:3]
    pre_ref[0] = real
    pre_ref[1] = imag
    real, imag = mix(smooth_gate(real), smooth_gate(imag), weights_ref, 2)
    real = real + vectors_ref[3:4]
    imag = imag + vectors_ref[4:5]
    turned = (turned_ref[0], turned_ref[1])
    for dp in range(2):
        both = jnp.concatenate(
            (real[half * dp : half * (dp + 1)], imag[half * dp : half * (dp + 1)]), axis=0
        )
        sent_ref[ranks * dp : ranks * (dp + 1)] = to_pieces(dot3(turned, split(both)))


def spectral_back_kernel(
    rows_ref, table_ref, turned_ref, weights_ref, vectors_ref, plain_ref, pre_ref, sent_ref, grads_ref, sums_ref
):
    ranks = rows_ref.shape[0] // 2
    half = 2 * ranks
    inner = grads_ref.shape[1]
    table = (table_ref[0], table_ref[1])
    found = [
        dot2(table, to_rows(rows_ref[ranks * dp : ranks * (dp + 1)])) for dp in range(2)
    ]
    real = jnp.concatenate((found[0][:half], found[1][:half]), axis=0)
    imag = jnp.concatenate((found[0][half:], found[1][half:]), axis=0)

    def weight_grads(first, second, grad_real, grad_imag, at):
        grads_ref[at] = compact(
            dot3(first, grad_real, 0, 0) + dot3(second, grad_imag, 0, 0), inner
        )
        grads_ref[at + 1] = compact(
            dot3(first, grad_imag, 0, 0) - dot3(second, grad_real, 0, 0), inner
        )

    sums_ref[3:4] = jnp.sum(real, axis=0, keepdims=True)
    sums_ref[4:5] = jnp.sum(imag, axis=0, keepdims=True)
    pre_real, pre_imag = pre_ref[0], pre_ref[1]
    real, imag = split(real), split(imag)
    weight_grads(split(smooth_gate(pre_real)), split(smooth_gate(pre_imag)), real, imag, 2)
    real, imag = mix_pull(real, imag, weights_ref, 2)
    real = real * gate_slope(pre_real)
    imag = imag * gate_slope(pre_imag)
    sums_ref[1:2] = jnp.sum(real, axis=0, keepdims=True)
    sums_ref[2:3] = jnp.sum(imag, axis=0, keepdims=True)
    gain = vectors_ref[0:1]
    real, imag = split(real), split(imag)
    plain_real, plain_imag = plain_ref[0], plain_ref[1]
    weight_grads(split(plain_real * gain), split(plain_imag * gain), real, imag, 0)
    real, imag = mix_pull(real, imag, weights_ref, 0)
    sums_ref[0:1] = jnp.sum(real * plain_real + imag * plain_imag, axis=0, keepdims=True)
    turned = (turned_ref[0], turned_ref[1])
    for dp in range(2):
        both = jnp.concatenate(
            (real[half * dp : half * (dp + 1)], imag[half * dp : half * (dp + 1)]), axis=0
        )
        sent_ref[ranks * dp : ranks * (dp + 1)] = to_pieces(dot3(turned, split(both)))


def call(kernel, outs, *args, grant=16, **more):
    return pl.pallas_call(
        kernel,
        out_shape=[jax.ShapeDtypeStruct(shape, kind) for shape, kind in outs],
        compiler_params=pltpu.CompilerParams(vmem_limit_bytes=grant << 20),
        **more,
    )(*args)


def whole(shape):
    zeros = (0,) * len(shape)
    return pl.BlockSpec(shape, lambda *_: zeros)


SMEM = pl.BlockSpec(memory_space=pltpu.SMEM)


def weight_kernel(place_ref, grad_ref, active_ref, flat_ref, cot_ref, mine_ref, other_ref):
    step = pl.program_id(0)
    low, at_z = step // 4, step % 4
    share = mine_ref.shape[1] // 2
    one = dot(grad_ref[...], flat_ref[...], 0, 0)
    two = dot(active_ref[...], cot_ref[...], 0, 0)
    x, y, core = place_ref[0], place_ref[1], place_ref[3]
    first = core == 0
    for at_y in range(4):
        for at_xh in range(2):
            at_x = 2 * at_xh + low
            at = (at_y * 2 + at_xh) * 2 * share
            pair = [
                jnp.concatenate((one[a : a + share], two[a : a + share])) for a in (at, at + share)
            ]
            spot = (
                ((at_x - x) & 3) * 16 + at_y * 4 + at_z,
                ((at_y - y) & 3) * 16 + at_z * 4 + at_x,
            )
            mine_ref[jnp.where(first, spot[0], spot[1])] = jnp.where(first, pair[0], pair[1])
            other_ref[jnp.where(first, spot[1], spot[0])] = jnp.where(
                first, pair[1], pair[0]
            ).astype(bf16)


def pair_kernel(mine_ref, came_ref, *outs):
    for r in range(3):
        here = pl.ds(16 * (r + 1), 16)
        outs[r][...] = (mine_ref[here] + came_ref[here].astype(f32)).astype(bf16)


def plane_kernel(place_ref, mine_ref, came_ref, *refs):
    got, own_ref, outs = refs[:3], refs[3], refs[4:]
    for d in range(4):
        for i in range(4):
            at = 4 * ((place_ref[4] + d) & 3) + i
            total = mine_ref[at] + came_ref[at].astype(f32)
            for r in range(3):
                total = total + got[r][at].astype(f32)
            if d == 0:
                own_ref[i] = total
            else:
                outs[d - 1][i] = total.astype(bf16)


def line_kernel(place_ref, own_in_ref, *refs):
    got, own_ref, outs = refs[:3], refs[3], refs[4:]
    for d in range(4):
        at = (place_ref[5] + d) & 3
        total = own_in_ref[at]
        for r in range(3):
            total = total + got[r][at].astype(f32)
        if d == 0:
            own_ref[...] = total
        else:
            outs[d - 1][...] = total.astype(bf16)


def point_kernel(scale, own_ref, *refs):
    got, one_ref, two_ref = refs[:3], refs[3], refs[4]
    share = two_ref.shape[0]
    total = own_ref[...]
    for r in range(3):
        total = total + got[r][...].astype(f32)
    total = total * scale
    one_ref[...] = total[:share]
    two_ref[...] = total[share:]


def neighbours(stage, far):
    pairs = []
    for rank in range(128):
        core, xh, y, z, low = rank & 1, (rank >> 1) & 1, (rank >> 2) & 3, (rank >> 4) & 3, rank >> 6
        at = [2 * xh + low, y, z]
        axis = (stage + core) % 3
        at[axis] = (at[axis] + far) & 3
        x, y, z = at
        pairs.append((rank, ((x & 1) << 6) | (z << 4) | (y << 2) | ((x >> 1) << 1) | core))
    return pairs


def send_all(pieces, stage):
    return [lax.ppermute(pieces[r], EVERY, neighbours(stage, r + 1)) for r in range(3)]


def after(value, others):
    return lax.optimization_barrier((value, others))[0]


def weight_place():
    core = lax.axis_index("c")
    x = 2 * lax.axis_index("xh") + lax.axis_index("dp")
    y, z = lax.axis_index("y"), lax.axis_index("z")
    first = core == 0
    return jnp.stack((x, y, z, core, jnp.where(first, y, z), jnp.where(first, z, x))).astype(
        jnp.int32
    )


def weight_start(place, grad_hidden, active, flat, cot):
    tokens, hidden = grad_hidden.shape
    width = flat.shape[1]
    share = hidden // 128
    full = (64, 2 * share, width)
    ahead = pl.BlockSpec((tokens, hidden // 8), lambda g: (0, g))
    mine, other = call(
        weight_kernel,
        [(full, f32), (full, bf16)],
        place,
        grad_hidden,
        active,
        flat,
        cot,
        grant=28,
        grid=(8,),
        in_specs=[SMEM, ahead, ahead, whole(flat.shape), whole(cot.shape)],
        out_specs=[whole(full)] * 2,
        cost_estimate=pl.CostEstimate(
            flops=4 * tokens * hidden * width, bytes_accessed=14 << 20, transcendentals=0
        ),
    )
    came = lax.ppermute(other, "c", [(0, 1), (1, 0)])
    sent = call(pair_kernel, [((16,) + full[1:], bf16)] * 3, mine, came, grant=24)
    return mine, came, sent


def weight_second(place, mine, came, got):
    line = mine.shape[1:]
    cube, row = (16,) + line, (4,) + line
    head = pl.BlockSpec(cube, lambda g: (0, 0, 0))
    return call(
        plane_kernel,
        [(row, f32)] + [(row, bf16)] * 3,
        place,
        mine,
        came,
        *got,
        grant=20,
        grid=(1,),
        in_specs=[SMEM, head, head] + [whole(cube)] * 3,
        out_specs=[whole(row)] * 4,
    )


def weight_third(place, own, got):
    row = own.shape
    line = row[1:]
    return call(
        line_kernel,
        [(line, f32)] + [(line, bf16)] * 3,
        place,
        own,
        *got,
        grid=(1,),
        in_specs=[SMEM, whole(row)] + [whole(row)] * 3,
        out_specs=[whole(line)] * 4,
    )


def block_diagonal(weights):
    blocks, inner = weights.shape[1:3]
    tall = weights.reshape(2, blocks * inner, inner)
    wide = jnp.concatenate((tall,) * blocks, axis=2)
    row = lax.broadcasted_iota(jnp.int32, wide.shape, 1) // inner
    lane = lax.broadcasted_iota(jnp.int32, wide.shape, 2) // inner
    return jnp.where(row == lane, wide, 0.0)


def local(
    stash,
    piece_map,
    gain_one,
    spec_one,
    bias_one,
    spec_two,
    bias_two,
    gain_two,
    fc_one,
    bias_fc,
    fc_two,
    cotangent,
):
    samples, _, lon_cells, width = cotangent.shape
    lat_total = lax.axis_size(SPACE)
    ranks = lax.axis_size(EVERY)
    tokens = samples * lon_cells
    hidden = fc_one.shape[1]
    half = width // 2
    rows = 4 * ranks
    piece = (ranks, 4, half)
    plain_table, doubled_table = zonal_tables(samples, lon_cells)
    meridian = meridian_table(samples, lat_total)
    down, back_down = high_low(plain_table), high_low(doubled_table)
    up, back_up = high_low(plain_table.T), high_low(doubled_table.T)
    forward, inverse = high_low(meridian), high_low(meridian.T)

    arrived = exchange(stash[0], SPACE)
    ordering = jnp.argsort(piece_map[:, 0])
    placed = jnp.take(arrived, ordering, axis=0)
    base = jnp.transpose(placed, (1, 0, 2)).reshape(tokens, width).astype(f32)
    upstream = cotangent.reshape(tokens, width)
    gains = jnp.stack((gain_one, gain_two))

    which = lax.axis_index("dp")
    blocks, inner = spec_one.shape[1:3]
    mine = blocks // 2
    both = jnp.concatenate(
        [
            block_diagonal(lax.dynamic_slice_in_dim(w, which * mine, mine, 1))
            for w in (spec_one, spec_two)
        ]
    )
    weights = jnp.stack(split(both))
    vectors = lax.dynamic_slice_in_dim(
        jnp.concatenate((gain_one[None], bias_one, bias_two)), which * half, half, 1
    )

    sent, xhat, rstd = call(
        first_kernel,
        [(piece, bf16), ((tokens, width), f32), ((tokens, 128), f32)],
        base,
        down,
    )
    got = exchange(sent, EVERY)
    sent, plain, pre = call(
        spectral_kernel,
        [(piece, bf16), ((2, rows // 2, half), f32), ((2, rows // 2, half), f32)],
        got,
        forward,
        inverse,
        weights,
        vectors,
    )
    got = exchange(sent, EVERY)
    normed_flat, xhat2, rstd2 = call(
        field_kernel,
        [((tokens, width), bf16), ((tokens, width), f32), ((tokens, 128), f32)],
        got,
        back_up,
        base,
        xhat,
        gains,
    )
    hidden_pre = jnp.dot(normed_flat, fc_one, preferred_element_type=f32) + bias_fc
    active_flat = smooth_gate(hidden_pre).astype(bf16)
    grad_active = jnp.einsum("td,fd->tf", upstream, fc_two, preferred_element_type=f32)
    grad_hidden = grad_active * gate_slope(hidden_pre)
    grad_hidden_flat = grad_hidden.astype(bf16)
    grad_normed_two = jnp.einsum("tf,df->td", grad_hidden_flat, fc_one, preferred_element_type=f32)
    sent, grad_mixed, sums = call(
        back_kernel,
        [(piece, bf16), ((tokens, width), f32), ((3, width), f32)],
        grad_normed_two,
        upstream,
        xhat2,
        rstd2,
        xhat,
        gains,
        back_down,
    )
    got = exchange(sent, EVERY)

    grad_scale = 1.0 / math.sqrt(samples * lax.axis_size("dp") * lat_total * lon_cells)
    place = weight_place()
    kept, came, sent = weight_start(
        place, grad_hidden_flat, active_flat, normed_flat, upstream
    )
    first_got = send_all(sent, 0)
    got = after(got, sent)

    sent, grads, mix_sums = call(
        spectral_back_kernel,
        [(piece, bf16), ((4, inner, half), f32), ((5, half), f32)],
        got,
        forward,
        inverse,
        weights,
        vectors,
        plain,
        pre,
    )
    bias_sum = jnp.sum(grad_hidden, axis=0)
    row_sums = jnp.concatenate((bias_sum.reshape(-1, half), sums.reshape(-1, half)))
    nothing = jnp.zeros_like(mix_sums)
    lines = jnp.concatenate(
        (
            row_sums,
            jnp.where(which == 0, mix_sums, nothing),
            jnp.where(which == 0, nothing, mix_sums),
        )
    )
    lines = jnp.pad(lines, ((0, ranks - lines.shape[0]), (0, 0)))
    packet = jnp.concatenate(
        (
            sent,
            grads.astype(bf16).reshape(ranks, 3, half),
            lines.astype(bf16).reshape(ranks, 1, half),
        ),
        axis=1,
    )
    got = exchange(packet, EVERY)
    own, *sent = weight_second(place, kept, came, first_got)
    second_got = send_all(sent, 1)
    (grad_input,) = call(
        last_kernel,
        [(cotangent.shape, f32)],
        after(got, sent),
        up,
        grad_mixed,
        xhat,
        rstd,
        gains,
    )
    sides = jnp.sum(got[:, 4:].reshape(2, ranks // 2, 4, half).astype(f32), axis=1)
    total = jnp.concatenate(
        (sides[0, :3], sides[1, :3], sides[0, 3:] + sides[1, 3:], jnp.zeros((1, half), f32))
    )
    total = (total * grad_scale).astype(bf16)
    spread = exchange(jnp.broadcast_to(total, (ranks,) + total.shape), EVERY).astype(f32)
    own, *sent = weight_third(place, own, second_got)
    third_got = send_all(sent, 2)
    spread = after(spread, sent)
    squares = [
        spread[:, 3 * h : 3 * h + 3].reshape(2, 2, inner, mine, inner) for h in range(2)
    ]
    spec_grads = jnp.concatenate(
        [jnp.transpose(s, (0, 1, 3, 2, 4)) for s in squares], axis=2
    )
    lines = spread[:, 6]
    fc_lines = hidden // half
    bias_grad = lines[:fc_lines].reshape(hidden)
    small = lines[fc_lines : fc_lines + 6].reshape(3, width)
    sides = lines[fc_lines + 6 : fc_lines + 16].reshape(2, 5, half)
    sides = jnp.concatenate((sides[0], sides[1]), axis=1)
    grad_one, grad_two = call(
        lambda *refs: point_kernel(grad_scale, *refs),
        [((hidden // ranks, width), f32)] * 2,
        own,
        *third_got,
    )
    return (
        grad_input,
        grad_one.T,
        grad_two,
        bias_grad,
        small[0],
        small[1] + sides[0],
        small[2],
        spec_grads[0],
        sides[1:3],
        spec_grads[1],
        sides[3:5],
    )


def solution(mesh):
    fine = Mesh(mesh.devices.reshape(2, 4, 4, 2, 2), EVERY)
    placed = (
        P(SPACE, None, "dp", None),
        P(None, SPACE),
        P(),
        P(),
        P(),
        P(),
        P(),
        P(),
        P(),
        P(),
        P(),
        P("dp", SPACE, None, None),
    )
    return jax.shard_map(
        local,
        mesh=fine,
        in_specs=placed,
        out_specs=(
            P("dp", SPACE, None, None),
            P(None, EVERY),
            P(EVERY, None),
        )
        + (P(),) * 8,
        check_vma=False,
    )
```

```python
import math

import jax
import jax.numpy as jnp
import numpy as np
from jax import lax
from jax.experimental import pallas as pl
from jax.experimental.pallas import tpu as pltpu
from jax.sharding import Mesh, PartitionSpec as P

KW = 64
SPACE = ("z", "y", "xh", "c")
EVERY = ("dp",) + SPACE

epsilon = 1e-05
bf16 = jnp.bfloat16
f32 = jnp.float32
ROOT = math.sqrt(2.0 / math.pi)
CUBE = 0.044715


def exchange(values, axes):
    return lax.all_to_all(values, axes, split_axis=0, concat_axis=0, tiled=True)


def high_low(table):
    table = np.asarray(table, np.float32)
    high = table.astype(bf16)
    low = (table - high.astype(np.float32)).astype(bf16)
    return np.stack((high, low))


def zonal_tables(samples, lon):
    angle = 2.0 * np.pi * (np.outer(np.arange(KW), np.arange(lon)) % lon) / lon
    both = np.stack((np.cos(angle), -np.sin(angle)), axis=1) / math.sqrt(lon)
    eye = np.eye(samples)
    plain = np.einsum("krw,ab->krabw", both, eye)
    plain = plain.reshape(KW * 2 * samples, samples * lon)
    double = np.where(np.arange(KW) == 0, 1.0, 2.0)
    doubled = plain * np.repeat(double, 2 * samples)[:, None]
    return plain, doubled


def meridian_table(samples, lat):
    angle = 2.0 * np.pi * (np.outer(np.arange(lat), np.arange(lat)) % lat) / lat
    cos, sin = np.cos(angle) / math.sqrt(lat), np.sin(angle) / math.sqrt(lat)
    turn = np.stack((np.stack((cos, sin), -1), np.stack((-sin, cos), -1)))
    whole = np.einsum("qksr,ab->qkasrb", turn, np.eye(samples))
    return whole.reshape(2 * lat * samples, lat * 2 * samples)


def dot(a, b, ca=1, cb=0):
    return lax.dot_general(a, b, (((ca,), (cb,)), ((), ())), preferred_element_type=f32)


def split(a):
    high = a.astype(bf16)
    return high, (a - high.astype(f32)).astype(bf16)


def dot3(a, b, ca=1, cb=0):
    return dot(a[0], b[0], ca, cb) + (dot(a[1], b[0], ca, cb) + dot(a[0], b[1], ca, cb))


def dot2(table, b):
    return dot(table[0], b) + dot(table[1], b)


def bend(x):
    return jnp.tanh(ROOT * (x + CUBE * (x * x * x)))


def smooth_gate(x):
    return 0.5 * x * (1.0 + bend(x))


def gate_slope(x):
    t = bend(x)
    return 0.5 * (1.0 + t) + (0.5 * x) * (1.0 - t * t) * (ROOT * (1.0 + (3.0 * CUBE) * (x * x)))


def normalise(x):
    centred = x - jnp.mean(x, axis=-1, keepdims=True)
    rstd = lax.rsqrt(jnp.mean(centred * centred, axis=-1, keepdims=True) + epsilon)
    return centred * rstd, rstd


def norm_pull(grad, gain, xhat, rstd):
    scaled = grad * gain
    return rstd * (
        scaled
        - jnp.mean(scaled, axis=-1, keepdims=True)
        - xhat * jnp.mean(scaled * xhat, axis=-1, keepdims=True)
    )


def to_rows(block):
    return block.astype(f32).reshape(block.shape[0] * block.shape[1], block.shape[2]).astype(bf16)


def to_pieces(values):
    return values.reshape(values.shape[0] // 4, 4, values.shape[1]).astype(bf16)


def project(values, table_ref, out_ref):
    half = out_ref.shape[2]
    ranks = out_ref.shape[0] // 2
    found = dot3((table_ref[0], table_ref[1]), split(values))
    out_ref[:ranks] = to_pieces(found[:, :half])
    out_ref[ranks:] = to_pieces(found[:, half:])


def expand(rows_ref, table_ref):
    ranks = rows_ref.shape[0] // 2
    table = (table_ref[0], table_ref[1])
    return jnp.concatenate(
        [dot2(table, to_rows(rows_ref[ranks * h : ranks * (h + 1), :4])) for h in range(2)], axis=1
    )


def first_kernel(base_ref, table_ref, sent_ref, xhat_ref, rstd_ref):
    xhat, rstd = normalise(base_ref[...])
    xhat_ref[...] = xhat
    rstd_ref[...] = jnp.broadcast_to(rstd, rstd_ref.shape)
    project(xhat, table_ref, sent_ref)


def field_kernel(rows_ref, table_ref, base_ref, xhat_ref, gains_ref, flat_ref, xhat2_ref, rstd2_ref):
    mixed = base_ref[...] + xhat_ref[...] * gains_ref[0:1] + expand(rows_ref, table_ref)
    xhat2, rstd2 = normalise(mixed)
    xhat2_ref[...] = xhat2
    rstd2_ref[...] = jnp.broadcast_to(rstd2, rstd2_ref.shape)
    flat_ref[...] = (xhat2 * gains_ref[1:2]).astype(bf16)


def back_kernel(
    grad_ref, cot_ref, xhat2_ref, rstd2_ref, xhat_ref, gains_ref, table_ref, sent_ref, mixed_ref, sums_ref
):
    grad = grad_ref[...]
    xhat2 = xhat2_ref[...]
    cot = cot_ref[...].astype(f32)
    mixed = cot + norm_pull(grad, gains_ref[1:2], xhat2, rstd2_ref[:, 0:1])
    mixed_ref[...] = mixed
    sums_ref[0:1] = jnp.sum(cot, axis=0, keepdims=True)
    sums_ref[1:2] = jnp.sum(mixed * xhat_ref[...], axis=0, keepdims=True)
    sums_ref[2:3] = jnp.sum(grad * xhat2, axis=0, keepdims=True)
    project(mixed, table_ref, sent_ref)


def last_kernel(rows_ref, table_ref, mixed_ref, xhat_ref, rstd_ref, gains_ref, out_ref):
    mixed = mixed_ref[...]
    grad = mixed + expand(rows_ref, table_ref)
    result = mixed + norm_pull(grad, gains_ref[0:1], xhat_ref[...], rstd_ref[:, 0:1])
    cells = out_ref.shape[2]
    for sample in range(out_ref.shape[0]):
        out_ref[sample, 0] = result[cells * sample : cells * (sample + 1)]


def mix(real, imag, weights, index):
    wr = (weights[0, index], weights[1, index])
    wi = (weights[0, index + 1], weights[1, index + 1])
    real, imag = split(real), split(imag)
    return dot3(real, wr) - dot3(imag, wi), dot3(real, wi) + dot3(imag, wr)


def mix_pull(real, imag, weights, index):
    wr = (weights[0, index], weights[1, index])
    wi = (weights[0, index + 1], weights[1, index + 1])
    return (
        dot3(real, wr, 1, 1) + dot3(imag, wi, 1, 1),
        dot3(imag, wr, 1, 1) - dot3(real, wi, 1, 1),
    )


def compact(full, inner):
    lane = lax.broadcasted_iota(jnp.int32, (inner, full.shape[1]), 1)
    kept = None
    for j in range(full.shape[0] // inner):
        here = (lane >= inner * j) & (lane < inner * (j + 1))
        part = jnp.where(here, full[inner * j : inner * (j + 1)], 0.0)
        kept = part if kept is None else kept + part
    return kept


def spectral_kernel(rows_ref, table_ref, turned_ref, weights_ref, vectors_ref, sent_ref, plain_ref, pre_ref):
    ranks = rows_ref.shape[0] // 2
    half = 2 * ranks
    table = (table_ref[0], table_ref[1])
    for dp in range(2):
        found = dot2(table, to_rows(rows_ref[ranks * dp : ranks * (dp + 1)]))
        plain_ref[0, half * dp : half * (dp + 1)] = found[:half]
        plain_ref[1, half * dp : half * (dp + 1)] = found[half:]
    gain = vectors_ref[0:1]
    real, imag = mix(plain_ref[0] * gain, plain_ref[1] * gain, weights_ref, 0)
    real = real + vectors_ref[1:2]
    imag = imag + vectors_ref[2:3]
    pre_ref[0] = real
    pre_ref[1] = imag
    real, imag = mix(smooth_gate(real), smooth_gate(imag), weights_ref, 2)
    real = real + vectors_ref[3:4]
    imag = imag + vectors_ref[4:5]
    turned = (turned_ref[0], turned_ref[1])
    for dp in range(2):
        both = jnp.concatenate(
            (real[half * dp : half * (dp + 1)], imag[half * dp : half * (dp + 1)]), axis=0
        )
        sent_ref[ranks * dp : ranks * (dp + 1)] = to_pieces(dot3(turned, split(both)))


def spectral_back_kernel(
    rows_ref, table_ref, turned_ref, weights_ref, vectors_ref, plain_ref, pre_ref, sent_ref, grads_ref, sums_ref
):
    ranks = rows_ref.shape[0] // 2
    half = 2 * ranks
    inner = grads_ref.shape[1]
    table = (table_ref[0], table_ref[1])
    found = [
        dot2(table, to_rows(rows_ref[ranks * dp : ranks * (dp + 1)])) for dp in range(2)
    ]
    real = jnp.concatenate((found[0][:half], found[1][:half]), axis=0)
    imag = jnp.concatenate((found[0][half:], found[1][half:]), axis=0)

    def weight_grads(first, second, grad_real, grad_imag, at):
        grads_ref[at] = compact(
            dot3(first, grad_real, 0, 0) + dot3(second, grad_imag, 0, 0), inner
        )
        grads_ref[at + 1] = compact(
            dot3(first, grad_imag, 0, 0) - dot3(second, grad_real, 0, 0), inner
        )

    sums_ref[3:4] = jnp.sum(real, axis=0, keepdims=True)
    sums_ref[4:5] = jnp.sum(imag, axis=0, keepdims=True)
    pre_real, pre_imag = pre_ref[0], pre_ref[1]
    real, imag = split(real), split(imag)
    weight_grads(split(smooth_gate(pre_real)), split(smooth_gate(pre_imag)), real, imag, 2)
    real, imag = mix_pull(real, imag, weights_ref, 2)
    real = real * gate_slope(pre_real)
    imag = imag * gate_slope(pre_imag)
    sums_ref[1:2] = jnp.sum(real, axis=0, keepdims=True)
    sums_ref[2:3] = jnp.sum(imag, axis=0, keepdims=True)
    gain = vectors_ref[0:1]
    real, imag = split(real), split(imag)
    plain_real, plain_imag = plain_ref[0], plain_ref[1]
    weight_grads(split(plain_real * gain), split(plain_imag * gain), real, imag, 0)
    real, imag = mix_pull(real, imag, weights_ref, 0)
    sums_ref[0:1] = jnp.sum(real * plain_real + imag * plain_imag, axis=0, keepdims=True)
    turned = (turned_ref[0], turned_ref[1])
    for dp in range(2):
        both = jnp.concatenate(
            (real[half * dp : half * (dp + 1)], imag[half * dp : half * (dp + 1)]), axis=0
        )
        sent_ref[ranks * dp : ranks * (dp + 1)] = to_pieces(dot3(turned, split(both)))


def whole(shape):
    zeros = (0,) * len(shape)
    return pl.BlockSpec(shape, lambda *_: zeros)


def call(kernel, outs, *args, grant=16, grid=(1,), in_specs=None, out_specs=None, free=(), **more):
    in_specs = in_specs or [whole(a.shape) for a in args]
    return pl.pallas_call(
        kernel,
        out_shape=[pltpu.HBM(shape, kind) for shape, kind in outs],
        compiler_params=pltpu.CompilerParams(vmem_limit_bytes=grant << 20),
        grid=grid,
        in_specs=in_specs,
        out_specs=out_specs or [whole(shape) for shape, _ in outs],
        **more,
    )(
        *(
            a if spec is SMEM or i in free else pltpu.with_memory_space_constraint(a, pltpu.HBM)
            for i, (a, spec) in enumerate(zip(args, in_specs))
        )
    )


SMEM = pl.BlockSpec(memory_space=pltpu.SMEM)


def weight_kernel(place_ref, grad_ref, active_ref, flat_ref, cot_ref, mine_ref, other_ref):
    step = pl.program_id(0)
    low, at_z = step // 4, step % 4
    share = mine_ref.shape[1] // 2
    one = dot(grad_ref[...], flat_ref[...], 0, 0)
    two = dot(active_ref[...], cot_ref[...], 0, 0)
    x, y, core = place_ref[0], place_ref[1], place_ref[3]
    first = core == 0
    for at_y in range(4):
        for at_xh in range(2):
            at_x = 2 * at_xh + low
            at = (at_y * 2 + at_xh) * 2 * share
            pair = [
                jnp.concatenate((one[a : a + share], two[a : a + share])) for a in (at, at + share)
            ]
            spot = (
                ((at_x - x) & 3) * 16 + at_y * 4 + at_z,
                ((at_y - y) & 3) * 16 + at_z * 4 + at_x,
            )
            mine_ref[jnp.where(first, spot[0], spot[1])] = jnp.where(first, pair[0], pair[1])
            other_ref[jnp.where(first, spot[1], spot[0])] = jnp.where(
                first, pair[1], pair[0]
            ).astype(bf16)


def pair_kernel(mine_ref, came_ref, *outs):
    step = pl.program_id(0)
    total = (mine_ref[...] + came_ref[...].astype(f32)).astype(bf16)
    for r in range(3):

        @pl.when(step // 4 == r)
        def _(r=r):
            outs[r][...] = total


def plane_kernel(place_ref, mine_ref, came_ref, *refs):
    got, own_ref, outs = refs[:3], refs[3], refs[4:]
    for d in range(4):
        for i in range(4):
            at = 4 * ((place_ref[4] + d) & 3) + i
            total = mine_ref[at] + came_ref[at].astype(f32)
            for r in range(3):
                total = total + got[r][at].astype(f32)
            if d == 0:
                own_ref[i] = total
            else:
                outs[d - 1][i] = total.astype(bf16)


def line_kernel(place_ref, own_in_ref, *refs):
    got, own_ref, outs = refs[:3], refs[3], refs[4:]
    for d in range(4):
        at = (place_ref[5] + d) & 3
        total = own_in_ref[at]
        for r in range(3):
            total = total + got[r][at].astype(f32)
        if d == 0:
            own_ref[...] = total
        else:
            outs[d - 1][...] = total.astype(bf16)


def point_kernel(scale, own_ref, *refs):
    got, one_ref, two_ref = refs[:3], refs[3], refs[4]
    share = two_ref.shape[0]
    total = own_ref[...]
    for r in range(3):
        total = total + got[r][...].astype(f32)
    total = total * scale
    one_ref[...] = total[:share]
    two_ref[...] = total[share:]


def neighbours(stage, far):
    pairs = []
    for rank in range(128):
        core, xh, y, z, low = rank & 1, (rank >> 1) & 1, (rank >> 2) & 3, (rank >> 4) & 3, rank >> 6
        at = [2 * xh + low, y, z]
        axis = (stage + core) % 3
        at[axis] = (at[axis] + far) & 3
        x, y, z = at
        pairs.append((rank, ((x & 1) << 6) | (z << 4) | (y << 2) | ((x >> 1) << 1) | core))
    return pairs


def send_all(pieces, stage):
    return [lax.ppermute(pieces[r], EVERY, neighbours(stage, r + 1)) for r in range(3)]


def after(value, others):
    return lax.optimization_barrier((value, others))[0]


def weight_place():
    core = lax.axis_index("c")
    x = 2 * lax.axis_index("xh") + lax.axis_index("dp")
    y, z = lax.axis_index("y"), lax.axis_index("z")
    first = core == 0
    return jnp.stack((x, y, z, core, jnp.where(first, y, z), jnp.where(first, z, x))).astype(
        jnp.int32
    )


def weight_start(place, grad_hidden, active, flat, cot):
    tokens, hidden = grad_hidden.shape
    width = flat.shape[1]
    share = hidden // 128
    full = (64, 2 * share, width)
    ahead = pl.BlockSpec((tokens, hidden // 8), lambda g: (0, g))
    mine, other = call(
        weight_kernel,
        [(full, f32), (full, bf16)],
        place,
        grad_hidden,
        active,
        flat,
        cot,
        grant=28,
        grid=(8,),
        in_specs=[SMEM, ahead, ahead, whole(flat.shape), whole(cot.shape)],
        out_specs=[whole(full)] * 2,
        cost_estimate=pl.CostEstimate(
            flops=4 * tokens * hidden * width, bytes_accessed=14 << 20, transcendentals=0
        ),
    )
    came = lax.ppermute(other, "c", [(0, 1), (1, 0)])
    quarter = (4,) + full[1:]
    far = pl.BlockSpec(quarter, lambda g: (g + 4, 0, 0))
    sent = call(
        pair_kernel,
        [((16,) + full[1:], bf16)] * 3,
        mine,
        came,
        grid=(12,),
        in_specs=[far] * 2,
        free=(1,),
        out_specs=[
            pl.BlockSpec(quarter, lambda g, r=r: (jnp.clip(g - 4 * r, 0, 3), 0, 0))
            for r in range(3)
        ],
    )
    return mine, came, sent


def weight_second(place, mine, came, got):
    line = mine.shape[1:]
    cube, row = (16,) + line, (4,) + line
    head = pl.BlockSpec(cube, lambda g: (0, 0, 0))
    return call(
        plane_kernel,
        [(row, f32)] + [(row, bf16)] * 3,
        place,
        mine,
        came,
        *got,
        grant=20,
        grid=(1,),
        in_specs=[SMEM, head, head] + [whole(cube)] * 3,
        out_specs=[whole(row)] * 4,
        free=(2, 3, 4, 5),
    )


def weight_third(place, own, got):
    row = own.shape
    line = row[1:]
    return call(
        line_kernel,
        [(line, f32)] + [(line, bf16)] * 3,
        place,
        own,
        *got,
        grid=(1,),
        in_specs=[SMEM, whole(row)] + [whole(row)] * 3,
        out_specs=[whole(line)] * 4,
        free=(2, 3, 4),
    )


def block_diagonal(weights):
    blocks, inner = weights.shape[1:3]
    tall = weights.reshape(2, blocks * inner, inner)
    wide = jnp.concatenate((tall,) * blocks, axis=2)
    row = lax.broadcasted_iota(jnp.int32, wide.shape, 1) // inner
    lane = lax.broadcasted_iota(jnp.int32, wide.shape, 2) // inner
    return jnp.where(row == lane, wide, 0.0)


def local(
    stash,
    piece_map,
    gain_one,
    spec_one,
    bias_one,
    spec_two,
    bias_two,
    gain_two,
    fc_one,
    bias_fc,
    fc_two,
    cotangent,
):
    samples, _, lon_cells, width = cotangent.shape
    lat_total = lax.axis_size(SPACE)
    ranks = lax.axis_size(EVERY)
    tokens = samples * lon_cells
    hidden = fc_one.shape[1]
    half = width // 2
    rows = 4 * ranks
    piece = (ranks, 4, half)
    plain_table, doubled_table = zonal_tables(samples, lon_cells)
    meridian = meridian_table(samples, lat_total)
    down, back_down = high_low(plain_table), high_low(doubled_table)
    up, back_up = high_low(plain_table.T), high_low(doubled_table.T)
    forward, inverse = high_low(meridian), high_low(meridian.T)

    arrived = exchange(stash[0], SPACE)
    ordering = jnp.argsort(piece_map[:, 0])
    placed = jnp.take(arrived, ordering, axis=0)
    base = jnp.transpose(placed, (1, 0, 2)).reshape(tokens, width).astype(f32)
    upstream = cotangent.reshape(tokens, width)
    gains = jnp.stack((gain_one, gain_two))

    which = lax.axis_index("dp")
    blocks, inner = spec_one.shape[1:3]
    mine = blocks // 2
    both = jnp.concatenate(
        [
            block_diagonal(lax.dynamic_slice_in_dim(w, which * mine, mine, 1))
            for w in (spec_one, spec_two)
        ]
    )
    weights = jnp.stack(split(both))
    vectors = lax.dynamic_slice_in_dim(
        jnp.concatenate((gain_one[None], bias_one, bias_two)), which * half, half, 1
    )

    sent, xhat, rstd = call(
        first_kernel,
        [(piece, bf16), ((tokens, width), f32), ((tokens, 128), f32)],
        base,
        down,
    )
    got = exchange(sent, EVERY)
    sent, plain, pre = call(
        spectral_kernel,
        [(piece, bf16), ((2, rows // 2, half), f32), ((2, rows // 2, half), f32)],
        got,
        forward,
        inverse,
        weights,
        vectors,
        free=(0,),
    )
    got = exchange(sent, EVERY)
    normed_flat, xhat2, rstd2 = call(
        field_kernel,
        [((tokens, width), bf16), ((tokens, width), f32), ((tokens, 128), f32)],
        got,
        back_up,
        base,
        xhat,
        gains,
        free=(0,),
    )
    hidden_pre = jnp.dot(normed_flat, fc_one, preferred_element_type=f32) + bias_fc
    active_flat = smooth_gate(hidden_pre).astype(bf16)
    grad_active = jnp.einsum("td,fd->tf", upstream, fc_two, preferred_element_type=f32)
    grad_hidden = grad_active * gate_slope(hidden_pre)
    grad_hidden_flat = grad_hidden.astype(bf16)
    grad_normed_two = jnp.einsum("tf,df->td", grad_hidden_flat, fc_one, preferred_element_type=f32)
    sent, grad_mixed, sums = call(
        back_kernel,
        [(piece, bf16), ((tokens, width), f32), ((3, width), f32)],
        grad_normed_two,
        upstream,
        xhat2,
        rstd2,
        xhat,
        gains,
        back_down,
    )
    got = exchange(sent, EVERY)

    grad_scale = 1.0 / math.sqrt(samples * lax.axis_size("dp") * lat_total * lon_cells)
    place = weight_place()
    kept, came, sent = weight_start(
        place, grad_hidden_flat, active_flat, normed_flat, upstream
    )
    first_got = send_all(sent, 0)
    got = after(got, sent)

    sent, grads, mix_sums = call(
        spectral_back_kernel,
        [(piece, bf16), ((4, inner, half), f32), ((5, half), f32)],
        got,
        forward,
        inverse,
        weights,
        vectors,
        plain,
        pre,
        free=(0,),
    )
    bias_sum = jnp.sum(grad_hidden, axis=0)
    row_sums = jnp.concatenate((bias_sum.reshape(-1, half), sums.reshape(-1, half)))
    nothing = jnp.zeros_like(mix_sums)
    lines = jnp.concatenate(
        (
            row_sums,
            jnp.where(which == 0, mix_sums, nothing),
            jnp.where(which == 0, nothing, mix_sums),
        )
    )
    lines = jnp.pad(lines, ((0, ranks - lines.shape[0]), (0, 0)))
    packet = jnp.concatenate(
        (
            sent,
            grads.astype(bf16).reshape(ranks, 3, half),
            lines.astype(bf16).reshape(ranks, 1, half),
        ),
        axis=1,
    )
    got = exchange(packet, EVERY)
    own, *sent = weight_second(place, kept, came, first_got)
    second_got = send_all(sent, 1)
    (grad_input,) = call(
        last_kernel,
        [(cotangent.shape, f32)],
        after(got, sent),
        up,
        grad_mixed,
        xhat,
        rstd,
        gains,
        free=(0,),
    )
    sides = jnp.sum(got[:, 4:].reshape(2, ranks // 2, 4, half).astype(f32), axis=1)
    total = jnp.concatenate(
        (sides[0, :3], sides[1, :3], sides[0, 3:] + sides[1, 3:], jnp.zeros((1, half), f32))
    )
    total = (total * grad_scale).astype(bf16)
    spread = exchange(jnp.broadcast_to(total, (ranks,) + total.shape), EVERY).astype(f32)
    own, *sent = weight_third(place, own, second_got)
    third_got = send_all(sent, 2)
    spread = after(spread, sent)
    squares = [
        spread[:, 3 * h : 3 * h + 3].reshape(2, 2, inner, mine, inner) for h in range(2)
    ]
    spec_grads = jnp.concatenate(
        [jnp.transpose(s, (0, 1, 3, 2, 4)) for s in squares], axis=2
    )
    lines = spread[:, 6]
    fc_lines = hidden // half
    bias_grad = lines[:fc_lines].reshape(hidden)
    small = lines[fc_lines : fc_lines + 6].reshape(3, width)
    sides = lines[fc_lines + 6 : fc_lines + 16].reshape(2, 5, half)
    sides = jnp.concatenate((sides[0], sides[1]), axis=1)
    grad_one, grad_two = call(
        lambda *refs: point_kernel(grad_scale, *refs),
        [((hidden // ranks, width), f32)] * 2,
        own,
        *third_got,
        free=(1, 2, 3),
    )
    return (
        grad_input,
        grad_one.T,
        grad_two,
        bias_grad,
        small[0],
        small[1] + sides[0],
        small[2],
        spec_grads[0],
        sides[1:3],
        spec_grads[1],
        sides[3:5],
    )


def solution(mesh):
    fine = Mesh(mesh.devices.reshape(2, 4, 4, 2, 2), EVERY)
    placed = (
        P(SPACE, None, "dp", None),
        P(None, SPACE),
        P(),
        P(),
        P(),
        P(),
        P(),
        P(),
        P(),
        P(),
        P(),
        P("dp", SPACE, None, None),
    )

    return jax.shard_map(
        local,
        mesh=fine,
        in_specs=placed,
        out_specs=(
            P("dp", SPACE, None, None),
            P(None, EVERY),
            P(EVERY, None),
        )
        + (P(),) * 8,
        check_vma=False,
    )
```

```python
import math

import jax
import jax.numpy as jnp
import numpy as np
from jax import lax
from jax.experimental import pallas as pl
from jax.experimental.pallas import tpu as pltpu
from jax.sharding import Mesh, PartitionSpec as P

KW = 64
SPACE = ("z", "y", "xh", "c")
EVERY = ("dp",) + SPACE

epsilon = 1e-05
bf16 = jnp.bfloat16
f32 = jnp.float32
ROOT = math.sqrt(2.0 / math.pi)
CUBE = 0.044715


def exchange(values, axes):
    return lax.all_to_all(values, axes, split_axis=0, concat_axis=0, tiled=True)


def high_low(table):
    table = np.asarray(table, np.float32)
    high = table.astype(bf16)
    low = (table - high.astype(np.float32)).astype(bf16)
    return np.stack((high, low))


def zonal_tables(samples, lon):
    angle = 2.0 * np.pi * (np.outer(np.arange(KW), np.arange(lon)) % lon) / lon
    both = np.stack((np.cos(angle), -np.sin(angle)), axis=1) / math.sqrt(lon)
    eye = np.eye(samples)
    plain = np.einsum("krw,ab->krabw", both, eye)
    plain = plain.reshape(KW * 2 * samples, samples * lon)
    double = np.where(np.arange(KW) == 0, 1.0, 2.0)
    doubled = plain * np.repeat(double, 2 * samples)[:, None]
    return plain, doubled


def meridian_table(samples, lat):
    angle = 2.0 * np.pi * (np.outer(np.arange(lat), np.arange(lat)) % lat) / lat
    cos, sin = np.cos(angle) / math.sqrt(lat), np.sin(angle) / math.sqrt(lat)
    turn = np.stack((np.stack((cos, sin), -1), np.stack((-sin, cos), -1)))
    whole = np.einsum("qksr,ab->qkasrb", turn, np.eye(samples))
    return whole.reshape(2 * lat * samples, lat * 2 * samples)


def dot(a, b, ca=1, cb=0):
    return lax.dot_general(a, b, (((ca,), (cb,)), ((), ())), preferred_element_type=f32)


def split(a):
    high = a.astype(bf16)
    return high, (a - high.astype(f32)).astype(bf16)


def dot3(a, b, ca=1, cb=0):
    return dot(a[0], b[0], ca, cb) + (dot(a[1], b[0], ca, cb) + dot(a[0], b[1], ca, cb))


def dot2(table, b):
    return dot(table[0], b) + dot(table[1], b)


def bend(x):
    return jnp.tanh(ROOT * (x + CUBE * (x * x * x)))


def smooth_gate(x):
    return 0.5 * x * (1.0 + bend(x))


def gate_slope(x):
    t = bend(x)
    return 0.5 * (1.0 + t) + (0.5 * x) * (1.0 - t * t) * (ROOT * (1.0 + (3.0 * CUBE) * (x * x)))


def normalise(x):
    centred = x - jnp.mean(x, axis=-1, keepdims=True)
    rstd = lax.rsqrt(jnp.mean(centred * centred, axis=-1, keepdims=True) + epsilon)
    return centred * rstd, rstd


def norm_pull(grad, gain, xhat, rstd):
    scaled = grad * gain
    return rstd * (
        scaled
        - jnp.mean(scaled, axis=-1, keepdims=True)
        - xhat * jnp.mean(scaled * xhat, axis=-1, keepdims=True)
    )


def to_rows(block):
    return block.astype(f32).reshape(block.shape[0] * block.shape[1], block.shape[2]).astype(bf16)


def to_pieces(values):
    return values.reshape(values.shape[0] // 4, 4, values.shape[1]).astype(bf16)


def project(values, table_ref, out_ref):
    half = out_ref.shape[2]
    ranks = out_ref.shape[0] // 2
    found = dot3((table_ref[0], table_ref[1]), split(values))
    out_ref[:ranks] = to_pieces(found[:, :half])
    out_ref[ranks:] = to_pieces(found[:, half:])


def expand(rows_ref, table_ref):
    ranks = rows_ref.shape[0] // 2
    table = (table_ref[0], table_ref[1])
    return jnp.concatenate(
        [dot2(table, to_rows(rows_ref[ranks * h : ranks * (h + 1), :4])) for h in range(2)], axis=1
    )


def first_kernel(base_ref, table_ref, sent_ref, xhat_ref, rstd_ref):
    xhat, rstd = normalise(base_ref[...])
    xhat_ref[...] = xhat
    rstd_ref[...] = jnp.broadcast_to(rstd, rstd_ref.shape)
    project(xhat, table_ref, sent_ref)


def field_kernel(rows_ref, table_ref, base_ref, xhat_ref, gains_ref, flat_ref, xhat2_ref, rstd2_ref):
    mixed = base_ref[...] + xhat_ref[...] * gains_ref[0:1] + expand(rows_ref, table_ref)
    xhat2, rstd2 = normalise(mixed)
    xhat2_ref[...] = xhat2
    rstd2_ref[...] = jnp.broadcast_to(rstd2, rstd2_ref.shape)
    flat_ref[...] = (xhat2 * gains_ref[1:2]).astype(bf16)


def back_kernel(
    grad_ref, cot_ref, xhat2_ref, rstd2_ref, xhat_ref, gains_ref, table_ref, sent_ref, mixed_ref, sums_ref
):
    grad = grad_ref[...]
    xhat2 = xhat2_ref[...]
    cot = cot_ref[...].astype(f32)
    mixed = cot + norm_pull(grad, gains_ref[1:2], xhat2, rstd2_ref[:, 0:1])
    mixed_ref[...] = mixed
    sums_ref[0:1] = jnp.sum(cot, axis=0, keepdims=True)
    sums_ref[1:2] = jnp.sum(mixed * xhat_ref[...], axis=0, keepdims=True)
    sums_ref[2:3] = jnp.sum(grad * xhat2, axis=0, keepdims=True)
    project(mixed, table_ref, sent_ref)


def last_kernel(rows_ref, table_ref, mixed_ref, xhat_ref, rstd_ref, gains_ref, out_ref):
    mixed = mixed_ref[...]
    grad = mixed + expand(rows_ref, table_ref)
    result = mixed + norm_pull(grad, gains_ref[0:1], xhat_ref[...], rstd_ref[:, 0:1])
    cells = out_ref.shape[2]
    for sample in range(out_ref.shape[0]):
        out_ref[sample, 0] = result[cells * sample : cells * (sample + 1)]


def mix(real, imag, weights, index):
    wr = (weights[0, index], weights[1, index])
    wi = (weights[0, index + 1], weights[1, index + 1])
    real, imag = split(real), split(imag)
    return dot3(real, wr) - dot3(imag, wi), dot3(real, wi) + dot3(imag, wr)


def mix_pull(real, imag, weights, index):
    wr = (weights[0, index], weights[1, index])
    wi = (weights[0, index + 1], weights[1, index + 1])
    return (
        dot3(real, wr, 1, 1) + dot3(imag, wi, 1, 1),
        dot3(imag, wr, 1, 1) - dot3(real, wi, 1, 1),
    )


def compact(full, inner):
    lane = lax.broadcasted_iota(jnp.int32, (inner, full.shape[1]), 1)
    kept = None
    for j in range(full.shape[0] // inner):
        here = (lane >= inner * j) & (lane < inner * (j + 1))
        part = jnp.where(here, full[inner * j : inner * (j + 1)], 0.0)
        kept = part if kept is None else kept + part
    return kept


def spectral_kernel(rows_ref, table_ref, turned_ref, weights_ref, vectors_ref, sent_ref, plain_ref, pre_ref):
    ranks = rows_ref.shape[0] // 2
    half = 2 * ranks
    table = (table_ref[0], table_ref[1])
    for dp in range(2):
        found = dot2(table, to_rows(rows_ref[ranks * dp : ranks * (dp + 1)]))
        plain_ref[0, half * dp : half * (dp + 1)] = found[:half]
        plain_ref[1, half * dp : half * (dp + 1)] = found[half:]
    gain = vectors_ref[0:1]
    real, imag = mix(plain_ref[0] * gain, plain_ref[1] * gain, weights_ref, 0)
    real = real + vectors_ref[1:2]
    imag = imag + vectors_ref[2:3]
    pre_ref[0] = real
    pre_ref[1] = imag
    real, imag = mix(smooth_gate(real), smooth_gate(imag), weights_ref, 2)
    real = real + vectors_ref[3:4]
    imag = imag + vectors_ref[4:5]
    turned = (turned_ref[0], turned_ref[1])
    for dp in range(2):
        both = jnp.concatenate(
            (real[half * dp : half * (dp + 1)], imag[half * dp : half * (dp + 1)]), axis=0
        )
        sent_ref[ranks * dp : ranks * (dp + 1)] = to_pieces(dot3(turned, split(both)))


def spectral_back_kernel(
    rows_ref, table_ref, turned_ref, weights_ref, vectors_ref, plain_ref, pre_ref, sent_ref, grads_ref, sums_ref
):
    ranks = rows_ref.shape[0] // 2
    half = 2 * ranks
    inner = grads_ref.shape[1]
    table = (table_ref[0], table_ref[1])
    found = [
        dot2(table, to_rows(rows_ref[ranks * dp : ranks * (dp + 1)])) for dp in range(2)
    ]
    real = jnp.concatenate((found[0][:half], found[1][:half]), axis=0)
    imag = jnp.concatenate((found[0][half:], found[1][half:]), axis=0)

    def weight_grads(first, second, grad_real, grad_imag, at):
        grads_ref[at] = compact(
            dot3(first, grad_real, 0, 0) + dot3(second, grad_imag, 0, 0), inner
        )
        grads_ref[at + 1] = compact(
            dot3(first, grad_imag, 0, 0) - dot3(second, grad_real, 0, 0), inner
        )

    sums_ref[3:4] = jnp.sum(real, axis=0, keepdims=True)
    sums_ref[4:5] = jnp.sum(imag, axis=0, keepdims=True)
    pre_real, pre_imag = pre_ref[0], pre_ref[1]
    real, imag = split(real), split(imag)
    weight_grads(split(smooth_gate(pre_real)), split(smooth_gate(pre_imag)), real, imag, 2)
    real, imag = mix_pull(real, imag, weights_ref, 2)
    real = real * gate_slope(pre_real)
    imag = imag * gate_slope(pre_imag)
    sums_ref[1:2] = jnp.sum(real, axis=0, keepdims=True)
    sums_ref[2:3] = jnp.sum(imag, axis=0, keepdims=True)
    gain = vectors_ref[0:1]
    real, imag = split(real), split(imag)
    plain_real, plain_imag = plain_ref[0], plain_ref[1]
    weight_grads(split(plain_real * gain), split(plain_imag * gain), real, imag, 0)
    real, imag = mix_pull(real, imag, weights_ref, 0)
    sums_ref[0:1] = jnp.sum(real * plain_real + imag * plain_imag, axis=0, keepdims=True)
    turned = (turned_ref[0], turned_ref[1])
    for dp in range(2):
        both = jnp.concatenate(
            (real[half * dp : half * (dp + 1)], imag[half * dp : half * (dp + 1)]), axis=0
        )
        sent_ref[ranks * dp : ranks * (dp + 1)] = to_pieces(dot3(turned, split(both)))


def whole(shape):
    zeros = (0,) * len(shape)
    return pl.BlockSpec(shape, lambda *_: zeros)


def call(kernel, outs, *args, grant=16, grid=(1,), in_specs=None, out_specs=None, free=(), free_outs=(), **more):
    in_specs = in_specs or [whole(a.shape) for a in args]
    return pl.pallas_call(
        kernel,
        out_shape=[
            (jax.ShapeDtypeStruct if i in free_outs else pltpu.HBM)(shape, kind)
            for i, (shape, kind) in enumerate(outs)
        ],
        compiler_params=pltpu.CompilerParams(vmem_limit_bytes=grant << 20),
        grid=grid,
        in_specs=in_specs,
        out_specs=out_specs or [whole(shape) for shape, _ in outs],
        **more,
    )(
        *(
            a if spec is SMEM or i in free else pltpu.with_memory_space_constraint(a, pltpu.HBM)
            for i, (a, spec) in enumerate(zip(args, in_specs))
        )
    )


SMEM = pl.BlockSpec(memory_space=pltpu.SMEM)


def weight_kernel(
    place_ref,
    grad_ref,
    active_ref,
    flat_ref,
    cot_ref,
    tall_ref,
    wide_ref,
    own_ref,
    out1_ref,
    out2_ref,
    out3_ref,
    acc_ref,
):
    step = pl.program_id(0)
    low, at_z = step // 4, step % 4
    share = own_ref.shape[1]
    x, y, core = place_ref[0], place_ref[1], place_ref[3]
    first = core == 0

    @pl.when(first)
    def _():
        acc_ref[...] = dot(grad_ref[...], flat_ref[...], 0, 0)

    @pl.when(core == 1)
    def _():
        acc_ref[...] = dot(active_ref[...], cot_ref[...], 0, 0)

    acc_ref[...] += dot(tall_ref[...], wide_ref[...], 0, 0)
    for at_y in range(4):
        for at_xh in range(2):
            at_x = 2 * at_xh + low
            at = (at_y * 2 + at_xh) * share
            far = jnp.where(first, at_x - x, at_y - y) & 3
            spot = jnp.where(first, at_y * 4 + at_z, at_z * 4 + at_x)
            for r, ref in enumerate((own_ref, out1_ref, out2_ref, out3_ref)):

                @pl.when(far == r)
                def _(ref=ref, at=at, spot=spot):
                    ref[spot] = acc_ref[at : at + share].astype(ref.dtype)


def plane_kernel(place_ref, own_in_ref, *refs):
    got, own_ref, outs = refs[:3], refs[3], refs[4:]
    for d in range(4):
        for i in range(4):
            at = 4 * ((place_ref[4] + d) & 3) + i
            total = own_in_ref[at]
            for r in range(3):
                total = total + got[r][at].astype(f32)
            if d == 0:
                own_ref[i] = total
            else:
                outs[d - 1][i] = total.astype(bf16)


def line_kernel(place_ref, own_in_ref, *refs):
    got, own_ref, outs = refs[:3], refs[3], refs[4:]
    for d in range(4):
        at = (place_ref[5] + d) & 3
        total = own_in_ref[at]
        for r in range(3):
            total = total + got[r][at].astype(f32)
        if d == 0:
            own_ref[...] = total
        else:
            outs[d - 1][...] = total.astype(bf16)


def point_kernel(scale, place_ref, own_ref, *refs):
    got, kept_ref, send_ref = refs[:3], refs[3], refs[4]
    share = kept_ref.shape[0]
    total = own_ref[...]
    for r in range(3):
        total = total + got[r][...].astype(f32)
    total = total * scale
    first = place_ref[3] == 0
    kept_ref[...] = jnp.where(first, total[:share], total[share:])
    send_ref[...] = jnp.where(first, total[share:], total[:share])


def neighbours(stage, far):
    pairs = []
    for rank in range(128):
        core, xh, y, z, low = rank & 1, (rank >> 1) & 1, (rank >> 2) & 3, (rank >> 4) & 3, rank >> 6
        at = [2 * xh + low, y, z]
        axis = (stage + core) % 3
        at[axis] = (at[axis] + far) & 3
        x, y, z = at
        pairs.append((rank, ((x & 1) << 6) | (z << 4) | (y << 2) | ((x >> 1) << 1) | core))
    return pairs


def send_all(pieces, stage):
    return [lax.ppermute(pieces[r], EVERY, neighbours(stage, r + 1)) for r in range(3)]


def after(value, others):
    return lax.optimization_barrier((value, others))[0]


def weight_place():
    core = lax.axis_index("c")
    x = 2 * lax.axis_index("xh") + lax.axis_index("dp")
    y, z = lax.axis_index("y"), lax.axis_index("z")
    first = core == 0
    return jnp.stack((x, y, z, core, jnp.where(first, y, z), jnp.where(first, z, x))).astype(
        jnp.int32
    )


def swap(values):
    return lax.ppermute(values, "c", [(0, 1), (1, 0)])


def weight_start(place, grad_hidden, active, flat, cot):
    tokens, hidden = grad_hidden.shape
    width = flat.shape[1]
    first = place[3] == 0
    tall = swap(jnp.where(first, active, grad_hidden))
    wide = swap(jnp.where(first, cot, flat))
    cube = (16, hidden // 64, width)
    ahead = pl.BlockSpec((tokens, hidden // 8), lambda g: (0, g))
    across = whole(flat.shape)
    return call(
        weight_kernel,
        [(cube, f32)] + [(cube, bf16)] * 3,
        place,
        grad_hidden,
        active,
        flat,
        cot,
        tall,
        wide,
        grant=24,
        grid=(8,),
        in_specs=[SMEM, ahead, ahead, across, across, ahead, across],
        out_specs=[whole(cube)] * 4,
        scratch_shapes=[pltpu.VMEM((hidden // 8, width), f32)],
        free=range(1, 7),
        cost_estimate=pl.CostEstimate(
            flops=4 * tokens * hidden * width, bytes_accessed=14 << 20, transcendentals=0
        ),
    )


def weight_second(place, own, got):
    cube = own.shape
    row = (4,) + cube[1:]
    return call(
        plane_kernel,
        [(row, f32)] + [(row, bf16)] * 3,
        place,
        own,
        *got,
        grid=(1,),
        in_specs=[SMEM] + [whole(cube)] * 4,
        out_specs=[whole(row)] * 4,
        free=range(5),
        free_outs=range(4),
    )


def weight_third(place, own, got):
    row = own.shape
    line = row[1:]
    return call(
        line_kernel,
        [(line, f32)] + [(line, bf16)] * 3,
        place,
        own,
        *got,
        grid=(1,),
        in_specs=[SMEM, whole(row)] + [whole(row)] * 3,
        out_specs=[whole(line)] * 4,
        free=range(5),
        free_outs=range(4),
    )


def block_diagonal(weights):
    blocks, inner = weights.shape[1:3]
    tall = weights.reshape(2, blocks * inner, inner)
    wide = jnp.concatenate((tall,) * blocks, axis=2)
    row = lax.broadcasted_iota(jnp.int32, wide.shape, 1) // inner
    lane = lax.broadcasted_iota(jnp.int32, wide.shape, 2) // inner
    return jnp.where(row == lane, wide, 0.0)


def local(
    stash,
    piece_map,
    gain_one,
    spec_one,
    bias_one,
    spec_two,
    bias_two,
    gain_two,
    fc_one,
    bias_fc,
    fc_two,
    cotangent,
):
    samples, _, lon_cells, width = cotangent.shape
    lat_total = lax.axis_size(SPACE)
    ranks = lax.axis_size(EVERY)
    tokens = samples * lon_cells
    hidden = fc_one.shape[1]
    half = width // 2
    rows = 4 * ranks
    piece = (ranks, 4, half)
    plain_table, doubled_table = zonal_tables(samples, lon_cells)
    meridian = meridian_table(samples, lat_total)
    down, back_down = high_low(plain_table), high_low(doubled_table)
    up, back_up = high_low(plain_table.T), high_low(doubled_table.T)
    forward, inverse = high_low(meridian), high_low(meridian.T)

    arrived = exchange(stash[0], SPACE)
    ordering = jnp.argsort(piece_map[:, 0])
    placed = jnp.take(arrived, ordering, axis=0)
    base = jnp.transpose(placed, (1, 0, 2)).reshape(tokens, width).astype(f32)
    upstream = cotangent.reshape(tokens, width)
    gains = jnp.stack((gain_one, gain_two))

    which = lax.axis_index("dp")
    blocks, inner = spec_one.shape[1:3]
    mine = blocks // 2
    both = jnp.concatenate(
        [
            block_diagonal(lax.dynamic_slice_in_dim(w, which * mine, mine, 1))
            for w in (spec_one, spec_two)
        ]
    )
    weights = jnp.stack(split(both))
    vectors = lax.dynamic_slice_in_dim(
        jnp.concatenate((gain_one[None], bias_one, bias_two)), which * half, half, 1
    )

    sent, xhat, rstd = call(
        first_kernel,
        [(piece, bf16), ((tokens, width), f32), ((tokens, 128), f32)],
        base,
        down,
        free=(0,),
    )
    got = exchange(sent, EVERY)
    sent, plain, pre = call(
        spectral_kernel,
        [(piece, bf16), ((2, rows // 2, half), f32), ((2, rows // 2, half), f32)],
        got,
        forward,
        inverse,
        weights,
        vectors,
        free=(0,),
    )
    got = exchange(sent, EVERY)
    normed_flat, xhat2, rstd2 = call(
        field_kernel,
        [((tokens, width), bf16), ((tokens, width), f32), ((tokens, 128), f32)],
        got,
        back_up,
        base,
        xhat,
        gains,
        free=(0,),
        free_outs=(0,),
    )
    hidden_pre = jnp.dot(normed_flat, fc_one, preferred_element_type=f32) + bias_fc
    active_flat = smooth_gate(hidden_pre).astype(bf16)
    grad_active = jnp.einsum("td,fd->tf", upstream, fc_two, preferred_element_type=f32)
    grad_hidden = grad_active * gate_slope(hidden_pre)
    grad_hidden_flat = grad_hidden.astype(bf16)
    grad_normed_two = jnp.einsum("tf,df->td", grad_hidden_flat, fc_one, preferred_element_type=f32)
    sent, grad_mixed, sums = call(
        back_kernel,
        [(piece, bf16), ((tokens, width), f32), ((3, width), f32)],
        grad_normed_two,
        upstream,
        xhat2,
        rstd2,
        xhat,
        gains,
        back_down,
        free=(0, 1),
    )
    got = exchange(sent, EVERY)

    grad_scale = 1.0 / math.sqrt(samples * lax.axis_size("dp") * lat_total * lon_cells)
    place = weight_place()
    own, *sent = weight_start(
        place, grad_hidden_flat, active_flat, normed_flat, upstream
    )
    first_got = send_all(sent, 0)
    got = after(got, sent)

    sent, grads, mix_sums = call(
        spectral_back_kernel,
        [(piece, bf16), ((4, inner, half), f32), ((5, half), f32)],
        got,
        forward,
        inverse,
        weights,
        vectors,
        plain,
        pre,
        free=(0,),
    )
    bias_sum = jnp.sum(grad_hidden, axis=0)
    row_sums = jnp.concatenate((bias_sum.reshape(-1, half), sums.reshape(-1, half)))
    nothing = jnp.zeros_like(mix_sums)
    lines = jnp.concatenate(
        (
            row_sums,
            jnp.where(which == 0, mix_sums, nothing),
            jnp.where(which == 0, nothing, mix_sums),
        )
    )
    lines = jnp.pad(lines, ((0, ranks - lines.shape[0]), (0, 0)))
    packet = jnp.concatenate(
        (
            sent,
            grads.astype(bf16).reshape(ranks, 3, half),
            lines.astype(bf16).reshape(ranks, 1, half),
        ),
        axis=1,
    )
    got = exchange(packet, EVERY)
    own, *sent = weight_second(place, own, first_got)
    second_got = send_all(sent, 1)
    (grad_input,) = call(
        last_kernel,
        [(cotangent.shape, f32)],
        after(got, sent),
        up,
        grad_mixed,
        xhat,
        rstd,
        gains,
        free=(0,),
    )
    sides = jnp.sum(got[:, 4:].reshape(2, ranks // 2, 4, half).astype(f32), axis=1)
    total = jnp.concatenate(
        (sides[0, :3], sides[1, :3], sides[0, 3:] + sides[1, 3:], jnp.zeros((1, half), f32))
    )
    total = (total * grad_scale).astype(bf16)
    spread = exchange(jnp.broadcast_to(total, (ranks,) + total.shape), EVERY).astype(f32)
    own, *sent = weight_third(place, after(own, grad_input), second_got)
    third_got = send_all(sent, 2)
    spread = after(spread, sent)
    squares = [
        spread[:, 3 * h : 3 * h + 3].reshape(2, 2, inner, mine, inner) for h in range(2)
    ]
    spec_grads = jnp.concatenate(
        [jnp.transpose(s, (0, 1, 3, 2, 4)) for s in squares], axis=2
    )
    lines = spread[:, 6]
    fc_lines = hidden // half
    bias_grad = lines[:fc_lines].reshape(hidden)
    small = lines[fc_lines : fc_lines + 6].reshape(3, width)
    sides = lines[fc_lines + 6 : fc_lines + 16].reshape(2, 5, half)
    sides = jnp.concatenate((sides[0], sides[1]), axis=1)
    kept, away = call(
        lambda *refs: point_kernel(grad_scale, *refs),
        [((hidden // ranks, width), f32)] * 2,
        place,
        own,
        *third_got,
        in_specs=[SMEM] + [whole(own.shape)] * 4,
        free=range(5),
        free_outs=range(2),
    )
    came = swap(away)
    first = place[3] == 0
    grad_one = jnp.where(first, kept, came)
    grad_two = jnp.where(first, came, kept)
    return (
        grad_input,
        grad_one.T,
        grad_two,
        bias_grad,
        small[0],
        small[1] + sides[0],
        small[2],
        spec_grads[0],
        sides[1:3],
        spec_grads[1],
        sides[3:5],
    )


def solution(mesh):
    fine = Mesh(mesh.devices.reshape(2, 4, 4, 2, 2), EVERY)
    placed = (
        P(SPACE, None, "dp", None),
        P(None, SPACE),
        P(),
        P(),
        P(),
        P(),
        P(),
        P(),
        P(),
        P(),
        P(),
        P("dp", SPACE, None, None),
    )

    return jax.shard_map(
        local,
        mesh=fine,
        in_specs=placed,
        out_specs=(
            P("dp", SPACE, None, None),
            P(None, EVERY),
            P(EVERY, None),
        )
        + (P(),) * 8,
        check_vma=False,
    )
```

```python
import math

import jax
import jax.numpy as jnp
import numpy as np
from jax import lax
from jax.experimental import pallas as pl
from jax.experimental.pallas import tpu as pltpu
from jax.sharding import Mesh, PartitionSpec as P

KW = 64
SPACE = ("z", "y", "xh", "c")
EVERY = ("dp",) + SPACE

epsilon = 1e-05
bf16 = jnp.bfloat16
f32 = jnp.float32
ROOT = math.sqrt(2.0 / math.pi)
CUBE = 0.044715


def exchange(values, axes):
    return lax.all_to_all(values, axes, split_axis=0, concat_axis=0, tiled=True)


def high_low(table):
    table = np.asarray(table, np.float32)
    high = table.astype(bf16)
    low = (table - high.astype(np.float32)).astype(bf16)
    return np.stack((high, low))


def zonal_tables(samples, lon):
    angle = 2.0 * np.pi * (np.outer(np.arange(KW), np.arange(lon)) % lon) / lon
    both = np.stack((np.cos(angle), -np.sin(angle)), axis=1) / math.sqrt(lon)
    eye = np.eye(samples)
    plain = np.einsum("krw,ab->krabw", both, eye)
    plain = plain.reshape(KW * 2 * samples, samples * lon)
    double = np.where(np.arange(KW) == 0, 1.0, 2.0)
    doubled = plain * np.repeat(double, 2 * samples)[:, None]
    return plain, doubled


def meridian_table(samples, lat):
    angle = 2.0 * np.pi * (np.outer(np.arange(lat), np.arange(lat)) % lat) / lat
    cos, sin = np.cos(angle) / math.sqrt(lat), np.sin(angle) / math.sqrt(lat)
    turn = np.stack((np.stack((cos, sin), -1), np.stack((-sin, cos), -1)))
    whole = np.einsum("qksr,ab->qkasrb", turn, np.eye(samples))
    return whole.reshape(2 * lat * samples, lat * 2 * samples)


def dot(a, b, ca=1, cb=0):
    return lax.dot_general(a, b, (((ca,), (cb,)), ((), ())), preferred_element_type=f32)


def split(a):
    high = a.astype(bf16)
    return high, (a - high.astype(f32)).astype(bf16)


def dot3(a, b, ca=1, cb=0):
    return dot(a[0], b[0], ca, cb) + (dot(a[1], b[0], ca, cb) + dot(a[0], b[1], ca, cb))


def dot2(table, b):
    return dot(table[0], b) + dot(table[1], b)


def bend(x):
    return jnp.tanh(ROOT * (x + CUBE * (x * x * x)))


def smooth_gate(x):
    return 0.5 * x * (1.0 + bend(x))


def gate_slope(x):
    t = bend(x)
    return 0.5 * (1.0 + t) + (0.5 * x) * (1.0 - t * t) * (ROOT * (1.0 + (3.0 * CUBE) * (x * x)))


def normalise(x):
    centred = x - jnp.mean(x, axis=-1, keepdims=True)
    rstd = lax.rsqrt(jnp.mean(centred * centred, axis=-1, keepdims=True) + epsilon)
    return centred * rstd, rstd


def norm_pull(grad, gain, xhat, rstd):
    scaled = grad * gain
    return rstd * (
        scaled
        - jnp.mean(scaled, axis=-1, keepdims=True)
        - xhat * jnp.mean(scaled * xhat, axis=-1, keepdims=True)
    )


def to_rows(block):
    return block.astype(f32).reshape(block.shape[0] * block.shape[1], block.shape[2]).astype(bf16)


def to_pieces(values):
    return values.reshape(values.shape[0] // 4, 4, values.shape[1]).astype(bf16)


def project(values, table_ref, out_ref):
    half = out_ref.shape[2]
    ranks = out_ref.shape[0] // 2
    found = dot3((table_ref[0], table_ref[1]), split(values))
    out_ref[:ranks] = to_pieces(found[:, :half])
    out_ref[ranks:] = to_pieces(found[:, half:])


def expand(rows_ref, table_ref):
    ranks = rows_ref.shape[0] // 2
    table = (table_ref[0], table_ref[1])
    return jnp.concatenate(
        [dot2(table, to_rows(rows_ref[ranks * h : ranks * (h + 1), :4])) for h in range(2)], axis=1
    )


def first_kernel(base_ref, table_ref, sent_ref, xhat_ref, rstd_ref):
    xhat, rstd = normalise(base_ref[...])
    xhat_ref[...] = xhat
    rstd_ref[...] = jnp.broadcast_to(rstd, rstd_ref.shape)
    project(xhat, table_ref, sent_ref)


def field_kernel(rows_ref, table_ref, base_ref, xhat_ref, gains_ref, flat_ref, xhat2_ref, rstd2_ref):
    mixed = base_ref[...] + xhat_ref[...] * gains_ref[0:1] + expand(rows_ref, table_ref)
    xhat2, rstd2 = normalise(mixed)
    xhat2_ref[...] = xhat2
    rstd2_ref[...] = jnp.broadcast_to(rstd2, rstd2_ref.shape)
    flat_ref[...] = (xhat2 * gains_ref[1:2]).astype(bf16)


def back_kernel(
    grad_ref, cot_ref, xhat2_ref, rstd2_ref, xhat_ref, gains_ref, table_ref, sent_ref, mixed_ref, sums_ref
):
    grad = grad_ref[...]
    xhat2 = xhat2_ref[...]
    cot = cot_ref[...].astype(f32)
    mixed = cot + norm_pull(grad, gains_ref[1:2], xhat2, rstd2_ref[:, 0:1])
    mixed_ref[...] = mixed
    sums_ref[0:1] = jnp.sum(cot, axis=0, keepdims=True)
    sums_ref[1:2] = jnp.sum(mixed * xhat_ref[...], axis=0, keepdims=True)
    sums_ref[2:3] = jnp.sum(grad * xhat2, axis=0, keepdims=True)
    project(mixed, table_ref, sent_ref)


def last_kernel(rows_ref, table_ref, mixed_ref, xhat_ref, rstd_ref, gains_ref, out_ref):
    mixed = mixed_ref[...]
    grad = mixed + expand(rows_ref, table_ref)
    result = mixed + norm_pull(grad, gains_ref[0:1], xhat_ref[...], rstd_ref[:, 0:1])
    out_ref[:, 0] = result


def hidden_kernel(
    place_ref, flat_ref, cot_ref, one_ref, bias_ref, two_ref, grad_ref, active_ref, tall_ref, sum_ref
):
    pre = dot(flat_ref[...], one_ref[...]) + bias_ref[...]
    up = dot(cot_ref[...], two_ref[...], 1, 1)
    t = bend(pre)
    half = 0.5 * (1.0 + t)
    active = pre * half
    grad = up * (half + (0.5 * pre) * (1.0 - t * t) * (ROOT + (3.0 * CUBE * ROOT) * (pre * pre)))
    grad_ref[...] = grad.astype(bf16)
    active_ref[...] = active.astype(bf16)
    tall_ref[...] = jnp.where(place_ref[3] == 0, active, grad).astype(bf16)
    sum_ref[0] = jnp.sum(grad, axis=0, keepdims=True)


def mix(real, imag, weights, index):
    wr = (weights[0, index], weights[1, index])
    wi = (weights[0, index + 1], weights[1, index + 1])
    real, imag = split(real), split(imag)
    return dot3(real, wr) - dot3(imag, wi), dot3(real, wi) + dot3(imag, wr)


def mix_pull(real, imag, weights, index):
    wr = (weights[0, index], weights[1, index])
    wi = (weights[0, index + 1], weights[1, index + 1])
    return (
        dot3(real, wr, 1, 1) + dot3(imag, wi, 1, 1),
        dot3(imag, wr, 1, 1) - dot3(real, wi, 1, 1),
    )


def compact(full, inner):
    lane = lax.broadcasted_iota(jnp.int32, (inner, full.shape[1]), 1)
    kept = None
    for j in range(full.shape[0] // inner):
        here = (lane >= inner * j) & (lane < inner * (j + 1))
        part = jnp.where(here, full[inner * j : inner * (j + 1)], 0.0)
        kept = part if kept is None else kept + part
    return kept


def spectral_kernel(rows_ref, table_ref, turned_ref, weights_ref, vectors_ref, sent_ref, plain_ref, pre_ref):
    ranks = rows_ref.shape[0] // 2
    half = 2 * ranks
    table = (table_ref[0], table_ref[1])
    for dp in range(2):
        found = dot2(table, to_rows(rows_ref[ranks * dp : ranks * (dp + 1)]))
        plain_ref[0, half * dp : half * (dp + 1)] = found[:half]
        plain_ref[1, half * dp : half * (dp + 1)] = found[half:]
    gain = vectors_ref[0:1]
    real, imag = mix(plain_ref[0] * gain, plain_ref[1] * gain, weights_ref, 0)
    real = real + vectors_ref[1:2]
    imag = imag + vectors_ref[2:3]
    pre_ref[0] = real
    pre_ref[1] = imag
    real, imag = mix(smooth_gate(real), smooth_gate(imag), weights_ref, 2)
    real = real + vectors_ref[3:4]
    imag = imag + vectors_ref[4:5]
    turned = (turned_ref[0], turned_ref[1])
    for dp in range(2):
        both = jnp.concatenate(
            (real[half * dp : half * (dp + 1)], imag[half * dp : half * (dp + 1)]), axis=0
        )
        sent_ref[ranks * dp : ranks * (dp + 1)] = to_pieces(dot3(turned, split(both)))


def spectral_back_kernel(
    rows_ref,
    table_ref,
    turned_ref,
    weights_ref,
    vectors_ref,
    plain_ref,
    pre_ref,
    lines_ref,
    place_ref,
    packet_ref,
    grads_ref,
    sums_ref,
    work_ref,
):
    ranks = rows_ref.shape[0] // 2
    half = 2 * ranks
    inner = grads_ref.shape[0] // 4
    table = (table_ref[0], table_ref[1])
    found = [
        dot2(table, to_rows(rows_ref[ranks * dp : ranks * (dp + 1)])) for dp in range(2)
    ]
    real = jnp.concatenate((found[0][:half], found[1][:half]), axis=0)
    imag = jnp.concatenate((found[0][half:], found[1][half:]), axis=0)

    def weight_grads(first, second, grad_real, grad_imag, at):
        grads_ref[inner * at : inner * (at + 1)] = compact(
            dot3(first, grad_real, 0, 0) + dot3(second, grad_imag, 0, 0), inner
        )
        grads_ref[inner * (at + 1) : inner * (at + 2)] = compact(
            dot3(first, grad_imag, 0, 0) - dot3(second, grad_real, 0, 0), inner
        )

    sums_ref[3:4] = jnp.sum(real, axis=0, keepdims=True)
    sums_ref[4:5] = jnp.sum(imag, axis=0, keepdims=True)
    pre_real, pre_imag = pre_ref[0], pre_ref[1]
    real, imag = split(real), split(imag)
    weight_grads(split(smooth_gate(pre_real)), split(smooth_gate(pre_imag)), real, imag, 2)
    real, imag = mix_pull(real, imag, weights_ref, 2)
    real = real * gate_slope(pre_real)
    imag = imag * gate_slope(pre_imag)
    sums_ref[1:2] = jnp.sum(real, axis=0, keepdims=True)
    sums_ref[2:3] = jnp.sum(imag, axis=0, keepdims=True)
    gain = vectors_ref[0:1]
    real, imag = split(real), split(imag)
    plain_real, plain_imag = plain_ref[0], plain_ref[1]
    weight_grads(split(plain_real * gain), split(plain_imag * gain), real, imag, 0)
    real, imag = mix_pull(real, imag, weights_ref, 0)
    sums_ref[0:1] = jnp.sum(real * plain_real + imag * plain_imag, axis=0, keepdims=True)
    turned = (turned_ref[0], turned_ref[1])
    for dp in range(2):
        both = jnp.concatenate(
            (real[half * dp : half * (dp + 1)], imag[half * dp : half * (dp + 1)]), axis=0
        )
        found = dot3(turned, split(both))
        work_ref[ranks * dp : ranks * (dp + 1), 0:4] = found.reshape(ranks, 4, found.shape[1])
    total = 2 * ranks
    for r in range(3):
        work_ref[:, 4 + r] = grads_ref[total * r : total * (r + 1)]
    known = lines_ref.shape[0]
    work_ref[:, 7] = jnp.zeros((total, found.shape[1]), f32)
    work_ref[:known, 7] = lines_ref[...]
    for h in range(2):

        @pl.when(place_ref[6] == h)
        def _(h=h):
            work_ref[known + 5 * h : known + 5 * h + 5, 7] = sums_ref[...]

    packet_ref[...] = work_ref[...].astype(bf16)


def unpack_kernel(spread_ref, one_ref, two_ref, fc_ref, out_ref, gain1_ref, gain2_ref, b1_ref, b2_ref, work_ref):
    total = spread_ref.shape[0]
    inner = one_ref.shape[2]
    wide = spread_ref[...].astype(f32)
    for h in range(2):
        for r in range(3):
            work_ref[h, total * r : total * (r + 1)] = wide[:, 3 * h + r]
        for m in range(4):
            for j in range(4):
                (one_ref, two_ref)[m // 2][m % 2, 4 * h + j] = work_ref[
                    h, inner * m : inner * (m + 1), inner * j : inner * (j + 1)
                ]
    lines = wide[:24, 6]

    def joined(*rows):
        return jnp.concatenate([lines[r : r + 1] for r in rows], axis=1)

    fc_ref[...] = joined(*range(8))
    out_ref[...] = joined(8, 9)
    gain1_ref[...] = joined(10, 11) + joined(14, 19)
    gain2_ref[...] = joined(12, 13)
    for i in range(2):
        b1_ref[i : i + 1] = joined(15 + i, 20 + i)
        b2_ref[i : i + 1] = joined(17 + i, 22 + i)


def whole(shape):
    zeros = (0,) * len(shape)
    return pl.BlockSpec(shape, lambda *_: zeros)


def call(kernel, outs, *args, grant=16, grid=(1,), in_specs=None, out_specs=None, free=(), free_outs=(), **more):
    in_specs = in_specs or [whole(a.shape) for a in args]
    return pl.pallas_call(
        kernel,
        out_shape=[
            (jax.ShapeDtypeStruct if i in free_outs else pltpu.HBM)(shape, kind)
            for i, (shape, kind) in enumerate(outs)
        ],
        compiler_params=pltpu.CompilerParams(vmem_limit_bytes=grant << 20),
        grid=grid,
        in_specs=in_specs,
        out_specs=out_specs or [whole(shape) for shape, _ in outs],
        **more,
    )(
        *(
            a if spec is SMEM or i in free else pltpu.with_memory_space_constraint(a, pltpu.HBM)
            for i, (a, spec) in enumerate(zip(args, in_specs))
        )
    )


SMEM = pl.BlockSpec(memory_space=pltpu.SMEM)


def weight_kernel(
    place_ref,
    grad_ref,
    active_ref,
    flat_ref,
    cot_ref,
    tall_ref,
    wide_ref,
    own_ref,
    out1_ref,
    out2_ref,
    out3_ref,
    acc_ref,
):
    step = pl.program_id(0)
    low, at_z = step // 4, step % 4
    share = own_ref.shape[1]
    x, y, core = place_ref[0], place_ref[1], place_ref[3]
    first = core == 0

    @pl.when(first)
    def _():
        acc_ref[...] = dot(grad_ref[...], flat_ref[...], 0, 0)

    @pl.when(core == 1)
    def _():
        acc_ref[...] = dot(active_ref[...], cot_ref[...], 0, 0)

    acc_ref[...] += dot(tall_ref[...], wide_ref[...], 0, 0)
    for at_y in range(4):
        for at_xh in range(2):
            at_x = 2 * at_xh + low
            at = (at_y * 2 + at_xh) * share
            far = jnp.where(first, at_x - x, at_y - y) & 3
            spot = jnp.where(first, at_y * 4 + at_z, at_z * 4 + at_x)
            for r, ref in enumerate((own_ref, out1_ref, out2_ref, out3_ref)):

                @pl.when(far == r)
                def _(ref=ref, at=at, spot=spot):
                    ref[spot] = acc_ref[at : at + share].astype(ref.dtype)


def plane_kernel(place_ref, own_in_ref, *refs):
    got, own_ref, outs = refs[:3], refs[3], refs[4:]
    for d in range(4):
        for i in range(4):
            at = 4 * ((place_ref[4] + d) & 3) + i
            total = own_in_ref[at]
            for r in range(3):
                total = total + got[r][at].astype(f32)
            if d == 0:
                own_ref[i] = total
            else:
                outs[d - 1][i] = total.astype(bf16)


def line_kernel(place_ref, own_in_ref, *refs):
    got, own_ref, outs = refs[:3], refs[3], refs[4:]
    for d in range(4):
        at = (place_ref[5] + d) & 3
        total = own_in_ref[at]
        for r in range(3):
            total = total + got[r][at].astype(f32)
        if d == 0:
            own_ref[...] = total
        else:
            outs[d - 1][...] = total.astype(bf16)


def point_kernel(scale, place_ref, own_ref, *refs):
    got, kept_ref, send_ref = refs[:3], refs[3], refs[4]
    share = kept_ref.shape[0]
    total = own_ref[...]
    for r in range(3):
        total = total + got[r][...].astype(f32)
    total = total * scale
    first = place_ref[3] == 0
    kept_ref[...] = jnp.where(first, total[:share], total[share:])
    send_ref[...] = jnp.where(first, total[share:], total[:share])


def neighbours(stage, far):
    pairs = []
    for rank in range(128):
        core, xh, y, z, low = rank & 1, (rank >> 1) & 1, (rank >> 2) & 3, (rank >> 4) & 3, rank >> 6
        at = [2 * xh + low, y, z]
        axis = (stage + core) % 3
        at[axis] = (at[axis] + far) & 3
        x, y, z = at
        pairs.append((rank, ((x & 1) << 6) | (z << 4) | (y << 2) | ((x >> 1) << 1) | core))
    return pairs


def send_all(pieces, stage):
    return [lax.ppermute(pieces[r], EVERY, neighbours(stage, r + 1)) for r in range(3)]


def after(value, others):
    return lax.optimization_barrier((value, others))[0]


def weight_place():
    core = lax.axis_index("c")
    x = 2 * lax.axis_index("xh") + lax.axis_index("dp")
    y, z = lax.axis_index("y"), lax.axis_index("z")
    first = core == 0
    return jnp.stack(
        (x, y, z, core, jnp.where(first, y, z), jnp.where(first, z, x), lax.axis_index("dp"))
    ).astype(
        jnp.int32
    )


def swap(values):
    return lax.ppermute(values, "c", [(0, 1), (1, 0)])


def weight_start(place, grad_hidden, active, flat, cot, tall):
    tokens, hidden = grad_hidden.shape
    width = flat.shape[1]
    first = place[3] == 0
    tall = swap(tall)
    wide = swap(jnp.where(first, cot, flat))
    cube = (16, hidden // 64, width)
    ahead = pl.BlockSpec((tokens, hidden // 8), lambda g: (0, g))
    across = whole(flat.shape)
    return call(
        weight_kernel,
        [(cube, f32)] + [(cube, bf16)] * 3,
        place,
        grad_hidden,
        active,
        flat,
        cot,
        tall,
        wide,
        grant=24,
        grid=(8,),
        in_specs=[SMEM, ahead, ahead, across, across, ahead, across],
        out_specs=[whole(cube)] * 4,
        scratch_shapes=[pltpu.VMEM((hidden // 8, width), f32)],
        free=range(1, 7),
        cost_estimate=pl.CostEstimate(
            flops=4 * tokens * hidden * width, bytes_accessed=14 << 20, transcendentals=0
        ),
    )


def weight_second(place, own, got):
    cube = own.shape
    row = (4,) + cube[1:]
    return call(
        plane_kernel,
        [(row, f32)] + [(row, bf16)] * 3,
        place,
        own,
        *got,
        grid=(1,),
        in_specs=[SMEM] + [whole(cube)] * 4,
        out_specs=[whole(row)] * 4,
        free=range(5),
        free_outs=range(4),
    )


def weight_third(place, own, got):
    row = own.shape
    line = row[1:]
    return call(
        line_kernel,
        [(line, f32)] + [(line, bf16)] * 3,
        place,
        own,
        *got,
        grid=(1,),
        in_specs=[SMEM, whole(row)] + [whole(row)] * 3,
        out_specs=[whole(line)] * 4,
        free=range(5),
        free_outs=range(4),
    )


def block_diagonal(weights):
    blocks, inner = weights.shape[1:3]
    tall = weights.reshape(2, blocks * inner, inner)
    wide = jnp.concatenate((tall,) * blocks, axis=2)
    row = lax.broadcasted_iota(jnp.int32, wide.shape, 1) // inner
    lane = lax.broadcasted_iota(jnp.int32, wide.shape, 2) // inner
    return jnp.where(row == lane, wide, 0.0)


def local(
    stash,
    piece_map,
    gain_one,
    spec_one,
    bias_one,
    spec_two,
    bias_two,
    gain_two,
    fc_one,
    bias_fc,
    fc_two,
    cotangent,
):
    samples, _, lon_cells, width = cotangent.shape
    lat_total = lax.axis_size(SPACE)
    ranks = lax.axis_size(EVERY)
    tokens = samples * lon_cells
    hidden = fc_one.shape[1]
    half = width // 2
    rows = 4 * ranks
    piece = (ranks, 4, half)
    plain_table, doubled_table = zonal_tables(samples, lon_cells)
    meridian = meridian_table(samples, lat_total)
    down, back_down = high_low(plain_table), high_low(doubled_table)
    up, back_up = high_low(plain_table.T), high_low(doubled_table.T)
    forward, inverse = high_low(meridian), high_low(meridian.T)

    arrived = exchange(stash[0], SPACE)
    ordering = jnp.argsort(piece_map[:, 0])
    placed = jnp.take(arrived, ordering, axis=0)
    base = jnp.transpose(placed, (1, 0, 2)).reshape(tokens, width).astype(f32)
    upstream = cotangent.reshape(tokens, width)
    gains = jnp.stack((gain_one, gain_two))

    which = lax.axis_index("dp")
    blocks, inner = spec_one.shape[1:3]
    mine = blocks // 2
    both = jnp.concatenate(
        [
            block_diagonal(lax.dynamic_slice_in_dim(w, which * mine, mine, 1))
            for w in (spec_one, spec_two)
        ]
    )
    weights = jnp.stack(split(both))
    vectors = lax.dynamic_slice_in_dim(
        jnp.concatenate((gain_one[None], bias_one, bias_two)), which * half, half, 1
    )

    sent, xhat, rstd = call(
        first_kernel,
        [(piece, bf16), ((tokens, width), f32), ((tokens, 128), f32)],
        base,
        down,
        free=(0,),
    )
    got = exchange(sent, EVERY)
    sent, plain, pre = call(
        spectral_kernel,
        [(piece, bf16), ((2, rows // 2, half), f32), ((2, rows // 2, half), f32)],
        got,
        forward,
        inverse,
        weights,
        vectors,
        free=(0,),
    )
    got = exchange(sent, EVERY)
    normed_flat, xhat2, rstd2 = call(
        field_kernel,
        [((tokens, width), bf16), ((tokens, width), f32), ((tokens, 128), f32)],
        got,
        back_up,
        base,
        xhat,
        gains,
        free=(0,),
        free_outs=(0,),
    )
    place = weight_place()
    block = (tokens, hidden // 8)
    across = pl.BlockSpec(block, lambda g: (0, g))
    grad_hidden_flat, active_flat, tall, bias_sum = call(
        hidden_kernel,
        [((tokens, hidden), bf16)] * 3 + [((8, 1, hidden // 8), f32)],
        place,
        normed_flat,
        upstream,
        fc_one,
        bias_fc.reshape(1, hidden),
        fc_two,
        grid=(8,),
        in_specs=[
            SMEM,
            whole(normed_flat.shape),
            whole(upstream.shape),
            pl.BlockSpec((width, hidden // 8), lambda g: (0, g)),
            pl.BlockSpec((1, hidden // 8), lambda g: (0, g)),
            pl.BlockSpec((hidden // 8, width), lambda g: (g, 0)),
        ],
        out_specs=[across] * 3 + [pl.BlockSpec((1, 1, hidden // 8), lambda g: (g, 0, 0))],
        free=(1, 2, 4),
        free_outs=(0, 1, 3),
        cost_estimate=pl.CostEstimate(
            flops=4 * tokens * hidden * width,
            bytes_accessed=18 << 20,
            transcendentals=tokens * hidden,
        ),
    )
    grad_normed_two = jnp.einsum("tf,df->td", grad_hidden_flat, fc_one, preferred_element_type=f32)
    sent, grad_mixed, sums = call(
        back_kernel,
        [(piece, bf16), ((tokens, width), f32), ((3, width), f32)],
        grad_normed_two,
        upstream,
        xhat2,
        rstd2,
        xhat,
        gains,
        back_down,
        free=(0, 1),
    )
    got = exchange(sent, EVERY)

    grad_scale = 1.0 / math.sqrt(samples * lax.axis_size("dp") * lat_total * lon_cells)
    own, *sent = weight_start(
        place, grad_hidden_flat, active_flat, normed_flat, upstream, tall
    )
    first_got = send_all(sent, 0)
    got = after(got, sent)

    lines = jnp.concatenate((bias_sum.reshape(-1, half), sums.reshape(-1, half)))
    matrices = (4 * inner, half)
    (packet,) = call(
        spectral_back_kernel,
        [((ranks, 8, half), bf16)],
        got,
        forward,
        inverse,
        weights,
        vectors,
        plain,
        pre,
        lines,
        place,
        in_specs=[whole(a.shape) for a in (got, forward, inverse, weights, vectors, plain, pre)]
        + [whole(lines.shape), SMEM],
        scratch_shapes=[
            pltpu.VMEM(matrices, f32),
            pltpu.VMEM((5, half), f32),
            pltpu.VMEM((ranks, 8, half), f32),
        ],
        free=(0, 7, 8),
        grant=20,
    )
    got = exchange(packet, EVERY)
    own, *sent = weight_second(place, own, first_got)
    second_got = send_all(sent, 1)
    (grad_input,) = call(
        last_kernel,
        [((tokens, 1, width), f32)],
        after(got, sent),
        up,
        grad_mixed,
        xhat,
        rstd,
        gains,
        free=(0,),
    )
    sides = jnp.sum(got[:, 4:].reshape(2, ranks // 2, 4, half).astype(f32), axis=1)
    total = jnp.concatenate(
        (sides[0, :3], sides[1, :3], sides[0, 3:] + sides[1, 3:], jnp.zeros((1, half), f32))
    )
    total = (total * grad_scale).astype(bf16)
    spread = exchange(jnp.broadcast_to(total, (ranks,) + total.shape), EVERY)
    own, *sent = weight_third(place, after(own, grad_input), second_got)
    third_got = send_all(sent, 2)
    spread = after(spread, sent)
    whole_spec = spec_one.shape
    unpacked = call(
        unpack_kernel,
        [
            (whole_spec, f32),
            (whole_spec, f32),
            ((1, hidden), f32),
            ((1, width), f32),
            ((1, width), f32),
            ((1, width), f32),
            ((2, width), f32),
            ((2, width), f32),
        ],
        spread,
        scratch_shapes=[pltpu.VMEM((2,) + matrices, f32)],
        free=(0,),
    )
    spec_one_grad, spec_two_grad, fc_grad, out_grad, gain1, gain2, bias1, bias2 = unpacked
    kept, away = call(
        lambda *refs: point_kernel(grad_scale, *refs),
        [((hidden // ranks, width), f32)] * 2,
        place,
        own,
        *third_got,
        in_specs=[SMEM] + [whole(own.shape)] * 4,
        free=range(5),
        free_outs=range(2),
    )
    came = swap(away)
    first = place[3] == 0
    grad_one = jnp.where(first, kept, came)
    grad_two = jnp.where(first, came, kept)
    return (
        grad_input.reshape(samples, lon_cells, 1, width).transpose(0, 2, 1, 3),
        grad_one.T,
        grad_two,
        fc_grad.reshape(hidden),
        out_grad.reshape(width),
        gain1.reshape(width),
        gain2.reshape(width),
        spec_one_grad,
        bias1,
        spec_two_grad,
        bias2,
    )


def solution(mesh):
    fine = Mesh(mesh.devices.reshape(2, 4, 4, 2, 2), EVERY)
    placed = (
        P(SPACE, None, "dp", None),
        P(None, SPACE),
        P(),
        P(),
        P(),
        P(),
        P(),
        P(),
        P(),
        P(),
        P(),
        P("dp", SPACE, None, None),
    )

    return jax.shard_map(
        local,
        mesh=fine,
        in_specs=placed,
        out_specs=(
            P("dp", SPACE, None, None),
            P(None, EVERY),
            P(EVERY, None),
        )
        + (P(),) * 8,
        check_vma=False,
    )
```

```python
import math

import jax
import jax.numpy as jnp
import numpy as np
from jax import lax
from jax.experimental import pallas as pl
from jax.experimental.pallas import tpu as pltpu
from jax.sharding import Mesh, PartitionSpec as P

KW = 64
SPACE = ("z", "y", "xh", "c")
EVERY = ("dp",) + SPACE

epsilon = 1e-05
bf16 = jnp.bfloat16
f32 = jnp.float32
ROOT = math.sqrt(2.0 / math.pi)
CUBE = 0.044715


def exchange(values, axes):
    return lax.all_to_all(values, axes, split_axis=0, concat_axis=0, tiled=True)


def high_low(table):
    table = np.asarray(table, np.float32)
    high = table.astype(bf16)
    low = (table - high.astype(np.float32)).astype(bf16)
    return np.stack((high, low))


def zonal_tables(samples, lon):
    angle = 2.0 * np.pi * (np.outer(np.arange(KW), np.arange(lon)) % lon) / lon
    both = np.stack((np.cos(angle), -np.sin(angle)), axis=1) / math.sqrt(lon)
    eye = np.eye(samples)
    plain = np.einsum("krw,ab->krabw", both, eye)
    plain = plain.reshape(KW * 2 * samples, samples * lon)
    double = np.where(np.arange(KW) == 0, 1.0, 2.0)
    doubled = plain * np.repeat(double, 2 * samples)[:, None]
    return plain, doubled


def meridian_table(samples, lat):
    angle = 2.0 * np.pi * (np.outer(np.arange(lat), np.arange(lat)) % lat) / lat
    cos, sin = np.cos(angle) / math.sqrt(lat), np.sin(angle) / math.sqrt(lat)
    turn = np.stack((np.stack((cos, sin), -1), np.stack((-sin, cos), -1)))
    whole = np.einsum("qksr,ab->qkasrb", turn, np.eye(samples))
    return whole.reshape(2 * lat * samples, lat * 2 * samples)


def dot(a, b, ca=1, cb=0):
    return lax.dot_general(a, b, (((ca,), (cb,)), ((), ())), preferred_element_type=f32)


def split(a):
    high = a.astype(bf16)
    return high, (a - high.astype(f32)).astype(bf16)


def dot3(a, b, ca=1, cb=0):
    return dot(a[0], b[0], ca, cb) + (dot(a[1], b[0], ca, cb) + dot(a[0], b[1], ca, cb))


def dot2(table, b):
    return dot(table[0], b) + dot(table[1], b)


def bend(x):
    return jnp.tanh(ROOT * (x + CUBE * (x * x * x)))


def smooth_gate(x):
    return 0.5 * x * (1.0 + bend(x))


def gate_slope(x):
    t = bend(x)
    return 0.5 * (1.0 + t) + (0.5 * x) * (1.0 - t * t) * (ROOT * (1.0 + (3.0 * CUBE) * (x * x)))


def normalise(x):
    centred = x - jnp.mean(x, axis=-1, keepdims=True)
    rstd = lax.rsqrt(jnp.mean(centred * centred, axis=-1, keepdims=True) + epsilon)
    return centred * rstd, rstd


def norm_pull(grad, gain, xhat, rstd):
    scaled = grad * gain
    return rstd * (
        scaled
        - jnp.mean(scaled, axis=-1, keepdims=True)
        - xhat * jnp.mean(scaled * xhat, axis=-1, keepdims=True)
    )


def to_rows(block):
    return block.astype(f32).reshape(block.shape[0] * block.shape[1], block.shape[2]).astype(bf16)


def to_pieces(values):
    return values.reshape(values.shape[0] // 4, 4, values.shape[1]).astype(bf16)


def project(values, table_ref, out_ref):
    half = out_ref.shape[2]
    ranks = out_ref.shape[0] // 2
    found = dot3((table_ref[0], table_ref[1]), split(values))
    out_ref[:ranks] = to_pieces(found[:, :half])
    out_ref[ranks:] = to_pieces(found[:, half:])


def expand(rows_ref, table_ref):
    ranks = rows_ref.shape[0] // 2
    table = (table_ref[0], table_ref[1])
    return jnp.concatenate(
        [dot2(table, to_rows(rows_ref[ranks * h : ranks * (h + 1), :4])) for h in range(2)], axis=1
    )


def first_kernel(base_ref, table_ref, sent_ref, xhat_ref, rstd_ref):
    xhat, rstd = normalise(base_ref[...])
    xhat_ref[...] = xhat
    rstd_ref[...] = jnp.broadcast_to(rstd, rstd_ref.shape)
    project(xhat, table_ref, sent_ref)


def field_kernel(rows_ref, table_ref, base_ref, xhat_ref, gains_ref, flat_ref, xhat2_ref, rstd2_ref):
    mixed = base_ref[...] + xhat_ref[...] * gains_ref[0:1] + expand(rows_ref, table_ref)
    xhat2, rstd2 = normalise(mixed)
    xhat2_ref[...] = xhat2
    rstd2_ref[...] = jnp.broadcast_to(rstd2, rstd2_ref.shape)
    flat_ref[...] = (xhat2 * gains_ref[1:2]).astype(bf16)


def back_kernel(
    grad_ref, cot_ref, xhat2_ref, rstd2_ref, xhat_ref, gains_ref, table_ref, sent_ref, mixed_ref, sums_ref
):
    grad = grad_ref[...]
    xhat2 = xhat2_ref[...]
    cot = cot_ref[...].astype(f32)
    mixed = cot + norm_pull(grad, gains_ref[1:2], xhat2, rstd2_ref[:, 0:1])
    mixed_ref[...] = mixed
    sums_ref[0:1] = jnp.sum(cot, axis=0, keepdims=True)
    sums_ref[1:2] = jnp.sum(mixed * xhat_ref[...], axis=0, keepdims=True)
    sums_ref[2:3] = jnp.sum(grad * xhat2, axis=0, keepdims=True)
    project(mixed, table_ref, sent_ref)


def last_kernel(rows_ref, table_ref, mixed_ref, xhat_ref, rstd_ref, gains_ref, out_ref):
    mixed = mixed_ref[...]
    grad = mixed + expand(rows_ref, table_ref)
    result = mixed + norm_pull(grad, gains_ref[0:1], xhat_ref[...], rstd_ref[:, 0:1])
    out_ref[:, 0] = result


def hidden_kernel(
    place_ref, flat_ref, cot_ref, one_ref, bias_ref, two_ref, grad_ref, active_ref, tall_ref, sum_ref
):
    pre = dot(flat_ref[...], one_ref[...]) + bias_ref[...]
    up = dot(cot_ref[...], two_ref[...], 1, 1)
    t = bend(pre)
    half = 0.5 * (1.0 + t)
    active = pre * half
    grad = up * (half + (0.5 * pre) * (1.0 - t * t) * (ROOT + (3.0 * CUBE * ROOT) * (pre * pre)))
    grad_ref[...] = grad.astype(bf16)
    active_ref[...] = active.astype(bf16)
    tall_ref[...] = jnp.where(place_ref[3] == 0, active, grad).astype(bf16)
    sum_ref[0] = jnp.sum(grad, axis=0, keepdims=True)


def mix(real, imag, weights, index):
    wr = (weights[0, index], weights[1, index])
    wi = (weights[0, index + 1], weights[1, index + 1])
    real, imag = split(real), split(imag)
    return dot3(real, wr) - dot3(imag, wi), dot3(real, wi) + dot3(imag, wr)


def mix_pull(real, imag, weights, index):
    wr = (weights[0, index], weights[1, index])
    wi = (weights[0, index + 1], weights[1, index + 1])
    return (
        dot3(real, wr, 1, 1) + dot3(imag, wi, 1, 1),
        dot3(imag, wr, 1, 1) - dot3(real, wi, 1, 1),
    )


def compact(full, inner):
    lane = lax.broadcasted_iota(jnp.int32, (inner, full.shape[1]), 1)
    kept = None
    for j in range(full.shape[0] // inner):
        here = (lane >= inner * j) & (lane < inner * (j + 1))
        part = jnp.where(here, full[inner * j : inner * (j + 1)], 0.0)
        kept = part if kept is None else kept + part
    return kept


def spectral_kernel(rows_ref, table_ref, turned_ref, weights_ref, vectors_ref, sent_ref, plain_ref, pre_ref):
    ranks = rows_ref.shape[0] // 2
    half = 2 * ranks
    table = (table_ref[0], table_ref[1])
    for dp in range(2):
        found = dot2(table, to_rows(rows_ref[ranks * dp : ranks * (dp + 1)]))
        plain_ref[0, half * dp : half * (dp + 1)] = found[:half]
        plain_ref[1, half * dp : half * (dp + 1)] = found[half:]
    gain = vectors_ref[0:1]
    real, imag = mix(plain_ref[0] * gain, plain_ref[1] * gain, weights_ref, 0)
    real = real + vectors_ref[1:2]
    imag = imag + vectors_ref[2:3]
    pre_ref[0] = real
    pre_ref[1] = imag
    real, imag = mix(smooth_gate(real), smooth_gate(imag), weights_ref, 2)
    real = real + vectors_ref[3:4]
    imag = imag + vectors_ref[4:5]
    turned = (turned_ref[0], turned_ref[1])
    for dp in range(2):
        both = jnp.concatenate(
            (real[half * dp : half * (dp + 1)], imag[half * dp : half * (dp + 1)]), axis=0
        )
        sent_ref[ranks * dp : ranks * (dp + 1)] = to_pieces(dot3(turned, split(both)))


def spectral_back_kernel(
    rows_ref,
    table_ref,
    turned_ref,
    weights_ref,
    vectors_ref,
    plain_ref,
    pre_ref,
    lines_ref,
    place_ref,
    packet_ref,
    grads_ref,
    sums_ref,
    work_ref,
):
    ranks = rows_ref.shape[0] // 2
    half = 2 * ranks
    inner = grads_ref.shape[0] // 4
    table = (table_ref[0], table_ref[1])
    found = [
        dot2(table, to_rows(rows_ref[ranks * dp : ranks * (dp + 1)])) for dp in range(2)
    ]
    real = jnp.concatenate((found[0][:half], found[1][:half]), axis=0)
    imag = jnp.concatenate((found[0][half:], found[1][half:]), axis=0)

    def weight_grads(first, second, grad_real, grad_imag, at):
        grads_ref[inner * at : inner * (at + 1)] = compact(
            dot3(first, grad_real, 0, 0) + dot3(second, grad_imag, 0, 0), inner
        )
        grads_ref[inner * (at + 1) : inner * (at + 2)] = compact(
            dot3(first, grad_imag, 0, 0) - dot3(second, grad_real, 0, 0), inner
        )

    sums_ref[3:4] = jnp.sum(real, axis=0, keepdims=True)
    sums_ref[4:5] = jnp.sum(imag, axis=0, keepdims=True)
    pre_real, pre_imag = pre_ref[0], pre_ref[1]
    real, imag = split(real), split(imag)
    weight_grads(split(smooth_gate(pre_real)), split(smooth_gate(pre_imag)), real, imag, 2)
    real, imag = mix_pull(real, imag, weights_ref, 2)
    real = real * gate_slope(pre_real)
    imag = imag * gate_slope(pre_imag)
    sums_ref[1:2] = jnp.sum(real, axis=0, keepdims=True)
    sums_ref[2:3] = jnp.sum(imag, axis=0, keepdims=True)
    gain = vectors_ref[0:1]
    real, imag = split(real), split(imag)
    plain_real, plain_imag = plain_ref[0], plain_ref[1]
    weight_grads(split(plain_real * gain), split(plain_imag * gain), real, imag, 0)
    real, imag = mix_pull(real, imag, weights_ref, 0)
    sums_ref[0:1] = jnp.sum(real * plain_real + imag * plain_imag, axis=0, keepdims=True)
    turned = (turned_ref[0], turned_ref[1])
    for dp in range(2):
        both = jnp.concatenate(
            (real[half * dp : half * (dp + 1)], imag[half * dp : half * (dp + 1)]), axis=0
        )
        found = dot3(turned, split(both))
        work_ref[ranks * dp : ranks * (dp + 1), 0:4] = found.reshape(ranks, 4, found.shape[1])
    total = 2 * ranks
    for r in range(3):
        work_ref[:, 4 + r] = grads_ref[total * r : total * (r + 1)]
    known = lines_ref.shape[0]
    work_ref[:, 7] = jnp.zeros((total, found.shape[1]), f32)
    work_ref[:known, 7] = lines_ref[...]
    for h in range(2):

        @pl.when(place_ref[6] == h)
        def _(h=h):
            work_ref[known + 5 * h : known + 5 * h + 5, 7] = sums_ref[...]

    packet_ref[...] = work_ref[...].astype(bf16)


def unpack_kernel(spread_ref, one_ref, two_ref, fc_ref, out_ref, gain1_ref, gain2_ref, b1_ref, b2_ref, work_ref):
    total = spread_ref.shape[0]
    inner = one_ref.shape[2]
    wide = spread_ref[...].astype(f32)
    for h in range(2):
        for r in range(3):
            work_ref[h, total * r : total * (r + 1)] = wide[:, 3 * h + r]
        for m in range(4):
            for j in range(4):
                (one_ref, two_ref)[m // 2][m % 2, 4 * h + j] = work_ref[
                    h, inner * m : inner * (m + 1), inner * j : inner * (j + 1)
                ]
    lines = wide[:24, 6]

    def joined(*rows):
        return jnp.concatenate([lines[r : r + 1] for r in rows], axis=1)

    fc_ref[...] = joined(*range(8))[0]
    out_ref[...] = joined(8, 9)[0]
    gain1_ref[...] = (joined(10, 11) + joined(14, 19))[0]
    gain2_ref[...] = joined(12, 13)[0]
    for i in range(2):
        b1_ref[i : i + 1] = joined(15 + i, 20 + i)
        b2_ref[i : i + 1] = joined(17 + i, 22 + i)


def whole(shape):
    zeros = (0,) * len(shape)
    return pl.BlockSpec(shape, lambda *_: zeros)


def call(kernel, outs, *args, grant=16, grid=(1,), in_specs=None, out_specs=None, free=(), free_outs=(), **more):
    in_specs = in_specs or [whole(a.shape) for a in args]
    return pl.pallas_call(
        kernel,
        out_shape=[
            (jax.ShapeDtypeStruct if i in free_outs else pltpu.HBM)(shape, kind)
            for i, (shape, kind) in enumerate(outs)
        ],
        compiler_params=pltpu.CompilerParams(vmem_limit_bytes=grant << 20),
        grid=grid,
        in_specs=in_specs,
        out_specs=out_specs or [whole(shape) for shape, _ in outs],
        **more,
    )(
        *(
            a if spec is SMEM or i in free else pltpu.with_memory_space_constraint(a, pltpu.HBM)
            for i, (a, spec) in enumerate(zip(args, in_specs))
        )
    )


SMEM = pl.BlockSpec(memory_space=pltpu.SMEM)


def weight_kernel(
    place_ref,
    grad_ref,
    active_ref,
    flat_ref,
    cot_ref,
    tall_ref,
    wide_ref,
    own_ref,
    out1_ref,
    near_ref,
    wrap_ref,
    out3_ref,
    acc_ref,
):
    step = pl.program_id(0)
    low, at_z = step // 4, step % 4
    share = own_ref.shape[1]
    x, y, core = place_ref[0], place_ref[1], place_ref[3]
    first = core == 0

    @pl.when(first)
    def _():
        acc_ref[...] = dot(grad_ref[...], flat_ref[...], 0, 0)

    @pl.when(core == 1)
    def _():
        acc_ref[...] = dot(active_ref[...], cot_ref[...], 0, 0)

    acc_ref[...] += dot(tall_ref[...], wide_ref[...], 0, 0)
    for at_y in range(4):
        for at_xh in range(2):
            at_x = 2 * at_xh + low
            at = (at_y * 2 + at_xh) * share
            far = jnp.where(first, at_x - x, at_y - y) & 3
            spot = jnp.where(first, at_y * 4 + at_z, at_z * 4 + at_x)
            upper = spot >= 8
            for ref, here, spot in (
                (own_ref, far == 0, spot),
                (out1_ref, far == 1, spot),
                (near_ref, (far == 2) & (spot < 8), spot),
                (wrap_ref, (far == 2) & upper, spot - 8),
                (out3_ref, far == 3, spot),
            ):

                @pl.when(here)
                def _(ref=ref, at=at, spot=spot):
                    ref[spot] = acc_ref[at : at + share].astype(ref.dtype)


def relay_kernel(out1_ref, out3_ref, near_ref, wrap_ref, plus_ref, minus_ref):
    plus_ref[:8] = (out1_ref[:8].astype(f32) + near_ref[...].astype(f32)).astype(bf16)
    plus_ref[8:] = out1_ref[8:]
    minus_ref[:8] = out3_ref[:8]
    minus_ref[8:] = (out3_ref[8:].astype(f32) + wrap_ref[...].astype(f32)).astype(bf16)


def plane_kernel(place_ref, own_in_ref, *refs):
    got, own_ref, outs = refs[:2], refs[2], refs[3:]
    for d in range(4):
        for i in range(4):
            at = 4 * ((place_ref[4] + d) & 3) + i
            total = own_in_ref[at]
            for r in range(2):
                total = total + got[r][at].astype(f32)
            if d == 0:
                own_ref[i] = total
            else:
                outs[d - 1][i] = total.astype(bf16)


def line_kernel(place_ref, own_in_ref, *refs):
    got, own_ref, outs = refs[:3], refs[3], refs[4:]
    for d in range(4):
        at = (place_ref[5] + d) & 3
        total = own_in_ref[at]
        for r in range(3):
            total = total + got[r][at].astype(f32)
        if d == 0:
            own_ref[...] = total
        else:
            outs[d - 1][...] = total.astype(bf16)


def point_kernel(scale, place_ref, own_ref, *refs):
    got, kept_ref, send_ref = refs[:3], refs[3], refs[4]
    share = kept_ref.shape[0]
    total = own_ref[...]
    for r in range(3):
        total = total + got[r][...].astype(f32)
    total = total * scale
    first = place_ref[3] == 0
    kept_ref[...] = jnp.where(first, total[:share], total[share:])
    send_ref[...] = jnp.where(first, total[share:], total[:share])


def neighbours(stage, far):
    pairs = []
    for rank in range(128):
        core, xh, y, z, low = rank & 1, (rank >> 1) & 1, (rank >> 2) & 3, (rank >> 4) & 3, rank >> 6
        at = [2 * xh + low, y, z]
        axis = (stage + core) % 3
        at[axis] = (at[axis] + far) & 3
        x, y, z = at
        pairs.append((rank, ((x & 1) << 6) | (z << 4) | (y << 2) | ((x >> 1) << 1) | core))
    return pairs


def send_all(pieces, stage):
    return [lax.ppermute(pieces[r], EVERY, neighbours(stage, r + 1)) for r in range(3)]


def after(value, others):
    return lax.optimization_barrier((value, others))[0]


def weight_place():
    core = lax.axis_index("c")
    x = 2 * lax.axis_index("xh") + lax.axis_index("dp")
    y, z = lax.axis_index("y"), lax.axis_index("z")
    first = core == 0
    return jnp.stack(
        (x, y, z, core, jnp.where(first, y, z), jnp.where(first, z, x), lax.axis_index("dp"))
    ).astype(
        jnp.int32
    )


def swap(values):
    return lax.ppermute(values, "c", [(0, 1), (1, 0)])


def weight_start(place, grad_hidden, active, flat, cot, tall):
    tokens, hidden = grad_hidden.shape
    width = flat.shape[1]
    first = place[3] == 0
    tall = swap(tall)
    wide = swap(jnp.where(first, cot, flat))
    cube = (16, hidden // 64, width)
    half = (8,) + cube[1:]
    ahead = pl.BlockSpec((tokens, hidden // 8), lambda g: (0, g))
    across = whole(flat.shape)
    return call(
        weight_kernel,
        [(cube, f32), (cube, bf16), (half, bf16), (half, bf16), (cube, bf16)],
        place,
        grad_hidden,
        active,
        flat,
        cot,
        tall,
        wide,
        grant=24,
        grid=(8,),
        in_specs=[SMEM, ahead, ahead, across, across, ahead, across],
        out_specs=[whole(cube), whole(cube), whole(half), whole(half), whole(cube)],
        scratch_shapes=[pltpu.VMEM((hidden // 8, width), f32)],
        free=(3, 4, 5, 6),
        cost_estimate=pl.CostEstimate(
            flops=4 * tokens * hidden * width, bytes_accessed=14 << 20, transcendentals=0
        ),
    )


def weight_second(place, own, got):
    cube = own.shape
    row = (4,) + cube[1:]
    return call(
        plane_kernel,
        [(row, f32)] + [(row, bf16)] * 3,
        place,
        own,
        *got,
        grid=(1,),
        in_specs=[SMEM] + [whole(cube)] * 3,
        out_specs=[whole(row)] * 4,
        free=range(4),
        free_outs=range(4),
    )


def weight_third(place, own, got):
    row = own.shape
    line = row[1:]
    return call(
        line_kernel,
        [(line, f32)] + [(line, bf16)] * 3,
        place,
        own,
        *got,
        grid=(1,),
        in_specs=[SMEM, whole(row)] + [whole(row)] * 3,
        out_specs=[whole(line)] * 4,
        free=range(5),
        free_outs=range(4),
    )


def block_diagonal(weights):
    blocks, inner = weights.shape[1:3]
    tall = weights.reshape(2, blocks * inner, inner)
    wide = jnp.concatenate((tall,) * blocks, axis=2)
    row = lax.broadcasted_iota(jnp.int32, wide.shape, 1) // inner
    lane = lax.broadcasted_iota(jnp.int32, wide.shape, 2) // inner
    return jnp.where(row == lane, wide, 0.0)


def local(
    stash,
    piece_map,
    gain_one,
    spec_one,
    bias_one,
    spec_two,
    bias_two,
    gain_two,
    fc_one,
    bias_fc,
    fc_two,
    cotangent,
):
    samples, _, lon_cells, width = cotangent.shape
    lat_total = lax.axis_size(SPACE)
    ranks = lax.axis_size(EVERY)
    tokens = samples * lon_cells
    hidden = fc_one.shape[1]
    half = width // 2
    rows = 4 * ranks
    piece = (ranks, 4, half)
    plain_table, doubled_table = zonal_tables(samples, lon_cells)
    meridian = meridian_table(samples, lat_total)
    down, back_down = high_low(plain_table), high_low(doubled_table)
    up, back_up = high_low(plain_table.T), high_low(doubled_table.T)
    forward, inverse = high_low(meridian), high_low(meridian.T)

    arrived = exchange(stash[0], SPACE)
    ordering = jnp.argsort(piece_map[:, 0])
    placed = jnp.take(arrived, ordering, axis=0)
    base = jnp.transpose(placed, (1, 0, 2)).reshape(tokens, width).astype(f32)
    upstream = cotangent.reshape(tokens, width)
    gains = jnp.stack((gain_one, gain_two))

    which = lax.axis_index("dp")
    blocks, inner = spec_one.shape[1:3]
    mine = blocks // 2
    both = jnp.concatenate(
        [
            block_diagonal(lax.dynamic_slice_in_dim(w, which * mine, mine, 1))
            for w in (spec_one, spec_two)
        ]
    )
    weights = jnp.stack(split(both))
    vectors = lax.dynamic_slice_in_dim(
        jnp.concatenate((gain_one[None], bias_one, bias_two)), which * half, half, 1
    )

    sent, xhat, rstd = call(
        first_kernel,
        [(piece, bf16), ((tokens, width), f32), ((tokens, 128), f32)],
        base,
        down,
        free=(0,),
    )
    got = exchange(sent, EVERY)
    sent, plain, pre = call(
        spectral_kernel,
        [(piece, bf16), ((2, rows // 2, half), f32), ((2, rows // 2, half), f32)],
        got,
        forward,
        inverse,
        weights,
        vectors,
        free=(0,),
    )
    got = exchange(sent, EVERY)
    normed_flat, xhat2, rstd2 = call(
        field_kernel,
        [((tokens, width), bf16), ((tokens, width), f32), ((tokens, 128), f32)],
        got,
        back_up,
        base,
        xhat,
        gains,
        free=(0,),
        free_outs=(0,),
    )
    place = weight_place()
    block = (tokens, hidden // 8)
    across = pl.BlockSpec(block, lambda g: (0, g))
    grad_hidden_flat, active_flat, tall, bias_sum = call(
        hidden_kernel,
        [((tokens, hidden), bf16)] * 3 + [((8, 1, hidden // 8), f32)],
        place,
        normed_flat,
        upstream,
        fc_one,
        bias_fc.reshape(1, hidden),
        fc_two,
        grid=(8,),
        in_specs=[
            SMEM,
            whole(normed_flat.shape),
            whole(upstream.shape),
            pl.BlockSpec((width, hidden // 8), lambda g: (0, g)),
            pl.BlockSpec((1, hidden // 8), lambda g: (0, g)),
            pl.BlockSpec((hidden // 8, width), lambda g: (g, 0)),
        ],
        out_specs=[across] * 3 + [pl.BlockSpec((1, 1, hidden // 8), lambda g: (g, 0, 0))],
        free=(1, 2, 4),
        free_outs=(3,),
        cost_estimate=pl.CostEstimate(
            flops=4 * tokens * hidden * width,
            bytes_accessed=18 << 20,
            transcendentals=tokens * hidden,
        ),
    )
    grad_normed_two = jnp.einsum("tf,df->td", grad_hidden_flat, fc_one, preferred_element_type=f32)
    sent, grad_mixed, sums = call(
        back_kernel,
        [(piece, bf16), ((tokens, width), f32), ((3, width), f32)],
        grad_normed_two,
        upstream,
        xhat2,
        rstd2,
        xhat,
        gains,
        back_down,
        free=(0, 1),
    )
    got = exchange(sent, EVERY)

    grad_scale = 1.0 / math.sqrt(samples * lax.axis_size("dp") * lat_total * lon_cells)
    own, *sent = weight_start(
        place, grad_hidden_flat, active_flat, normed_flat, upstream, tall
    )
    near = lax.ppermute(sent[1], EVERY, neighbours(0, 1))
    wrap = lax.ppermute(sent[2], EVERY, neighbours(0, 3))
    got = after(got, sent)

    lines = jnp.concatenate((bias_sum.reshape(-1, half), sums.reshape(-1, half)))
    matrices = (4 * inner, half)
    (packet,) = call(
        spectral_back_kernel,
        [((ranks, 8, half), bf16)],
        got,
        forward,
        inverse,
        weights,
        vectors,
        plain,
        pre,
        lines,
        place,
        in_specs=[whole(a.shape) for a in (got, forward, inverse, weights, vectors, plain, pre)]
        + [whole(lines.shape), SMEM],
        scratch_shapes=[
            pltpu.VMEM(matrices, f32),
            pltpu.VMEM((5, half), f32),
            pltpu.VMEM((ranks, 8, half), f32),
        ],
        free=(0, 7, 8),
        grant=20,
    )
    got = exchange(packet, EVERY)
    plus, minus = call(
        relay_kernel, [(plane, bf16) for plane in (own.shape,) * 2], sent[0], sent[3], near, wrap, free=(2, 3)
    )
    first_got = [
        lax.ppermute(plus, EVERY, neighbours(0, 1)),
        lax.ppermute(minus, EVERY, neighbours(0, 3)),
    ]
    own, *sent = weight_second(place, own, first_got)
    second_got = send_all(sent, 1)
    (grad_input,) = call(
        last_kernel,
        [((tokens, 1, width), f32)],
        after(got, sent),
        up,
        grad_mixed,
        xhat,
        rstd,
        gains,
        free=(0,),
    )
    sides = jnp.sum(got[:, 4:].reshape(2, ranks // 2, 4, half).astype(f32), axis=1)
    total = jnp.concatenate(
        (sides[0, :3], sides[1, :3], sides[0, 3:] + sides[1, 3:], jnp.zeros((1, half), f32))
    )
    total = (total * grad_scale).astype(bf16)
    spread = exchange(jnp.broadcast_to(total, (ranks,) + total.shape), EVERY)
    own, *sent = weight_third(place, after(own, grad_input), second_got)
    third_got = send_all(sent, 2)
    spread = after(spread, sent)
    whole_spec = spec_one.shape
    unpacked = call(
        unpack_kernel,
        [
            (whole_spec, f32),
            (whole_spec, f32),
            ((hidden,), f32),
            ((width,), f32),
            ((width,), f32),
            ((width,), f32),
            ((2, width), f32),
            ((2, width), f32),
        ],
        spread,
        scratch_shapes=[pltpu.VMEM((2,) + matrices, f32)],
        free=(0,),
    )
    spec_one_grad, spec_two_grad, fc_grad, out_grad, gain1, gain2, bias1, bias2 = unpacked
    kept, away = call(
        lambda *refs: point_kernel(grad_scale, *refs),
        [((hidden // ranks, width), f32)] * 2,
        place,
        after(own, fc_grad),
        *third_got,
        in_specs=[SMEM] + [whole(own.shape)] * 4,
        free=range(5),
        free_outs=range(2),
    )
    came = swap(away)
    first = place[3] == 0
    grad_one = jnp.where(first, kept, came)
    grad_two = jnp.where(first, came, kept)
    return (
        grad_input.reshape(samples, lon_cells, 1, width).transpose(0, 2, 1, 3),
        grad_one.T,
        grad_two,
        fc_grad,
        out_grad,
        gain1,
        gain2,
        spec_one_grad,
        bias1,
        spec_two_grad,
        bias2,
    )


def solution(mesh):
    fine = Mesh(mesh.devices.reshape(2, 4, 4, 2, 2), EVERY)
    placed = (
        P(SPACE, None, "dp", None),
        P(None, SPACE),
        P(),
        P(),
        P(),
        P(),
        P(),
        P(),
        P(),
        P(),
        P(),
        P("dp", SPACE, None, None),
    )

    return jax.shard_map(
        local,
        mesh=fine,
        in_specs=placed,
        out_specs=(
            P("dp", SPACE, None, None),
            P(None, EVERY),
            P(EVERY, None),
        )
        + (P(),) * 8,
        check_vma=False,
    )
```

```python
import math

import jax
import jax.numpy as jnp
import numpy as np
from jax import lax
from jax.experimental import pallas as pl
from jax.experimental.pallas import tpu as pltpu
from jax.sharding import Mesh, PartitionSpec as P

KW = 64
SPACE = ("z", "y", "xh", "c")
EVERY = ("dp",) + SPACE

epsilon = 1e-05
bf16 = jnp.bfloat16
f32 = jnp.float32
ROOT = math.sqrt(2.0 / math.pi)
CUBE = 0.044715


def exchange(values, axes):
    return lax.all_to_all(values, axes, split_axis=0, concat_axis=0, tiled=True)


def high_low(table):
    table = np.asarray(table, np.float32)
    high = table.astype(bf16)
    low = (table - high.astype(np.float32)).astype(bf16)
    return np.stack((high, low))


def zonal_tables(samples, lon):
    angle = 2.0 * np.pi * (np.outer(np.arange(KW), np.arange(lon)) % lon) / lon
    both = np.stack((np.cos(angle), -np.sin(angle)), axis=1) / math.sqrt(lon)
    eye = np.eye(samples)
    plain = np.einsum("krw,ab->krabw", both, eye)
    plain = plain.reshape(KW * 2 * samples, samples * lon)
    double = np.where(np.arange(KW) == 0, 1.0, 2.0)
    doubled = plain * np.repeat(double, 2 * samples)[:, None]
    return plain, doubled


def meridian_table(samples, lat):
    angle = 2.0 * np.pi * (np.outer(np.arange(lat), np.arange(lat)) % lat) / lat
    cos, sin = np.cos(angle) / math.sqrt(lat), np.sin(angle) / math.sqrt(lat)
    turn = np.stack((np.stack((cos, sin), -1), np.stack((-sin, cos), -1)))
    whole = np.einsum("qksr,ab->qkasrb", turn, np.eye(samples))
    return whole.reshape(2 * lat * samples, lat * 2 * samples)


def dot(a, b, ca=1, cb=0):
    return lax.dot_general(a, b, (((ca,), (cb,)), ((), ())), preferred_element_type=f32)


def split(a):
    high = a.astype(bf16)
    return high, (a - high.astype(f32)).astype(bf16)


def dot3(a, b, ca=1, cb=0):
    return dot(a[0], b[0], ca, cb) + (dot(a[1], b[0], ca, cb) + dot(a[0], b[1], ca, cb))


def dot2(table, b):
    return dot(table[0], b) + dot(table[1], b)


def bend(x):
    return jnp.tanh(ROOT * (x + CUBE * (x * x * x)))


def smooth_gate(x):
    return 0.5 * x * (1.0 + bend(x))


def gate_slope(x):
    t = bend(x)
    return 0.5 * (1.0 + t) + (0.5 * x) * (1.0 - t * t) * (ROOT * (1.0 + (3.0 * CUBE) * (x * x)))


def normalise(x):
    centred = x - jnp.mean(x, axis=-1, keepdims=True)
    rstd = lax.rsqrt(jnp.mean(centred * centred, axis=-1, keepdims=True) + epsilon)
    return centred * rstd, rstd


def norm_pull(grad, gain, xhat, rstd):
    scaled = grad * gain
    return rstd * (
        scaled
        - jnp.mean(scaled, axis=-1, keepdims=True)
        - xhat * jnp.mean(scaled * xhat, axis=-1, keepdims=True)
    )


def to_rows(block):
    return block.astype(f32).reshape(block.shape[0] * block.shape[1], block.shape[2]).astype(bf16)


def to_pieces(values):
    return values.reshape(values.shape[0] // 4, 4, values.shape[1]).astype(bf16)


def project(values, table_ref, out_ref):
    half = out_ref.shape[2]
    ranks = out_ref.shape[0] // 2
    found = dot3((table_ref[0], table_ref[1]), split(values))
    out_ref[:ranks] = to_pieces(found[:, :half])
    out_ref[ranks:] = to_pieces(found[:, half:])


def expand(rows_ref, table_ref):
    ranks = rows_ref.shape[0] // 2
    table = (table_ref[0], table_ref[1])
    return jnp.concatenate(
        [dot2(table, to_rows(rows_ref[ranks * h : ranks * (h + 1), :4])) for h in range(2)], axis=1
    )


def first_kernel(base_ref, table_ref, sent_ref, xhat_ref, rstd_ref):
    xhat, rstd = normalise(base_ref[...])
    xhat_ref[...] = xhat
    rstd_ref[...] = jnp.broadcast_to(rstd, rstd_ref.shape)
    project(xhat, table_ref, sent_ref)


def field_kernel(rows_ref, table_ref, base_ref, xhat_ref, gains_ref, flat_ref, xhat2_ref, rstd2_ref):
    mixed = base_ref[...] + xhat_ref[...] * gains_ref[0:1] + expand(rows_ref, table_ref)
    xhat2, rstd2 = normalise(mixed)
    xhat2_ref[...] = xhat2
    rstd2_ref[...] = jnp.broadcast_to(rstd2, rstd2_ref.shape)
    flat_ref[...] = (xhat2 * gains_ref[1:2]).astype(bf16)


def back_kernel(
    grad_ref, cot_ref, xhat2_ref, rstd2_ref, xhat_ref, gains_ref, table_ref, sent_ref, mixed_ref, sums_ref
):
    grad = grad_ref[...]
    xhat2 = xhat2_ref[...]
    cot = cot_ref[...].astype(f32)
    mixed = cot + norm_pull(grad, gains_ref[1:2], xhat2, rstd2_ref[:, 0:1])
    mixed_ref[...] = mixed
    sums_ref[0:1] = jnp.sum(cot, axis=0, keepdims=True)
    sums_ref[1:2] = jnp.sum(mixed * xhat_ref[...], axis=0, keepdims=True)
    sums_ref[2:3] = jnp.sum(grad * xhat2, axis=0, keepdims=True)
    project(mixed, table_ref, sent_ref)


def last_kernel(rows_ref, table_ref, mixed_ref, xhat_ref, rstd_ref, gains_ref, out_ref):
    mixed = mixed_ref[...]
    grad = mixed + expand(rows_ref, table_ref)
    result = mixed + norm_pull(grad, gains_ref[0:1], xhat_ref[...], rstd_ref[:, 0:1])
    out_ref[:, 0] = result


def hidden_kernel(
    place_ref, flat_ref, cot_ref, one_ref, bias_ref, two_ref, grad_ref, active_ref, tall_ref, sum_ref
):
    pre = dot(flat_ref[...], one_ref[...]) + bias_ref[...]
    up = dot(cot_ref[...], two_ref[...], 1, 1)
    t = bend(pre)
    half = 0.5 * (1.0 + t)
    active = pre * half
    grad = up * (half + (0.5 * pre) * (1.0 - t * t) * (ROOT + (3.0 * CUBE * ROOT) * (pre * pre)))
    grad_ref[...] = grad.astype(bf16)
    active_ref[...] = active.astype(bf16)
    tall_ref[...] = jnp.where(place_ref[3] == 0, active, grad).astype(bf16)
    sum_ref[0] = jnp.sum(grad, axis=0, keepdims=True)


def mix(real, imag, weights, index):
    both = (weights[0, index], weights[1, index])
    first, second = dot3(split(real), both), dot3(split(imag), both)
    n = first.shape[1] // 2
    return first[:, :n] - second[:, n:], first[:, n:] + second[:, :n]


def beside(left, right):
    return tuple(jnp.concatenate(pair, axis=1) for pair in zip(left, right))


def mix_pull(real, imag, weights, index):
    both = (weights[0, index], weights[1, index])
    turned = beside(imag, tuple(-r for r in real))
    return dot3(beside(real, imag), both, 1, 1), dot3(turned, both, 1, 1)


def compact(full, inner):
    lane = lax.broadcasted_iota(jnp.int32, (inner, full.shape[1]), 1)
    kept = None
    for j in range(full.shape[0] // inner):
        here = (lane >= inner * j) & (lane < inner * (j + 1))
        part = jnp.where(here, full[inner * j : inner * (j + 1)], 0.0)
        kept = part if kept is None else kept + part
    return kept


def spectral_kernel(rows_ref, table_ref, turned_ref, weights_ref, vectors_ref, sent_ref, plain_ref, pre_ref):
    ranks = rows_ref.shape[0] // 2
    half = 2 * ranks
    table = (table_ref[0], table_ref[1])
    for dp in range(2):
        found = dot2(table, to_rows(rows_ref[ranks * dp : ranks * (dp + 1)]))
        plain_ref[0, half * dp : half * (dp + 1)] = found[:half]
        plain_ref[1, half * dp : half * (dp + 1)] = found[half:]
    gain = vectors_ref[0:1]
    real, imag = mix(plain_ref[0] * gain, plain_ref[1] * gain, weights_ref, 0)
    real = real + vectors_ref[1:2]
    imag = imag + vectors_ref[2:3]
    pre_ref[0] = real
    pre_ref[1] = imag
    real, imag = mix(smooth_gate(real), smooth_gate(imag), weights_ref, 1)
    real = real + vectors_ref[3:4]
    imag = imag + vectors_ref[4:5]
    turned = (turned_ref[0], turned_ref[1])
    for dp in range(2):
        both = jnp.concatenate(
            (real[half * dp : half * (dp + 1)], imag[half * dp : half * (dp + 1)]), axis=0
        )
        sent_ref[ranks * dp : ranks * (dp + 1)] = to_pieces(dot3(turned, split(both)))


def spectral_back_kernel(
    rows_ref,
    table_ref,
    turned_ref,
    weights_ref,
    vectors_ref,
    plain_ref,
    pre_ref,
    lines_ref,
    place_ref,
    packet_ref,
    grads_ref,
    sums_ref,
    work_ref,
):
    ranks = rows_ref.shape[0] // 2
    half = 2 * ranks
    inner = grads_ref.shape[0] // 4
    table = (table_ref[0], table_ref[1])
    found = [
        dot2(table, to_rows(rows_ref[ranks * dp : ranks * (dp + 1)])) for dp in range(2)
    ]
    real = jnp.concatenate((found[0][:half], found[1][:half]), axis=0)
    imag = jnp.concatenate((found[0][half:], found[1][half:]), axis=0)

    def weight_grads(first, second, grad_real, grad_imag, at):
        both = beside(grad_real, grad_imag)
        a, b = dot3(first, both, 0, 0), dot3(second, both, 0, 0)
        n = a.shape[1] // 2
        grads_ref[inner * at : inner * (at + 1)] = compact(a[:, :n] + b[:, n:], inner)
        grads_ref[inner * (at + 1) : inner * (at + 2)] = compact(a[:, n:] - b[:, :n], inner)

    sums_ref[3:4] = jnp.sum(real, axis=0, keepdims=True)
    sums_ref[4:5] = jnp.sum(imag, axis=0, keepdims=True)
    pre_real, pre_imag = pre_ref[0], pre_ref[1]
    real, imag = split(real), split(imag)
    weight_grads(split(smooth_gate(pre_real)), split(smooth_gate(pre_imag)), real, imag, 2)
    real, imag = mix_pull(real, imag, weights_ref, 1)
    real = real * gate_slope(pre_real)
    imag = imag * gate_slope(pre_imag)
    sums_ref[1:2] = jnp.sum(real, axis=0, keepdims=True)
    sums_ref[2:3] = jnp.sum(imag, axis=0, keepdims=True)
    gain = vectors_ref[0:1]
    real, imag = split(real), split(imag)
    plain_real, plain_imag = plain_ref[0], plain_ref[1]
    weight_grads(split(plain_real * gain), split(plain_imag * gain), real, imag, 0)
    real, imag = mix_pull(real, imag, weights_ref, 0)
    sums_ref[0:1] = jnp.sum(real * plain_real + imag * plain_imag, axis=0, keepdims=True)
    turned = (turned_ref[0], turned_ref[1])
    for dp in range(2):
        both = jnp.concatenate(
            (real[half * dp : half * (dp + 1)], imag[half * dp : half * (dp + 1)]), axis=0
        )
        found = dot3(turned, split(both))
        work_ref[ranks * dp : ranks * (dp + 1), 0:4] = found.reshape(ranks, 4, found.shape[1])
    total = 2 * ranks
    for r in range(3):
        work_ref[:, 4 + r] = grads_ref[total * r : total * (r + 1)]
    known = lines_ref.shape[0]
    work_ref[:, 7] = jnp.zeros((total, found.shape[1]), f32)
    work_ref[:known, 7] = lines_ref[...]
    for h in range(2):

        @pl.when(place_ref[6] == h)
        def _(h=h):
            work_ref[known + 5 * h : known + 5 * h + 5, 7] = sums_ref[...]

    packet_ref[...] = work_ref[...].astype(bf16)


def unpack_kernel(spread_ref, one_ref, two_ref, fc_ref, out_ref, gain1_ref, gain2_ref, b1_ref, b2_ref, work_ref):
    total = spread_ref.shape[0]
    inner = one_ref.shape[2]
    wide = spread_ref[...].astype(f32)
    for h in range(2):
        for r in range(3):
            work_ref[h, total * r : total * (r + 1)] = wide[:, 3 * h + r]
        for m in range(4):
            for j in range(4):
                (one_ref, two_ref)[m // 2][m % 2, 4 * h + j] = work_ref[
                    h, inner * m : inner * (m + 1), inner * j : inner * (j + 1)
                ]
    lines = wide[:24, 6]

    def joined(*rows):
        return jnp.concatenate([lines[r : r + 1] for r in rows], axis=1)

    fc_ref[...] = joined(*range(8))[0]
    out_ref[...] = joined(8, 9)[0]
    gain1_ref[...] = (joined(10, 11) + joined(14, 19))[0]
    gain2_ref[...] = joined(12, 13)[0]
    for i in range(2):
        b1_ref[i : i + 1] = joined(15 + i, 20 + i)
        b2_ref[i : i + 1] = joined(17 + i, 22 + i)


def whole(shape):
    zeros = (0,) * len(shape)
    return pl.BlockSpec(shape, lambda *_: zeros)


def call(kernel, outs, *args, grant=16, grid=(1,), in_specs=None, out_specs=None, free=(), free_outs=(), **more):
    in_specs = in_specs or [whole(a.shape) for a in args]
    return pl.pallas_call(
        kernel,
        out_shape=[
            (jax.ShapeDtypeStruct if i in free_outs else pltpu.HBM)(shape, kind)
            for i, (shape, kind) in enumerate(outs)
        ],
        compiler_params=pltpu.CompilerParams(vmem_limit_bytes=grant << 20),
        grid=grid,
        in_specs=in_specs,
        out_specs=out_specs or [whole(shape) for shape, _ in outs],
        **more,
    )(
        *(
            a if spec is SMEM or i in free else pltpu.with_memory_space_constraint(a, pltpu.HBM)
            for i, (a, spec) in enumerate(zip(args, in_specs))
        )
    )


SMEM = pl.BlockSpec(memory_space=pltpu.SMEM)


def weight_kernel(
    place_ref,
    grad_ref,
    active_ref,
    flat_ref,
    cot_ref,
    tall_ref,
    wide_ref,
    own_ref,
    out1_ref,
    near_ref,
    wrap_ref,
    out3_ref,
    acc_ref,
):
    step = pl.program_id(0)
    low, at_z = step // 4, step % 4
    share = own_ref.shape[1]
    x, y, core = place_ref[0], place_ref[1], place_ref[3]
    first = core == 0

    @pl.when(first)
    def _():
        acc_ref[...] = dot(grad_ref[...], flat_ref[...], 0, 0)

    @pl.when(core == 1)
    def _():
        acc_ref[...] = dot(active_ref[...], cot_ref[...], 0, 0)

    acc_ref[...] += dot(tall_ref[...], wide_ref[...], 0, 0)
    for at_y in range(4):
        for at_xh in range(2):
            at_x = 2 * at_xh + low
            at = (at_y * 2 + at_xh) * share
            far = jnp.where(first, at_x - x, at_y - y) & 3
            spot = jnp.where(first, at_y * 4 + at_z, at_z * 4 + at_x)
            upper = spot >= 8
            for ref, here, spot in (
                (own_ref, far == 0, spot),
                (out1_ref, far == 1, spot),
                (near_ref, (far == 2) & (spot < 8), spot),
                (wrap_ref, (far == 2) & upper, spot - 8),
                (out3_ref, far == 3, spot),
            ):

                @pl.when(here)
                def _(ref=ref, at=at, spot=spot):
                    ref[spot] = acc_ref[at : at + share].astype(ref.dtype)


def relay_kernel(out1_ref, out3_ref, near_ref, wrap_ref, plus_ref, minus_ref):
    plus_ref[:8] = (out1_ref[:8].astype(f32) + near_ref[...].astype(f32)).astype(bf16)
    plus_ref[8:] = out1_ref[8:]
    minus_ref[:8] = out3_ref[:8]
    minus_ref[8:] = (out3_ref[8:].astype(f32) + wrap_ref[...].astype(f32)).astype(bf16)


def plane_kernel(place_ref, own_in_ref, *refs):
    got, own_ref, outs = refs[:2], refs[2], refs[3:]
    for d in range(4):
        for i in range(4):
            at = 4 * ((place_ref[4] + d) & 3) + i
            total = own_in_ref[at]
            for r in range(2):
                total = total + got[r][at].astype(f32)
            if d == 0:
                own_ref[i] = total
            else:
                outs[d - 1][i] = total.astype(bf16)


def line_kernel(place_ref, own_in_ref, *refs):
    got, own_ref, outs = refs[:3], refs[3], refs[4:]
    for d in range(4):
        at = (place_ref[5] + d) & 3
        total = own_in_ref[at]
        for r in range(3):
            total = total + got[r][at].astype(f32)
        if d == 0:
            own_ref[...] = total
        else:
            outs[d - 1][...] = total.astype(bf16)


def point_kernel(scale, place_ref, own_ref, *refs):
    got, kept_ref, send_ref = refs[:3], refs[3], refs[4]
    share = kept_ref.shape[0]
    total = own_ref[...]
    for r in range(3):
        total = total + got[r][...].astype(f32)
    total = total * scale
    first = place_ref[3] == 0
    kept_ref[...] = jnp.where(first, total[:share], total[share:])
    send_ref[...] = jnp.where(first, total[share:], total[:share])


def neighbours(stage, far):
    pairs = []
    for rank in range(128):
        core, xh, y, z, low = rank & 1, (rank >> 1) & 1, (rank >> 2) & 3, (rank >> 4) & 3, rank >> 6
        at = [2 * xh + low, y, z]
        axis = (stage + core) % 3
        at[axis] = (at[axis] + far) & 3
        x, y, z = at
        pairs.append((rank, ((x & 1) << 6) | (z << 4) | (y << 2) | ((x >> 1) << 1) | core))
    return pairs


def send_all(pieces, stage):
    return [lax.ppermute(pieces[r], EVERY, neighbours(stage, r + 1)) for r in range(3)]


def after(value, others):
    return lax.optimization_barrier((value, others))[0]


def weight_place():
    core = lax.axis_index("c")
    x = 2 * lax.axis_index("xh") + lax.axis_index("dp")
    y, z = lax.axis_index("y"), lax.axis_index("z")
    first = core == 0
    return jnp.stack(
        (x, y, z, core, jnp.where(first, y, z), jnp.where(first, z, x), lax.axis_index("dp"))
    ).astype(
        jnp.int32
    )


def swap(values):
    return lax.ppermute(values, "c", [(0, 1), (1, 0)])


def weight_start(place, grad_hidden, active, flat, cot, tall):
    tokens, hidden = grad_hidden.shape
    width = flat.shape[1]
    first = place[3] == 0
    tall = swap(tall)
    wide = swap(jnp.where(first, cot, flat))
    cube = (16, hidden // 64, width)
    half = (8,) + cube[1:]
    ahead = pl.BlockSpec((tokens, hidden // 8), lambda g: (0, g))
    across = whole(flat.shape)
    return call(
        weight_kernel,
        [(cube, f32), (cube, bf16), (half, bf16), (half, bf16), (cube, bf16)],
        place,
        grad_hidden,
        active,
        flat,
        cot,
        tall,
        wide,
        grant=24,
        grid=(8,),
        in_specs=[SMEM, ahead, ahead, across, across, ahead, across],
        out_specs=[whole(cube), whole(cube), whole(half), whole(half), whole(cube)],
        scratch_shapes=[pltpu.VMEM((hidden // 8, width), f32)],
        free=(3, 4, 5, 6),
        cost_estimate=pl.CostEstimate(
            flops=4 * tokens * hidden * width, bytes_accessed=14 << 20, transcendentals=0
        ),
    )


def weight_second(place, own, got):
    cube = own.shape
    row = (4,) + cube[1:]
    return call(
        plane_kernel,
        [(row, f32)] + [(row, bf16)] * 3,
        place,
        own,
        *got,
        grid=(1,),
        in_specs=[SMEM] + [whole(cube)] * 3,
        out_specs=[whole(row)] * 4,
        free=(2, 3),
        free_outs=range(4),
    )


def weight_third(place, own, got):
    row = own.shape
    line = row[1:]
    return call(
        line_kernel,
        [(line, f32)] + [(line, bf16)] * 3,
        place,
        own,
        *got,
        grid=(1,),
        in_specs=[SMEM, whole(row)] + [whole(row)] * 3,
        out_specs=[whole(line)] * 4,
        free=range(5),
        free_outs=range(4),
    )


def block_diagonal(weights):
    blocks, inner = weights.shape[1:3]
    tall = weights.reshape(2, blocks * inner, inner)
    wide = jnp.concatenate((tall,) * blocks, axis=2)
    row = lax.broadcasted_iota(jnp.int32, wide.shape, 1) // inner
    lane = lax.broadcasted_iota(jnp.int32, wide.shape, 2) // inner
    return jnp.where(row == lane, wide, 0.0)


def local(
    stash,
    piece_map,
    gain_one,
    spec_one,
    bias_one,
    spec_two,
    bias_two,
    gain_two,
    fc_one,
    bias_fc,
    fc_two,
    cotangent,
):
    samples, _, lon_cells, width = cotangent.shape
    lat_total = lax.axis_size(SPACE)
    ranks = lax.axis_size(EVERY)
    tokens = samples * lon_cells
    hidden = fc_one.shape[1]
    half = width // 2
    rows = 4 * ranks
    piece = (ranks, 4, half)
    plain_table, doubled_table = zonal_tables(samples, lon_cells)
    meridian = meridian_table(samples, lat_total)
    down, back_down = high_low(plain_table), high_low(doubled_table)
    up, back_up = high_low(plain_table.T), high_low(doubled_table.T)
    forward, inverse = high_low(meridian), high_low(meridian.T)

    arrived = exchange(stash[0], SPACE)
    ordering = jnp.argsort(piece_map[:, 0])
    placed = jnp.take(arrived, ordering, axis=0)
    base = jnp.transpose(placed, (1, 0, 2)).reshape(tokens, width).astype(f32)
    upstream = cotangent.reshape(tokens, width)
    gains = jnp.stack((gain_one, gain_two))

    which = lax.axis_index("dp")
    blocks, inner = spec_one.shape[1:3]
    mine = blocks // 2
    wide = [
        block_diagonal(lax.dynamic_slice_in_dim(w, which * mine, mine, 1))
        for w in (spec_one, spec_two)
    ]
    both = jnp.stack([jnp.concatenate((w[0], w[1]), axis=1) for w in wide])
    weights = jnp.stack(split(both))
    vectors = lax.dynamic_slice_in_dim(
        jnp.concatenate((gain_one[None], bias_one, bias_two)), which * half, half, 1
    )

    sent, xhat, rstd = call(
        first_kernel,
        [(piece, bf16), ((tokens, width), f32), ((tokens, 128), f32)],
        base,
        down,
        free=(0,),
    )
    got = exchange(sent, EVERY)
    sent, plain, pre = call(
        spectral_kernel,
        [(piece, bf16), ((2, rows // 2, half), f32), ((2, rows // 2, half), f32)],
        got,
        forward,
        inverse,
        weights,
        vectors,
        free=(0,),
    )
    got = exchange(sent, EVERY)
    normed_flat, xhat2, rstd2 = call(
        field_kernel,
        [((tokens, width), bf16), ((tokens, width), f32), ((tokens, 128), f32)],
        got,
        back_up,
        base,
        xhat,
        gains,
        free=(0,),
        free_outs=(0,),
    )
    place = weight_place()
    block = (tokens, hidden // 8)
    across = pl.BlockSpec(block, lambda g: (0, g))
    grad_hidden_flat, active_flat, tall, bias_sum = call(
        hidden_kernel,
        [((tokens, hidden), bf16)] * 3 + [((8, 1, hidden // 8), f32)],
        place,
        normed_flat,
        upstream,
        fc_one,
        bias_fc.reshape(1, hidden),
        fc_two,
        grid=(8,),
        in_specs=[
            SMEM,
            whole(normed_flat.shape),
            whole(upstream.shape),
            pl.BlockSpec((width, hidden // 8), lambda g: (0, g)),
            pl.BlockSpec((1, hidden // 8), lambda g: (0, g)),
            pl.BlockSpec((hidden // 8, width), lambda g: (g, 0)),
        ],
        out_specs=[across] * 3 + [pl.BlockSpec((1, 1, hidden // 8), lambda g: (g, 0, 0))],
        free=(1, 2, 4),
        free_outs=(3,),
        cost_estimate=pl.CostEstimate(
            flops=4 * tokens * hidden * width,
            bytes_accessed=18 << 20,
            transcendentals=tokens * hidden,
        ),
    )
    grad_normed_two = jnp.einsum("tf,df->td", grad_hidden_flat, fc_one, preferred_element_type=f32)
    sent, grad_mixed, sums = call(
        back_kernel,
        [(piece, bf16), ((tokens, width), f32), ((3, width), f32)],
        grad_normed_two,
        upstream,
        xhat2,
        rstd2,
        xhat,
        gains,
        back_down,
        free=(0, 1),
    )
    got = exchange(sent, EVERY)

    grad_scale = 1.0 / math.sqrt(samples * lax.axis_size("dp") * lat_total * lon_cells)
    own, *sent = weight_start(
        place, grad_hidden_flat, active_flat, normed_flat, upstream, tall
    )
    near = lax.ppermute(sent[1], EVERY, neighbours(0, 1))
    wrap = lax.ppermute(sent[2], EVERY, neighbours(0, 3))
    got = after(got, sent)

    lines = jnp.concatenate((bias_sum.reshape(-1, half), sums.reshape(-1, half)))
    matrices = (4 * inner, half)
    (packet,) = call(
        spectral_back_kernel,
        [((ranks, 8, half), bf16)],
        got,
        forward,
        inverse,
        weights,
        vectors,
        plain,
        pre,
        lines,
        place,
        in_specs=[whole(a.shape) for a in (got, forward, inverse, weights, vectors, plain, pre)]
        + [whole(lines.shape), SMEM],
        scratch_shapes=[
            pltpu.VMEM(matrices, f32),
            pltpu.VMEM((5, half), f32),
            pltpu.VMEM((ranks, 8, half), f32),
        ],
        free=(0, 7, 8),
        grant=20,
    )
    got = exchange(packet, EVERY)
    plus, minus = call(
        relay_kernel, [(plane, bf16) for plane in (own.shape,) * 2], sent[0], sent[3], near, wrap, free=(2, 3)
    )
    first_got = [
        lax.ppermute(plus, EVERY, neighbours(0, 1)),
        lax.ppermute(minus, EVERY, neighbours(0, 3)),
    ]
    own, *sent = weight_second(place, own, first_got)
    second_got = send_all(sent, 1)
    (grad_input,) = call(
        last_kernel,
        [((tokens, 1, width), f32)],
        after(got, sent),
        up,
        grad_mixed,
        xhat,
        rstd,
        gains,
        free=(0,),
    )
    sides = jnp.sum(got[:, 4:].reshape(2, ranks // 2, 4, half).astype(f32), axis=1)
    total = jnp.concatenate(
        (sides[0, :3], sides[1, :3], sides[0, 3:] + sides[1, 3:], jnp.zeros((1, half), f32))
    )
    total = (total * grad_scale).astype(bf16)
    spread = exchange(jnp.broadcast_to(total, (ranks,) + total.shape), EVERY)
    own, *sent = weight_third(place, after(own, grad_input), second_got)
    third_got = send_all(sent, 2)
    spread = after(spread, sent)
    whole_spec = spec_one.shape
    unpacked = call(
        unpack_kernel,
        [
            (whole_spec, f32),
            (whole_spec, f32),
            ((hidden,), f32),
            ((width,), f32),
            ((width,), f32),
            ((width,), f32),
            ((2, width), f32),
            ((2, width), f32),
        ],
        spread,
        scratch_shapes=[pltpu.VMEM((2,) + matrices, f32)],
        free=(0,),
    )
    spec_one_grad, spec_two_grad, fc_grad, out_grad, gain1, gain2, bias1, bias2 = unpacked
    kept, away = call(
        lambda *refs: point_kernel(grad_scale, *refs),
        [((hidden // ranks, width), f32)] * 2,
        place,
        after(own, fc_grad),
        *third_got,
        in_specs=[SMEM] + [whole(own.shape)] * 4,
        free=range(5),
        free_outs=range(2),
    )
    came = swap(away)
    first = place[3] == 0
    grad_one = jnp.where(first, kept, came)
    grad_two = jnp.where(first, came, kept)
    return (
        grad_input.reshape(samples, lon_cells, 1, width).transpose(0, 2, 1, 3),
        grad_one.T,
        grad_two,
        fc_grad,
        out_grad,
        gain1,
        gain2,
        spec_one_grad,
        bias1,
        spec_two_grad,
        bias2,
    )


def solution(mesh):
    fine = Mesh(mesh.devices.reshape(2, 4, 4, 2, 2), EVERY)
    placed = (
        P(SPACE, None, "dp", None),
        P(None, SPACE),
        P(),
        P(),
        P(),
        P(),
        P(),
        P(),
        P(),
        P(),
        P(),
        P("dp", SPACE, None, None),
    )

    return jax.shard_map(
        local,
        mesh=fine,
        in_specs=placed,
        out_specs=(
            P("dp", SPACE, None, None),
            P(None, EVERY),
            P(EVERY, None),
        )
        + (P(),) * 8,
        check_vma=False,
    )
```

```python
import math

import jax
import jax.numpy as jnp
import numpy as np
from jax import lax
from jax.experimental import pallas as pl
from jax.experimental.pallas import tpu as pltpu
from jax.sharding import Mesh, PartitionSpec as P

KW = 64
SPACE = ("z", "y", "xh", "c")
EVERY = ("dp",) + SPACE

epsilon = 1e-05
bf16 = jnp.bfloat16
f32 = jnp.float32
ROOT = math.sqrt(2.0 / math.pi)
CUBE = 0.044715


def exchange(values, axes):
    return lax.all_to_all(values, axes, split_axis=0, concat_axis=0, tiled=True)


def high_low(table):
    table = np.asarray(table, np.float32)
    high = table.astype(bf16)
    low = (table - high.astype(np.float32)).astype(bf16)
    return np.stack((high, low))


def zonal_tables(samples, lon):
    angle = 2.0 * np.pi * (np.outer(np.arange(KW), np.arange(lon)) % lon) / lon
    both = np.stack((np.cos(angle), -np.sin(angle)), axis=1) / math.sqrt(lon)
    eye = np.eye(samples)
    plain = np.einsum("krw,ab->krabw", both, eye)
    plain = plain.reshape(KW * 2 * samples, samples * lon)
    double = np.where(np.arange(KW) == 0, 1.0, 2.0)
    doubled = plain * np.repeat(double, 2 * samples)[:, None]
    return plain, doubled


def meridian_table(samples, lat):
    angle = 2.0 * np.pi * (np.outer(np.arange(lat), np.arange(lat)) % lat) / lat
    cos, sin = np.cos(angle) / math.sqrt(lat), np.sin(angle) / math.sqrt(lat)
    turn = np.stack((np.stack((cos, sin), -1), np.stack((-sin, cos), -1)))
    whole = np.einsum("qksr,ab->qkasrb", turn, np.eye(samples))
    return whole.reshape(2 * lat * samples, lat * 2 * samples)


def dot(a, b, ca=1, cb=0):
    return lax.dot_general(a, b, (((ca,), (cb,)), ((), ())), preferred_element_type=f32)


def split(a):
    high = a.astype(bf16)
    return high, (a - high.astype(f32)).astype(bf16)


def dot3(a, b, ca=1, cb=0):
    return dot(a[0], b[0], ca, cb) + (dot(a[1], b[0], ca, cb) + dot(a[0], b[1], ca, cb))


def dot2(table, b):
    return dot(table[0], b) + dot(table[1], b)


def bend(x):
    return jnp.tanh(ROOT * (x + CUBE * (x * x * x)))


def smooth_gate(x):
    return 0.5 * x * (1.0 + bend(x))


def gate_slope(x):
    t = bend(x)
    return 0.5 * (1.0 + t) + (0.5 * x) * (1.0 - t * t) * (ROOT * (1.0 + (3.0 * CUBE) * (x * x)))


def normalise(x):
    centred = x - jnp.mean(x, axis=-1, keepdims=True)
    rstd = lax.rsqrt(jnp.mean(centred * centred, axis=-1, keepdims=True) + epsilon)
    return centred * rstd, rstd


def norm_pull(grad, gain, xhat, rstd):
    scaled = grad * gain
    return rstd * (
        scaled
        - jnp.mean(scaled, axis=-1, keepdims=True)
        - xhat * jnp.mean(scaled * xhat, axis=-1, keepdims=True)
    )


def to_rows(block):
    return block.astype(f32).reshape(block.shape[0] * block.shape[1], block.shape[2]).astype(bf16)


def to_pieces(values):
    return values.reshape(values.shape[0] // 4, 4, values.shape[1]).astype(bf16)


def project(values, table_ref, out_ref):
    half = out_ref.shape[2]
    ranks = out_ref.shape[0] // 2
    found = dot3((table_ref[0], table_ref[1]), split(values))
    out_ref[:ranks] = to_pieces(found[:, :half])
    out_ref[ranks:] = to_pieces(found[:, half:])


def expand(rows_ref, table_ref):
    ranks = rows_ref.shape[0] // 2
    table = (table_ref[0], table_ref[1])
    return jnp.concatenate(
        [dot2(table, to_rows(rows_ref[ranks * h : ranks * (h + 1), :4])) for h in range(2)], axis=1
    )


def first_kernel(base_ref, table_ref, sent_ref, xhat_ref, rstd_ref):
    xhat, rstd = normalise(base_ref[...])
    xhat_ref[...] = xhat
    rstd_ref[...] = jnp.broadcast_to(rstd, rstd_ref.shape)
    project(xhat, table_ref, sent_ref)


def field_kernel(rows_ref, table_ref, base_ref, xhat_ref, gains_ref, flat_ref, xhat2_ref, rstd2_ref):
    mixed = base_ref[...] + xhat_ref[...] * gains_ref[0:1] + expand(rows_ref, table_ref)
    xhat2, rstd2 = normalise(mixed)
    xhat2_ref[...] = xhat2
    rstd2_ref[...] = jnp.broadcast_to(rstd2, rstd2_ref.shape)
    flat_ref[...] = (xhat2 * gains_ref[1:2]).astype(bf16)


def back_kernel(
    grad_ref, cot_ref, xhat2_ref, rstd2_ref, xhat_ref, gains_ref, table_ref, sent_ref, mixed_ref, sums_ref
):
    grad = grad_ref[...]
    xhat2 = xhat2_ref[...]
    cot = cot_ref[...].astype(f32)
    mixed = cot + norm_pull(grad, gains_ref[1:2], xhat2, rstd2_ref[:, 0:1])
    mixed_ref[...] = mixed
    sums_ref[0:1] = jnp.sum(cot, axis=0, keepdims=True)
    sums_ref[1:2] = jnp.sum(mixed * xhat_ref[...], axis=0, keepdims=True)
    sums_ref[2:3] = jnp.sum(grad * xhat2, axis=0, keepdims=True)
    project(mixed, table_ref, sent_ref)


def last_kernel(rows_ref, table_ref, mixed_ref, xhat_ref, rstd_ref, gains_ref, out_ref):
    mixed = mixed_ref[...]
    grad = mixed + expand(rows_ref, table_ref)
    result = mixed + norm_pull(grad, gains_ref[0:1], xhat_ref[...], rstd_ref[:, 0:1])
    out_ref[:, 0] = result


def hidden_kernel(
    place_ref, flat_ref, cot_ref, one_ref, bias_ref, two_ref, grad_ref, active_ref, tall_ref, sum_ref
):
    pre = dot(flat_ref[...], one_ref[...]) + bias_ref[...]
    up = dot(cot_ref[...], two_ref[...], 1, 1)
    t = bend(pre)
    half = 0.5 * (1.0 + t)
    active = pre * half
    grad = up * (half + (0.5 * pre) * (1.0 - t * t) * (ROOT + (3.0 * CUBE * ROOT) * (pre * pre)))
    grad_ref[...] = grad.astype(bf16)
    active_ref[...] = active.astype(bf16)
    tall_ref[...] = jnp.where(place_ref[3] == 0, active, grad).astype(bf16)
    sum_ref[0] = jnp.sum(grad, axis=0, keepdims=True)


def mix(real, imag, weights, index):
    n = weights.shape[3] // 2
    wr = (weights[0, index, :, :n], weights[1, index, :, :n])
    wi = (weights[0, index, :, n:], weights[1, index, :, n:])
    real, imag = split(real), split(imag)
    return dot3(real, wr) - dot3(imag, wi), dot3(real, wi) + dot3(imag, wr)


def beside(left, right):
    return tuple(jnp.concatenate(pair, axis=1) for pair in zip(left, right))


def mix_pull(real, imag, weights, index):
    both = (weights[0, index], weights[1, index])
    turned = beside(imag, tuple(-r for r in real))
    return dot3(beside(real, imag), both, 1, 1), dot3(turned, both, 1, 1)


def compact(full, inner):
    lane = lax.broadcasted_iota(jnp.int32, (inner, full.shape[1]), 1)
    kept = None
    for j in range(full.shape[0] // inner):
        here = (lane >= inner * j) & (lane < inner * (j + 1))
        part = jnp.where(here, full[inner * j : inner * (j + 1)], 0.0)
        kept = part if kept is None else kept + part
    return kept


def spectral_kernel(rows_ref, table_ref, turned_ref, weights_ref, vectors_ref, sent_ref, plain_ref, pre_ref):
    ranks = rows_ref.shape[0] // 2
    half = 2 * ranks
    table = (table_ref[0], table_ref[1])
    for dp in range(2):
        found = dot2(table, to_rows(rows_ref[ranks * dp : ranks * (dp + 1)]))
        plain_ref[0, half * dp : half * (dp + 1)] = found[:half]
        plain_ref[1, half * dp : half * (dp + 1)] = found[half:]
    gain = vectors_ref[0:1]
    real, imag = mix(plain_ref[0] * gain, plain_ref[1] * gain, weights_ref, 0)
    real = real + vectors_ref[1:2]
    imag = imag + vectors_ref[2:3]
    pre_ref[0] = real
    pre_ref[1] = imag
    real, imag = mix(smooth_gate(real), smooth_gate(imag), weights_ref, 1)
    real = real + vectors_ref[3:4]
    imag = imag + vectors_ref[4:5]
    turned = (turned_ref[0], turned_ref[1])
    for dp in range(2):
        both = jnp.concatenate(
            (real[half * dp : half * (dp + 1)], imag[half * dp : half * (dp + 1)]), axis=0
        )
        sent_ref[ranks * dp : ranks * (dp + 1)] = to_pieces(dot3(turned, split(both)))


def spectral_back_kernel(
    rows_ref,
    table_ref,
    turned_ref,
    weights_ref,
    vectors_ref,
    plain_ref,
    pre_ref,
    lines_ref,
    place_ref,
    packet_ref,
    grads_ref,
    sums_ref,
    work_ref,
):
    ranks = rows_ref.shape[0] // 2
    half = 2 * ranks
    inner = grads_ref.shape[0] // 4
    table = (table_ref[0], table_ref[1])
    found = [
        dot2(table, to_rows(rows_ref[ranks * dp : ranks * (dp + 1)])) for dp in range(2)
    ]
    real = jnp.concatenate((found[0][:half], found[1][:half]), axis=0)
    imag = jnp.concatenate((found[0][half:], found[1][half:]), axis=0)

    def weight_grads(first, second, grad_real, grad_imag, at):
        both = beside(grad_real, grad_imag)
        a, b = dot3(first, both, 0, 0), dot3(second, both, 0, 0)
        n = a.shape[1] // 2
        grads_ref[inner * at : inner * (at + 1)] = compact(a[:, :n] + b[:, n:], inner)
        grads_ref[inner * (at + 1) : inner * (at + 2)] = compact(a[:, n:] - b[:, :n], inner)

    sums_ref[3:4] = jnp.sum(real, axis=0, keepdims=True)
    sums_ref[4:5] = jnp.sum(imag, axis=0, keepdims=True)
    pre_real, pre_imag = pre_ref[0], pre_ref[1]
    real, imag = split(real), split(imag)
    weight_grads(split(smooth_gate(pre_real)), split(smooth_gate(pre_imag)), real, imag, 2)
    real, imag = mix_pull(real, imag, weights_ref, 1)
    real = real * gate_slope(pre_real)
    imag = imag * gate_slope(pre_imag)
    sums_ref[1:2] = jnp.sum(real, axis=0, keepdims=True)
    sums_ref[2:3] = jnp.sum(imag, axis=0, keepdims=True)
    gain = vectors_ref[0:1]
    real, imag = split(real), split(imag)
    plain_real, plain_imag = plain_ref[0], plain_ref[1]
    weight_grads(split(plain_real * gain), split(plain_imag * gain), real, imag, 0)
    real, imag = mix_pull(real, imag, weights_ref, 0)
    sums_ref[0:1] = jnp.sum(real * plain_real + imag * plain_imag, axis=0, keepdims=True)
    turned = (turned_ref[0], turned_ref[1])
    for dp in range(2):
        both = jnp.concatenate(
            (real[half * dp : half * (dp + 1)], imag[half * dp : half * (dp + 1)]), axis=0
        )
        found = dot3(turned, split(both))
        work_ref[ranks * dp : ranks * (dp + 1), 0:4] = found.reshape(ranks, 4, found.shape[1])
    total = 2 * ranks
    for r in range(3):
        work_ref[:, 4 + r] = grads_ref[total * r : total * (r + 1)]
    known = lines_ref.shape[0]
    work_ref[:, 7] = jnp.zeros((total, found.shape[1]), f32)
    work_ref[:known, 7] = lines_ref[...]
    for h in range(2):

        @pl.when(place_ref[6] == h)
        def _(h=h):
            work_ref[known + 5 * h : known + 5 * h + 5, 7] = sums_ref[...]

    packet_ref[...] = work_ref[...].astype(bf16)


def unpack_kernel(spread_ref, one_ref, two_ref, fc_ref, out_ref, gain1_ref, gain2_ref, b1_ref, b2_ref, work_ref):
    total = spread_ref.shape[0]
    inner = one_ref.shape[2]
    wide = spread_ref[...].astype(f32)
    for h in range(2):
        for r in range(3):
            work_ref[h, total * r : total * (r + 1)] = wide[:, 3 * h + r]
        for m in range(4):
            for j in range(4):
                (one_ref, two_ref)[m // 2][m % 2, 4 * h + j] = work_ref[
                    h, inner * m : inner * (m + 1), inner * j : inner * (j + 1)
                ]
    lines = wide[:24, 6]

    def joined(*rows):
        return jnp.concatenate([lines[r : r + 1] for r in rows], axis=1)

    fc_ref[...] = joined(*range(8))[0]
    out_ref[...] = joined(8, 9)[0]
    gain1_ref[...] = (joined(10, 11) + joined(14, 19))[0]
    gain2_ref[...] = joined(12, 13)[0]
    for i in range(2):
        b1_ref[i : i + 1] = joined(15 + i, 20 + i)
        b2_ref[i : i + 1] = joined(17 + i, 22 + i)


def whole(shape):
    zeros = (0,) * len(shape)
    return pl.BlockSpec(shape, lambda *_: zeros)


def call(kernel, outs, *args, grant=16, grid=(1,), in_specs=None, out_specs=None, free=(), free_outs=(), **more):
    in_specs = in_specs or [whole(a.shape) for a in args]
    return pl.pallas_call(
        kernel,
        out_shape=[
            (jax.ShapeDtypeStruct if i in free_outs else pltpu.HBM)(shape, kind)
            for i, (shape, kind) in enumerate(outs)
        ],
        compiler_params=pltpu.CompilerParams(vmem_limit_bytes=grant << 20),
        grid=grid,
        in_specs=in_specs,
        out_specs=out_specs or [whole(shape) for shape, _ in outs],
        **more,
    )(
        *(
            a if spec is SMEM or i in free else pltpu.with_memory_space_constraint(a, pltpu.HBM)
            for i, (a, spec) in enumerate(zip(args, in_specs))
        )
    )


SMEM = pl.BlockSpec(memory_space=pltpu.SMEM)


def weight_kernel(
    place_ref,
    grad_ref,
    active_ref,
    flat_ref,
    cot_ref,
    tall_ref,
    wide_ref,
    own_ref,
    out1_ref,
    near_ref,
    wrap_ref,
    out3_ref,
    acc_ref,
):
    step = pl.program_id(0)
    low, at_z = step // 4, step % 4
    share = own_ref.shape[1]
    x, y, core = place_ref[0], place_ref[1], place_ref[3]
    first = core == 0

    @pl.when(first)
    def _():
        acc_ref[...] = dot(grad_ref[...], flat_ref[...], 0, 0)

    @pl.when(core == 1)
    def _():
        acc_ref[...] = dot(active_ref[...], cot_ref[...], 0, 0)

    acc_ref[...] += dot(tall_ref[...], wide_ref[...], 0, 0)
    for at_y in range(4):
        for at_xh in range(2):
            at_x = 2 * at_xh + low
            at = (at_y * 2 + at_xh) * share
            far = jnp.where(first, at_x - x, at_y - y) & 3
            spot = jnp.where(first, at_y * 4 + at_z, at_z * 4 + at_x)
            upper = spot >= 8
            for ref, here, spot in (
                (own_ref, far == 0, spot),
                (out1_ref, far == 1, spot),
                (near_ref, (far == 2) & (spot < 8), spot),
                (wrap_ref, (far == 2) & upper, spot - 8),
                (out3_ref, far == 3, spot),
            ):

                @pl.when(here)
                def _(ref=ref, at=at, spot=spot):
                    ref[spot] = acc_ref[at : at + share].astype(ref.dtype)


def relay_kernel(out1_ref, out3_ref, near_ref, wrap_ref, plus_ref, minus_ref):
    plus_ref[:8] = (out1_ref[:8].astype(f32) + near_ref[...].astype(f32)).astype(bf16)
    plus_ref[8:] = out1_ref[8:]
    minus_ref[:8] = out3_ref[:8]
    minus_ref[8:] = (out3_ref[8:].astype(f32) + wrap_ref[...].astype(f32)).astype(bf16)


def plane_kernel(place_ref, own_in_ref, *refs):
    got, own_ref, outs = refs[:2], refs[2], refs[3:]
    for d in range(4):
        for i in range(4):
            at = 4 * ((place_ref[4] + d) & 3) + i
            total = own_in_ref[at]
            for r in range(2):
                total = total + got[r][at].astype(f32)
            if d == 0:
                own_ref[i] = total
            else:
                outs[d - 1][i] = total.astype(bf16)


def line_kernel(place_ref, own_in_ref, *refs):
    got, own_ref, outs = refs[:3], refs[3], refs[4:]
    for d in range(4):
        at = (place_ref[5] + d) & 3
        total = own_in_ref[at]
        for r in range(3):
            total = total + got[r][at].astype(f32)
        if d == 0:
            own_ref[...] = total
        else:
            outs[d - 1][...] = total.astype(bf16)


def point_kernel(scale, place_ref, own_ref, *refs):
    got, kept_ref, send_ref = refs[:3], refs[3], refs[4]
    share = kept_ref.shape[0]
    total = own_ref[...]
    for r in range(3):
        total = total + got[r][...].astype(f32)
    total = total * scale
    first = place_ref[3] == 0
    kept_ref[...] = jnp.where(first, total[:share], total[share:])
    send_ref[...] = jnp.where(first, total[share:], total[:share])


def neighbours(stage, far):
    pairs = []
    for rank in range(128):
        core, xh, y, z, low = rank & 1, (rank >> 1) & 1, (rank >> 2) & 3, (rank >> 4) & 3, rank >> 6
        at = [2 * xh + low, y, z]
        axis = (stage + core) % 3
        at[axis] = (at[axis] + far) & 3
        x, y, z = at
        pairs.append((rank, ((x & 1) << 6) | (z << 4) | (y << 2) | ((x >> 1) << 1) | core))
    return pairs


def send_all(pieces, stage):
    return [lax.ppermute(pieces[r], EVERY, neighbours(stage, r + 1)) for r in range(3)]


def after(value, others):
    return lax.optimization_barrier((value, others))[0]


def weight_place():
    core = lax.axis_index("c")
    x = 2 * lax.axis_index("xh") + lax.axis_index("dp")
    y, z = lax.axis_index("y"), lax.axis_index("z")
    first = core == 0
    return jnp.stack(
        (x, y, z, core, jnp.where(first, y, z), jnp.where(first, z, x), lax.axis_index("dp"))
    ).astype(
        jnp.int32
    )


def swap(values):
    return lax.ppermute(values, "c", [(0, 1), (1, 0)])


def weight_start(place, grad_hidden, active, flat, cot, tall):
    tokens, hidden = grad_hidden.shape
    width = flat.shape[1]
    first = place[3] == 0
    tall = swap(tall)
    wide = swap(jnp.where(first, cot, flat))
    cube = (16, hidden // 64, width)
    half = (8,) + cube[1:]
    ahead = pl.BlockSpec((tokens, hidden // 8), lambda g: (0, g))
    across = whole(flat.shape)
    return call(
        weight_kernel,
        [(cube, f32), (cube, bf16), (half, bf16), (half, bf16), (cube, bf16)],
        place,
        grad_hidden,
        active,
        flat,
        cot,
        tall,
        wide,
        grant=24,
        grid=(8,),
        in_specs=[SMEM, ahead, ahead, across, across, ahead, across],
        out_specs=[whole(cube), whole(cube), whole(half), whole(half), whole(cube)],
        scratch_shapes=[pltpu.VMEM((hidden // 8, width), f32)],
        free=(3, 4, 5, 6),
        cost_estimate=pl.CostEstimate(
            flops=4 * tokens * hidden * width, bytes_accessed=14 << 20, transcendentals=0
        ),
    )


def weight_second(place, own, got):
    cube = own.shape
    row = (4,) + cube[1:]
    return call(
        plane_kernel,
        [(row, f32)] + [(row, bf16)] * 3,
        place,
        own,
        *got,
        grid=(1,),
        in_specs=[SMEM] + [whole(cube)] * 3,
        out_specs=[whole(row)] * 4,
        free=(2, 3),
        free_outs=range(4),
    )


def weight_third(place, own, got):
    row = own.shape
    line = row[1:]
    return call(
        line_kernel,
        [(line, f32)] + [(line, bf16)] * 3,
        place,
        own,
        *got,
        grid=(1,),
        in_specs=[SMEM, whole(row)] + [whole(row)] * 3,
        out_specs=[whole(line)] * 4,
        free=range(5),
        free_outs=range(4),
    )


def block_diagonal(weights):
    blocks, inner = weights.shape[1:3]
    tall = weights.reshape(2, blocks * inner, inner)
    wide = jnp.concatenate((tall,) * blocks, axis=2)
    row = lax.broadcasted_iota(jnp.int32, wide.shape, 1) // inner
    lane = lax.broadcasted_iota(jnp.int32, wide.shape, 2) // inner
    return jnp.where(row == lane, wide, 0.0)


def local(
    stash,
    piece_map,
    gain_one,
    spec_one,
    bias_one,
    spec_two,
    bias_two,
    gain_two,
    fc_one,
    bias_fc,
    fc_two,
    cotangent,
):
    samples, _, lon_cells, width = cotangent.shape
    lat_total = lax.axis_size(SPACE)
    ranks = lax.axis_size(EVERY)
    tokens = samples * lon_cells
    hidden = fc_one.shape[1]
    half = width // 2
    rows = 4 * ranks
    piece = (ranks, 4, half)
    plain_table, doubled_table = zonal_tables(samples, lon_cells)
    meridian = meridian_table(samples, lat_total)
    down, back_down = high_low(plain_table), high_low(doubled_table)
    up, back_up = high_low(plain_table.T), high_low(doubled_table.T)
    forward, inverse = high_low(meridian), high_low(meridian.T)

    arrived = exchange(stash[0], SPACE)
    ordering = jnp.argsort(piece_map[:, 0])
    placed = jnp.take(arrived, ordering, axis=0)
    base = jnp.transpose(placed, (1, 0, 2)).reshape(tokens, width).astype(f32)
    upstream = cotangent.reshape(tokens, width)
    gains = jnp.stack((gain_one, gain_two))

    which = lax.axis_index("dp")
    blocks, inner = spec_one.shape[1:3]
    mine = blocks // 2
    wide = [
        block_diagonal(lax.dynamic_slice_in_dim(w, which * mine, mine, 1))
        for w in (spec_one, spec_two)
    ]
    both = jnp.stack([jnp.concatenate((w[0], w[1]), axis=1) for w in wide])
    weights = jnp.stack(split(both))
    vectors = lax.dynamic_slice_in_dim(
        jnp.concatenate((gain_one[None], bias_one, bias_two)), which * half, half, 1
    )

    sent, xhat, rstd = call(
        first_kernel,
        [(piece, bf16), ((tokens, width), f32), ((tokens, 128), f32)],
        base,
        down,
        free=(0,),
    )
    got = exchange(sent, EVERY)
    sent, plain, pre = call(
        spectral_kernel,
        [(piece, bf16), ((2, rows // 2, half), f32), ((2, rows // 2, half), f32)],
        got,
        forward,
        inverse,
        weights,
        vectors,
        free=(0,),
    )
    got = exchange(sent, EVERY)
    normed_flat, xhat2, rstd2 = call(
        field_kernel,
        [((tokens, width), bf16), ((tokens, width), f32), ((tokens, 128), f32)],
        got,
        back_up,
        base,
        xhat,
        gains,
        free=(0,),
        free_outs=(0,),
    )
    place = weight_place()
    block = (tokens, hidden // 8)
    across = pl.BlockSpec(block, lambda g: (0, g))
    grad_hidden_flat, active_flat, tall, bias_sum = call(
        hidden_kernel,
        [((tokens, hidden), bf16)] * 3 + [((8, 1, hidden // 8), f32)],
        place,
        normed_flat,
        upstream,
        fc_one,
        bias_fc.reshape(1, hidden),
        fc_two,
        grid=(8,),
        in_specs=[
            SMEM,
            whole(normed_flat.shape),
            whole(upstream.shape),
            pl.BlockSpec((width, hidden // 8), lambda g: (0, g)),
            pl.BlockSpec((1, hidden // 8), lambda g: (0, g)),
            pl.BlockSpec((hidden // 8, width), lambda g: (g, 0)),
        ],
        out_specs=[across] * 3 + [pl.BlockSpec((1, 1, hidden // 8), lambda g: (g, 0, 0))],
        free=(1, 2, 4),
        free_outs=(3,),
        cost_estimate=pl.CostEstimate(
            flops=4 * tokens * hidden * width,
            bytes_accessed=18 << 20,
            transcendentals=tokens * hidden,
        ),
    )
    grad_normed_two = jnp.einsum("tf,df->td", grad_hidden_flat, fc_one, preferred_element_type=f32)
    sent, grad_mixed, sums = call(
        back_kernel,
        [(piece, bf16), ((tokens, width), f32), ((3, width), f32)],
        grad_normed_two,
        upstream,
        xhat2,
        rstd2,
        xhat,
        gains,
        back_down,
        free=(0, 1),
    )
    got = exchange(sent, EVERY)

    grad_scale = 1.0 / math.sqrt(samples * lax.axis_size("dp") * lat_total * lon_cells)
    own, *sent = weight_start(
        place, grad_hidden_flat, active_flat, normed_flat, upstream, tall
    )
    near = lax.ppermute(sent[1], EVERY, neighbours(0, 1))
    wrap = lax.ppermute(sent[2], EVERY, neighbours(0, 3))
    got = after(got, sent)

    lines = jnp.concatenate((bias_sum.reshape(-1, half), sums.reshape(-1, half)))
    matrices = (4 * inner, half)
    (packet,) = call(
        spectral_back_kernel,
        [((ranks, 8, half), bf16)],
        got,
        forward,
        inverse,
        weights,
        vectors,
        plain,
        pre,
        lines,
        place,
        in_specs=[whole(a.shape) for a in (got, forward, inverse, weights, vectors, plain, pre)]
        + [whole(lines.shape), SMEM],
        scratch_shapes=[
            pltpu.VMEM(matrices, f32),
            pltpu.VMEM((5, half), f32),
            pltpu.VMEM((ranks, 8, half), f32),
        ],
        free=(0, 7, 8),
        grant=20,
    )
    got = exchange(packet, EVERY)
    plus, minus = call(
        relay_kernel, [(plane, bf16) for plane in (own.shape,) * 2], sent[0], sent[3], near, wrap, free=(2, 3)
    )
    first_got = [
        lax.ppermute(plus, EVERY, neighbours(0, 1)),
        lax.ppermute(minus, EVERY, neighbours(0, 3)),
    ]
    own, *sent = weight_second(place, own, first_got)
    second_got = send_all(sent, 1)
    (grad_input,) = call(
        last_kernel,
        [((tokens, 1, width), f32)],
        after(got, sent),
        up,
        grad_mixed,
        xhat,
        rstd,
        gains,
        free=(0,),
    )
    sides = jnp.sum(got[:, 4:].reshape(2, ranks // 2, 4, half).astype(f32), axis=1)
    total = jnp.concatenate(
        (sides[0, :3], sides[1, :3], sides[0, 3:] + sides[1, 3:], jnp.zeros((1, half), f32))
    )
    total = (total * grad_scale).astype(bf16)
    spread = exchange(jnp.broadcast_to(total, (ranks,) + total.shape), EVERY)
    own, *sent = weight_third(place, after(own, grad_input), second_got)
    third_got = send_all(sent, 2)
    spread = after(spread, sent)
    whole_spec = spec_one.shape
    unpacked = call(
        unpack_kernel,
        [
            (whole_spec, f32),
            (whole_spec, f32),
            ((hidden,), f32),
            ((width,), f32),
            ((width,), f32),
            ((width,), f32),
            ((2, width), f32),
            ((2, width), f32),
        ],
        spread,
        scratch_shapes=[pltpu.VMEM((2,) + matrices, f32)],
        free=(0,),
    )
    spec_one_grad, spec_two_grad, fc_grad, out_grad, gain1, gain2, bias1, bias2 = unpacked
    kept, away = call(
        lambda *refs: point_kernel(grad_scale, *refs),
        [((hidden // ranks, width), f32)] * 2,
        place,
        after(own, fc_grad),
        *third_got,
        in_specs=[SMEM] + [whole(own.shape)] * 4,
        free=range(5),
        free_outs=range(2),
    )
    came = swap(away)
    first = place[3] == 0
    grad_one = jnp.where(first, kept, came)
    grad_two = jnp.where(first, came, kept)
    return (
        grad_input.reshape(samples, lon_cells, 1, width).transpose(0, 2, 1, 3),
        grad_one.T,
        grad_two,
        fc_grad,
        out_grad,
        gain1,
        gain2,
        spec_one_grad,
        bias1,
        spec_two_grad,
        bias2,
    )


def solution(mesh):
    fine = Mesh(mesh.devices.reshape(2, 4, 4, 2, 2), EVERY)
    placed = (
        P(SPACE, None, "dp", None),
        P(None, SPACE),
        P(),
        P(),
        P(),
        P(),
        P(),
        P(),
        P(),
        P(),
        P(),
        P("dp", SPACE, None, None),
    )

    return jax.shard_map(
        local,
        mesh=fine,
        in_specs=placed,
        out_specs=(
            P("dp", SPACE, None, None),
            P(None, EVERY),
            P(EVERY, None),
        )
        + (P(),) * 8,
        check_vma=False,
    )
```
